32 devices in a mesh: dp: 8 (over z, core), space: 4 (over y, x).
Axes of the slice: x: 2, y: 2, z: 4, core: 2. Of those that a mesh axis runs over, the one named last changes fastest.
Arguments:
- features: bfloat16 [8, 16, 64, 512], P('dp', 'space'), may hold values from -6 to 6
- conv_master: float32 [13824, 512], P(('dp', 'space')), may hold values from -0.125 to 0.125
- head_master: float32 [512, 1792], P(('dp', 'space')), may hold values from -0.25 to 0.25
- scale_master: float32 [1792], P(('dp', 'space')), may hold values from 8 to 24
- join_master: float32 [5376], P(('dp', 'space')), may hold values from 0.2 to 0.8
- affine_scale: float32 [3, 512], replicated, may hold values from 0.5 to 1.5
- affine_shift: float32 [3, 512], replicated, may hold values from -1.5 to 1.5
- head_cotangent: bfloat16 [8, 16, 64, 1792], P('dp', 'space'), may hold values from -6 to 6
- pool_cotangent: float32 [8, 256], P('dp'), may hold values from -16 to 16
- box_counts: int32 [8], P('dp'), may hold values from 1 to 128, as said below
- proposals: int32 [8, 128], P('dp'), may hold values from 0 to 1023
Outputs:
- head_maps: bfloat16 [8, 16, 64, 1792], P('dp', 'space')
- pooled: float32 [8, 256], P('dp')
- input_grad: float32 [8, 16, 64, 512], P('dp', 'space')
- conv_grad: float32 [13824, 512], P(('dp', 'space'))
- head_grad: float32 [512, 1792], P(('dp', 'space'))
- scale_grad: float32 [1792], P(('dp', 'space'))
- join_grad: float32 [5376], P(('dp', 'space'))
The draws below stay inside these ranges and needn't reach their ends.
Inputs may be any that keep to these rules, and one draw needn't show every extreme that they name: `box_counts`: each image has between 64 and 128 live slots; some image has all 128 live in every draw; a pixel may appear in several slots.
All inputs are finite; a program needn't handle non-finite values.
Results may differ from the reference program's by a relative error of at most 0.011.
Values may be sent and summed in bfloat16 or wider, within the bound.
No kernel may reach another device: no remote copies, remote signals or barrier semaphores. Data moves between devices by JAX's collectives and lax.ppermute only.
A program may use at most 192 MiB of HBM per device.

```python
import jax
import jax.numpy as jnp
from jax import lax

CHANNELS = 512
HEAD_CH = 256
TASK_HEADS = 7
IMG_WIDTH = 64
PROPOSALS = 128
SCALES = 3
IMAGES = 8
HEIGHT = 16
PIXELS = 1024


def draw_box_counts(key, part):
    first = jax.random.fold_in(key, 11)
    second = jax.random.fold_in(key, 23)
    counts = jax.random.randint(first, (IMAGES,), PROPOSALS // 2, PROPOSALS + 1)
    chosen = jax.random.randint(second, (), 0, IMAGES)
    return jnp.where(jnp.arange(IMAGES) == chosen, PROPOSALS, counts).astype(jnp.int32)


def with_ends(result, key, low, high):
    longest = result.shape.index(max(result.shape))
    spots = []
    for shift in (0, 1):
        where = [jax.random.randint(jax.random.fold_in(key, axis), (), 0, length) for axis, length in enumerate(result.shape)]
        where[longest] = (where[longest] + shift) % result.shape[longest]
        spots.append(tuple(where))
    return result.at[spots[0]].set(low).at[spots[1]].set(high)


def levels(key, shape, pieces, least, largest):
    factor_of, own = 1.0, jax.random.fold_in(key, 6)
    for dim, shards_of in pieces:
        draws = jnp.exp(jax.random.uniform(jax.random.fold_in(own, dim), (shards_of,), jnp.float32, least / len(pieces), largest / len(pieces)))
        factor_of = factor_of * jnp.repeat(draws, shape[dim] // shards_of).reshape([-1 if axis == dim else 1 for axis in range(len(shape))])
    return factor_of


def gaussian(key, shape, width, reach, pieces=(), held_as=jnp.bfloat16):
    array = width * jax.random.normal(key, shape, jnp.float32)
    if pieces:
        array = array * levels(key, shape, pieces, -0.22, 0.18)
    return jnp.clip(array, -reach, reach).astype(held_as)


def setup_inputs(seed: int = 0) -> dict:
    arg_keys = jax.random.split(jax.random.key(seed), 12)
    return {
        "features": gaussian(arg_keys[0], (IMAGES, HEIGHT, IMG_WIDTH, CHANNELS), 1.0, 6.0, ((0, 8), (1, 4))),
        "conv_master": gaussian(arg_keys[1], (27 * CHANNELS, CHANNELS), (9 * CHANNELS // 2) ** -0.5, 0.125, ((0, 32),), jnp.float32),
        "head_master": gaussian(arg_keys[2], (CHANNELS, TASK_HEADS * HEAD_CH), CHANNELS ** -0.5, 0.25, ((0, 32),), jnp.float32),
        "scale_master": jnp.clip(8.0 + 16.0 * jax.random.uniform(arg_keys[3], (TASK_HEADS * HEAD_CH,), jnp.float32) ** levels(arg_keys[3], (TASK_HEADS * HEAD_CH,), ((0, 32),), -0.2, 0.2), 8.0, 24.0),
        "join_master": jnp.clip(0.2 + 0.6 * jax.random.uniform(arg_keys[4], (SCALES * TASK_HEADS * HEAD_CH,), jnp.float32) ** levels(arg_keys[4], (SCALES * TASK_HEADS * HEAD_CH,), ((0, 32),), -0.2, 0.2), 0.2, 0.8),
        "affine_scale": jnp.clip(1.0 + 0.1 * jax.random.normal(arg_keys[5], (3, CHANNELS), jnp.float32), 0.5, 1.5),
        "affine_shift": gaussian(arg_keys[6], (3, CHANNELS), 0.3, 1.5, (), jnp.float32),
        "head_cotangent": gaussian(arg_keys[7], (IMAGES, HEIGHT, IMG_WIDTH, TASK_HEADS * HEAD_CH), 1.0, 6.0, ((0, 8), (1, 4))),
        "pool_cotangent": gaussian(arg_keys[8], (IMAGES, HEAD_CH), 3.0, 16.0, ((0, 8),), jnp.float32),
        "box_counts": draw_box_counts(jax.random.fold_in(arg_keys[11], 71), 0),
        "proposals": with_ends(jax.random.randint(arg_keys[10], (IMAGES, PROPOSALS), 0, PIXELS), jax.random.fold_in(arg_keys[10], 1), 0, PIXELS - 1).astype(jnp.int32),
    }


@jax.custom_vjp
def low(v):
    return lax.optimization_barrier(v.astype(jnp.bfloat16)).astype(jnp.float32)

@jax.custom_vjp
def low_back(v):
    return v

def low_keep(v):
    return (low(v), None)

def low_pass(kept, grad):
    return (grad,)

def back_keep(v):
    return (v, None)

def back_low(kept, grad):
    return (low(grad),)
low.defvjp(low_keep, low_pass)
low_back.defvjp(back_keep, back_low)
epsilon = 1e-06

def shrink_mean(images, factor):
    count, height_all, width_all, depth = images.shape
    blocks = images.reshape(count, height_all // factor, factor, width_all // factor, factor, depth)
    return lax.optimization_barrier(jnp.mean(blocks, axis=(2, 4)))

def widen(maps, factor):
    return jnp.repeat(jnp.repeat(maps, factor, axis=1), factor, axis=2)

def forward(images, convs, heads, gains, joins, affine_scale, affine_shift, box_counts, proposals):
    weights = low(convs).reshape(3, 3, 3, CHANNELS, CHANNELS)
    head_weights = low(heads)
    head_gain = low(gains).reshape(TASK_HEADS, HEAD_CH)
    join_weights = low(joins).reshape(SCALES, TASK_HEADS * HEAD_CH)
    joined = jnp.zeros((IMAGES, HEIGHT, IMG_WIDTH, TASK_HEADS * HEAD_CH), jnp.float32)
    for scale_idx in range(SCALES):
        factor = 2 ** scale_idx
        if factor == 1:
            active = images
        else:
            active = low(shrink_mean(images, factor))
        for layer_idx in range(3):
            conv_out = lax.conv_general_dilated(active, weights[layer_idx], (1, 1), 'SAME', dimension_numbers=('NHWC', 'HWIO', 'NHWC'), precision=lax.Precision.HIGHEST)
            conv_out = low_back(conv_out)
            active = low(jax.nn.silu(conv_out * affine_scale[layer_idx] + affine_shift[layer_idx]))
        projected = jnp.einsum('nhwc,cd->nhwd', active, head_weights, precision=lax.Precision.HIGHEST)
        projected = low_back(projected)
        shape_here = projected.shape
        grouped = projected.reshape(shape_here[0], shape_here[1], shape_here[2], TASK_HEADS, HEAD_CH)
        inverse = lax.rsqrt(lax.optimization_barrier(jnp.sum(grouped * grouped, axis=-1, keepdims=True)) + epsilon)
        normed = (grouped * inverse * head_gain).reshape(shape_here)
        joined = joined + join_weights[scale_idx] * widen(normed, factor)
    detect = joined[:, :, :, :HEAD_CH].reshape(IMAGES, PIXELS, HEAD_CH)
    picked = jax.vmap(lambda table, where: table[where])(detect, proposals)
    valid = (jnp.arange(PROPOSALS).astype(jnp.int32)[None, :] < box_counts[:, None]).astype(joined.dtype)
    pooled = lax.optimization_barrier(jnp.sum(picked * valid[:, :, None], axis=1)) / box_counts[:, None].astype(joined.dtype)
    return (joined, pooled)

def reference(features, conv_master, head_master, scale_master, join_master, affine_scale, affine_shift, head_cotangent, pool_cotangent, box_counts, proposals):

    def wrapped(images, convs, heads, gains, joins):
        return forward(images, convs, heads, gains, joins, affine_scale, affine_shift, box_counts, proposals)
    outputs, pullback = jax.vjp(wrapped, features.astype(jnp.float32), conv_master, head_master, scale_master, join_master)
    input_grad, conv_grad, head_grad, scale_grad, join_grad = pullback((head_cotangent.astype(jnp.float32), pool_cotangent))
    return (outputs[0].astype(jnp.bfloat16), outputs[1], input_grad, conv_grad, head_grad, scale_grad, join_grad)
```

```python
import functools

import jax
import jax.numpy as jnp
import numpy as np
from jax import lax
from jax.experimental import pallas as pl
from jax.experimental.pallas import tpu as pltpu
from jax.sharding import PartitionSpec as P

HEAD_CH = 256
TASK_HEADS = 7
SCALES = 3
LAYERS = 3
PAD = 8
VMEM_LIMIT = 56 << 20

epsilon = 1e-06
f32 = jnp.float32
bf16 = jnp.bfloat16
NN = (((1,), (0,)), ((), ()))
NT = (((1,), (1,)), ((), ()))
TN = (((0,), (0,)), ((), ()))


def mm(left, right, dims=NN):
    return lax.dot_general(left, right, dims, preferred_element_type=f32)


def split_mm(left, right):
    high = right.astype(bf16)
    low = (right - high.astype(f32)).astype(bf16)
    return mm(left, high) + mm(left, low)


class Strip:
    def __init__(self, rows, cols):
        self.rows = [rows >> s for s in range(SCALES)]
        self.cols = [cols >> s for s in range(SCALES)]

    def sizes(self, halo):
        return [(r + 2 * halo) * c for r, c in zip(self.rows, self.cols)]

    def starts(self, halo):
        sizes = self.sizes(halo)
        return [sum(sizes[:s]) for s in range(SCALES)]

    def total(self, halo):
        return sum(self.sizes(halo))

    def own(self, halo):
        return [st + halo * c for st, c in zip(self.starts(halo), self.cols)]


def spread_matrix(strip):
    rows, cols = strip.rows[0], strip.cols[0]
    parts = []
    for s in range(1, SCALES):
        mat = np.zeros((rows * cols, strip.rows[s] * strip.cols[s]), np.float32)
        for r in range(rows):
            for c in range(cols):
                mat[r * cols + c, (r >> s) * strip.cols[s] + (c >> s)] = 1.0
        parts.append(mat)
    return np.concatenate(parts, axis=1)


def column_of(strip, scale, count):
    return lax.broadcasted_iota(jnp.int32, (count, 1), 0) % strip.cols[scale]


def shifted_copies(strip, halo, act, wide, depth):
    for s in range(SCALES):
        start, count, cols = strip.starts(halo)[s], strip.sizes(halo)[s], strip.cols[s]
        column = column_of(strip, s, count)
        for k in range(3):
            rows = act[PAD + start + k - 1 : PAD + start + k - 1 + count, :]
            if k == 0:
                rows = jnp.where(column == 0, 0.0, rows)
            if k == 2:
                rows = jnp.where(column == cols - 1, 0.0, rows)
            wide[start : start + count, k * depth : (k + 1) * depth] = rows.astype(bf16)


def patches(strip, halo, wide, cells, depth, flip=False):
    for s in range(SCALES):
        cols = strip.cols[s]
        count = strip.sizes(halo)[s]
        source, target = strip.starts(halo + 1)[s], strip.starts(halo)[s]
        for ky in range(3):
            first = source + (2 - ky if flip else ky) * cols
            for kx in range(3):
                col = (2 - kx if flip else kx) * depth
                tap = 3 * ky + kx
                cells[target : target + count, tap * depth : (tap + 1) * depth] = wide[
                    first : first + count, col : col + depth
                ]


def forward_kernel(
    strip, depth, place, x_ref, w_hbm, scale_ref, shift_ref,
    p0_ref, p1_ref, p2_ref, c0_hbm, c1_hbm, c2_hbm, a3_ref,
    weights, act, wide, cells, w_sem, c_sem,
):
    taps = 9 * depth
    loads = []
    for layer in range(LAYERS):
        copy = pltpu.make_async_copy(
            w_hbm.at[pl.ds(layer * taps, taps), :], weights.at[pl.ds(layer * taps, taps), :], w_sem.at[layer]
        )
        copy.start()
        loads.append(copy)
    here, ranks = place[0], place[1]
    first_in = strip.total(3)
    act[PAD : PAD + first_in, :] = x_ref[...].astype(f32)
    p_refs = (p0_ref, p1_ref, p2_ref)
    c_hbms = (c0_hbm, c1_hbm, c2_hbm)
    stores = []
    for layer in range(LAYERS):
        halo = LAYERS - 1 - layer
        count = strip.total(halo)
        shifted_copies(strip, halo + 1, act, wide, depth)
        for copy in stores:
            copy.wait()
        patches(strip, halo, wide, cells, depth)
        stores = []
        own = strip.own(halo)
        flat = strip.starts(0)
        for s in range(SCALES):
            size = strip.sizes(0)[s]
            copy = pltpu.make_async_copy(
                cells.at[pl.ds(own[s], size), :], c_hbms[layer].at[pl.ds(flat[s], size), :], c_sem.at[s]
            )
            copy.start()
            stores.append(copy)
        loads[layer].wait()
        for half in range(depth // 256):
            lanes = slice(half * 256, (half + 1) * 256)
            z = mm(cells[:count, :], weights[layer * taps : (layer + 1) * taps, lanes])
            p = z * scale_ref[layer : layer + 1, lanes] + shift_ref[layer : layer + 1, lanes]
            a = (p / (1.0 + jnp.exp(-p))).astype(bf16)
            for s in range(SCALES):
                size = strip.sizes(0)[s]
                p_refs[layer][flat[s] : flat[s] + size, lanes] = p[own[s] : own[s] + size]
            if layer == LAYERS - 1:
                a3_ref[:, lanes] = a
            else:
                for s in range(SCALES):
                    start, size = strip.starts(halo)[s], strip.sizes(halo)[s]
                    row = lax.broadcasted_iota(jnp.int32, (size, 1), 0) // strip.cols[s]
                    row = row + here * strip.rows[s] - halo
                    inside = (row >= 0) & (row < ranks * strip.rows[s])
                    act[PAD + start : PAD + start + size, lanes] = jnp.where(
                        inside, a[start : start + size].astype(f32), 0.0
                    )
    for copy in stores:
        copy.wait()


def slope(p):
    sigma = 1.0 / (1.0 + jnp.exp(-p))
    return sigma * (1.0 + p * (1.0 - sigma))


def head_kernel(
    strip, place, a3_ref, w_ref, gain_ref, join_ref, cot_ref, share_ref, where_ref, spread_ref, gather_ref,
    scale_ref, p2_ref,
    maps_ref, pool_ref, join_grad_ref, gain_grad_ref, w_grad_ref, dz_ref, da3,
):
    head = pl.program_id(0)
    fine = strip.sizes(0)[0]
    starts, sizes = strip.starts(0), strip.sizes(0)
    a3 = a3_ref[...]
    weight = w_ref[...]
    g = mm(a3, weight)
    inverse = lax.rsqrt(jnp.sum(g * g, axis=-1, keepdims=True) + epsilon)
    unit = g * inverse
    gain = gain_ref[...]
    normed = unit * gain
    join = join_ref[...]
    coarse = jnp.concatenate(
        [normed[starts[s] : starts[s] + sizes[s]] * join[s : s + 1] for s in range(1, SCALES)], axis=0
    )
    joined = normed[:fine] * join[0:1] + split_mm(spread_ref[...], coarse)
    maps_ref[...] = joined.astype(bf16)
    slots = where_ref.shape[1]
    first = place[0] * fine
    pixel = lax.broadcasted_iota(jnp.int32, (fine, slots), 0) + first
    slot = lax.broadcasted_iota(jnp.int32, (fine, slots), 1)
    hits = jnp.where((where_ref[...] == pixel) & (slot < place[2]) & (head == 0), 1.0, 0.0)
    hits = jnp.sum(hits, axis=-1, keepdims=True)

    @pl.when(head == 0)
    def _():
        pool_ref[...] = jnp.sum(joined * hits, axis=0, keepdims=True)

    fused = cot_ref[...].astype(f32) + hits * share_ref[...]
    down_coarse = split_mm(gather_ref[...], fused)
    down = jnp.concatenate([fused, down_coarse], axis=0)
    product = down * normed
    scaled = []
    for s in range(SCALES):
        part = slice(starts[s], starts[s] + sizes[s])
        join_grad_ref[s : s + 1, :] = jnp.sum(product[part], axis=0, keepdims=True)
        scaled.append(down[part] * join[s : s + 1])
    dn = jnp.concatenate(scaled, axis=0)
    gain_grad_ref[...] = jnp.sum(dn * unit, axis=0, keepdims=True)
    du = dn * gain
    dg = (inverse * (du - unit * jnp.sum(du * unit, axis=-1, keepdims=True))).astype(bf16)
    w_grad_ref[...] = mm(a3, dg, TN).astype(w_grad_ref.dtype)
    part = mm(dg, weight, NT)

    @pl.when(head == 0)
    def _():
        da3[...] = part

    @pl.when(head > 0)
    def _():
        da3[...] += part

    @pl.when(head == pl.num_programs(0) - 1)
    def _():
        dz_ref[...] = (da3[...] * scale_ref[...] * slope(p2_ref[...])).astype(bf16)


def weight_grad_kernel(cells_ref, dz_ref, *refs):
    out_ref = refs[-1]
    out_ref[...] = mm(cells_ref[...], dz_ref[...], TN).astype(out_ref.dtype)


def data_grad_kernel(
    strip, depth, last, dz_ref, above_ref, below_ref, w_ref, *refs
):
    if last:
        spread_ref, out_ref, act, wide, cells, total = refs
    else:
        scale_ref, p_ref, out_ref, act, wide, cells, total = refs
    step = pl.program_id(0)

    @pl.when(step == 0)
    def _():
        edge = 0
        for s in range(SCALES):
            start, size, cols = strip.starts(1)[s], strip.sizes(0)[s], strip.cols[s]
            flat = strip.starts(0)[s]
            act[PAD + start : PAD + start + cols, :] = above_ref[edge : edge + cols, :].astype(f32)
            act[PAD + start + cols : PAD + start + cols + size, :] = dz_ref[flat : flat + size, :].astype(f32)
            act[PAD + start + cols + size : PAD + start + 2 * cols + size, :] = below_ref[
                edge : edge + cols, :
            ].astype(f32)
            edge += cols
        shifted_copies(strip, 1, act, wide, depth)
        patches(strip, 0, wide, cells, depth, flip=True)
        total[...] = jnp.zeros(total.shape, f32)

    for ky in range(3):
        @pl.when(step == ky)
        def _():
            value = total[...]
            for kx in range(3):
                tap = 3 * ky + kx
                value += mm(cells[:, tap * depth : (tap + 1) * depth], w_ref[kx * depth : (kx + 1) * depth, :], NT)
            total[...] = value

    @pl.when(step == 2)
    def _():
        if last:
            fine = strip.sizes(0)[0]
            coarse = jnp.concatenate(
                [
                    total[st : st + size, :] * (0.25**s)
                    for s, (st, size) in enumerate(zip(strip.starts(0), strip.sizes(0)))
                    if s
                ],
                axis=0,
            )
            out_ref[...] = total[:fine, :] + split_mm(spread_ref[...], coarse)
        else:
            out_ref[...] = (total[...] * scale_ref[...] * slope(p_ref[...])).astype(bf16)


def vmem(shape=None, index=None):
    if shape is None:
        return pl.BlockSpec(memory_space=pltpu.VMEM)
    return pl.BlockSpec(shape, index)


SMEM = pl.BlockSpec(memory_space=pltpu.SMEM)
ANY = pl.BlockSpec(memory_space=pl.ANY)


def params():
    return pltpu.CompilerParams(vmem_limit_bytes=VMEM_LIMIT)


def forward(strip, place, x, conv, scale, shift):
    depth = x.shape[1]
    own = strip.total(0)
    wide_rows = strip.total(3)
    return pl.pallas_call(
        functools.partial(forward_kernel, strip, depth),
        name="forward",
        out_shape=[jax.ShapeDtypeStruct((own, depth), f32)] * 3
        + [jax.ShapeDtypeStruct((own, 9 * depth), bf16)] * 3
        + [jax.ShapeDtypeStruct((own, depth), bf16)],
        in_specs=[SMEM, vmem(), ANY, vmem(), vmem()],
        out_specs=[vmem()] * 3 + [ANY] * 3 + [vmem()],
        scratch_shapes=[
            pltpu.VMEM(conv.shape, bf16),
            pltpu.VMEM((wide_rows + 2 * PAD, depth), f32),
            pltpu.VMEM((wide_rows, 3 * depth), bf16),
            pltpu.VMEM((strip.total(2), 9 * depth), bf16),
            pltpu.SemaphoreType.DMA((LAYERS,)),
            pltpu.SemaphoreType.DMA((SCALES,)),
        ],
        compiler_params=params(),
    )(place, x, conv, scale, shift)


def head(strip, place, a3, weight, gain, join, cot, share, where, spread, scale, p2):
    own, depth = a3.shape
    total = weight.shape[1]
    fine = strip.sizes(0)[0]
    ch = HEAD_CH
    gather = spread.T

    def whole(array):
        return pl.BlockSpec(array.shape, lambda t: (0,) * array.ndim)

    def part(rows):
        return pl.BlockSpec((rows, ch), lambda t: (0, t))

    return pl.pallas_call(
        functools.partial(head_kernel, strip),
        name="heads",
        grid=(total // ch,),
        out_shape=[
            jax.ShapeDtypeStruct((fine, total), bf16),
            jax.ShapeDtypeStruct((1, ch), f32),
            jax.ShapeDtypeStruct((SCALES, total), f32),
            jax.ShapeDtypeStruct((1, total), f32),
            jax.ShapeDtypeStruct((depth, total), bf16),
            jax.ShapeDtypeStruct((own, depth), bf16),
        ],
        in_specs=[
            SMEM, whole(a3), part(depth), part(1), part(SCALES), part(fine), whole(share), whole(where),
            whole(spread), whole(gather), whole(scale), whole(p2),
        ],
        out_specs=[
            part(fine),
            pl.BlockSpec((1, ch), lambda t: (0, 0)),
            part(SCALES),
            part(1),
            part(depth),
            pl.BlockSpec((own, depth), lambda t: (0, 0)),
        ],
        scratch_shapes=[pltpu.VMEM((own, depth), f32)],
        compiler_params=params(),
    )(place, a3, weight, gain, join, cot, share, where, spread, gather, scale, p2)


def weight_grad(layer, cells, dz, into):
    own, depth = dz.shape
    extra = [] if into is None else [into]
    return pl.pallas_call(
        weight_grad_kernel,
        name="weight_grad",
        grid=(9,),
        out_shape=jax.ShapeDtypeStruct((LAYERS * 9 * depth, depth), bf16),
        in_specs=[
            pl.BlockSpec((own, depth), lambda t: (0, t)),
            pl.BlockSpec((own, depth), lambda t: (0, 0)),
        ]
        + [ANY] * len(extra),
        out_specs=pl.BlockSpec((depth, depth), lambda t: (layer * 9 + t, 0)),
        input_output_aliases={} if into is None else {2: 0},
        compiler_params=params(),
    )(cells, dz, *extra)


def data_grad(strip, layer, dz, above, below, conv, others):
    own, depth = dz.shape
    last = layer == 0

    def whole(array):
        return pl.BlockSpec(array.shape, lambda t: (0, 0))

    out = (strip.sizes(0)[0], depth) if last else (own, depth)
    return pl.pallas_call(
        functools.partial(data_grad_kernel, strip, depth, last),
        name="data_grad",
        grid=(3,),
        out_shape=jax.ShapeDtypeStruct(out, f32 if last else bf16),
        in_specs=[whole(dz), whole(above), whole(below), pl.BlockSpec((3 * depth, depth), lambda t: (layer * 3 + t, 0))]
        + [whole(o) for o in others],
        out_specs=pl.BlockSpec(out, lambda t: (0, 0)),
        scratch_shapes=[
            pltpu.VMEM((strip.total(1) + 2 * PAD, depth), f32),
            pltpu.VMEM((strip.total(1), 3 * depth), bf16),
            pltpu.VMEM((own, 9 * depth), bf16),
            pltpu.VMEM((own, depth), f32),
        ],
        compiler_params=params(),
    )(dz, above, below, conv, *others)


def from_neighbour(cells, distance, axis):
    count = lax.axis_size(axis)
    pairs = [(i, i + distance) for i in range(count) if 0 <= i + distance < count]
    return lax.ppermute(cells, axis, pairs)


def with_rows(strip, levels, axis):
    halo = 3
    above = [[] for _ in levels]
    below = [[] for _ in levels]
    left = [halo] * len(levels)
    distance = 1
    while max(left) > 0:
        take = [min(n, r) for n, r in zip(left, strip.rows)]
        tails = [v[v.shape[0] - t * c :] for v, t, c in zip(levels, take, strip.cols) if t]
        heads = [v[: t * c] for v, t, c in zip(levels, take, strip.cols) if t]
        got_tail = from_neighbour(jnp.concatenate(tails, axis=0), distance, axis)
        got_head = from_neighbour(jnp.concatenate(heads, axis=0), -distance, axis)
        at = 0
        for s, (t, c) in enumerate(zip(take, strip.cols)):
            if t:
                above[s].insert(0, got_tail[at : at + t * c])
                below[s].append(got_head[at : at + t * c])
                at += t * c
        left = [n - t for n, t in zip(left, take)]
        distance += 1
    pieces = []
    for s, v in enumerate(levels):
        pieces += above[s] + [v] + below[s]
    return jnp.concatenate(pieces, axis=0)


def edges(strip, dz, axis):
    starts, sizes = strip.starts(0), strip.sizes(0)
    head_rows = jnp.concatenate([dz[st : st + c] for st, c in zip(starts, strip.cols)], axis=0)
    tail_rows = jnp.concatenate([dz[st + n - c : st + n] for st, n, c in zip(starts, sizes, strip.cols)], axis=0)
    return from_neighbour(tail_rows, 1, axis), from_neighbour(head_rows, -1, axis)


def shards(
    features,
    conv_master,
    head_master,
    scale_master,
    join_master,
    affine_scale,
    affine_shift,
    head_cotangent,
    pool_cotangent,
    box_counts,
    proposals,
):
    images, rows, cols, depth = features.shape
    total = head_master.shape[1]
    strip = Strip(rows, cols)
    every = ("dp", "space")
    conv_full = lax.all_gather(conv_master.astype(bf16), every, axis=0, tiled=True)
    head_full = lax.all_gather(head_master.astype(bf16), every, axis=0, tiled=True)
    small = jnp.concatenate([scale_master, join_master]).astype(bf16)[None]
    small = lax.all_gather(small, every, axis=0, tiled=True).astype(f32)
    own_gain = scale_master.shape[0]
    gain = small[:, :own_gain].reshape(1, total)
    join = small[:, own_gain:].reshape(SCALES, total)

    place = jnp.stack([lax.axis_index("space"), jnp.int32(lax.axis_size("space")), box_counts[0]]).astype(jnp.int32)
    spread = jnp.asarray(spread_matrix(strip), bf16)
    fine = features.reshape(rows * cols, depth)
    means = []
    for s in range(1, SCALES):
        at = strip.starts(0)[s] - strip.starts(0)[1]
        pick = spread[:, at : at + strip.sizes(0)[s]]
        means.append((mm(pick, fine, TN) * (0.25**s)).astype(bf16))
    x = with_rows(strip, [fine] + means, "space")
    p0, p1, p2, c0, c1, c2, a3 = forward(strip, place, x, conv_full, affine_scale, affine_shift)
    pre, cells = (p0, p1, p2), (c0, c1, c2)

    count = box_counts.astype(f32)[:, None]
    share = pool_cotangent / count
    maps, pool, join_grad, gain_grad, head_grad, dz = head(
        strip, place, a3, head_full, gain, join, head_cotangent.reshape(rows * cols, total), share, proposals,
        spread, affine_scale[2:3], p2,
    )
    pooled = lax.psum(pool, "space") / count
    grad = None
    for layer in (2, 1, 0):
        above, below = edges(strip, dz, "space")
        grad = weight_grad(layer, cells[layer], dz, grad)
        if layer:
            dz = data_grad(
                strip, layer, dz, above, below, conv_full, [affine_scale[layer - 1 : layer], pre[layer - 1]]
            )
        else:
            input_grad = data_grad(strip, layer, dz, above, below, conv_full, [spread])
    conv_grad = lax.psum_scatter(grad, every, scatter_dimension=0, tiled=True).astype(f32)
    head_grad = lax.psum_scatter(head_grad, every, scatter_dimension=0, tiled=True).astype(f32)
    ranks = small.shape[0]
    small_grad = jnp.concatenate([gain_grad.reshape(ranks, -1), join_grad.reshape(ranks, -1)], axis=1)
    small_grad = lax.psum_scatter(small_grad, every, scatter_dimension=0, tiled=True)
    return (
        maps.reshape(images, rows, cols, total),
        pooled,
        input_grad.reshape(images, rows, cols, depth),
        conv_grad,
        head_grad,
        small_grad[0, :own_gain],
        small_grad[0, own_gain:],
    )


def solution(mesh):
    return jax.shard_map(
        shards,
        mesh=mesh,
        in_specs=(
            P("dp", "space", None, None),
            P(("dp", "space"), None),
            P(("dp", "space"), None),
            P(("dp", "space")),
            P(("dp", "space")),
            P(),
            P(),
            P("dp", "space", None, None),
            P("dp", None),
            P("dp"),
            P("dp", None),
        ),
        out_specs=(
            P("dp", "space", None, None),
            P("dp", None),
            P("dp", "space", None, None),
            P(("dp", "space"), None),
            P(("dp", "space"), None),
            P(("dp", "space")),
            P(("dp", "space")),
        ),
        check_vma=False,
    )
```

```python
import functools

import jax
import jax.numpy as jnp
import numpy as np
from jax import lax
from jax.experimental import pallas as pl
from jax.experimental.pallas import tpu as pltpu
from jax.sharding import PartitionSpec as P

HEAD_CH = 256
TASK_HEADS = 7
SCALES = 3
LAYERS = 3
PAD = 8
VMEM_LIMIT = 56 << 20

epsilon = 1e-06
f32 = jnp.float32
bf16 = jnp.bfloat16
NN = (((1,), (0,)), ((), ()))
NT = (((1,), (1,)), ((), ()))
TN = (((0,), (0,)), ((), ()))


def mm(left, right, dims=NN):
    return lax.dot_general(left, right, dims, preferred_element_type=f32)


def split_mm(left, right):
    high = right.astype(bf16)
    low = (right - high.astype(f32)).astype(bf16)
    return mm(left, high) + mm(left, low)


class Strip:
    def __init__(self, rows, cols):
        self.rows = [rows >> s for s in range(SCALES)]
        self.cols = [cols >> s for s in range(SCALES)]

    def sizes(self, halo):
        return [(r + 2 * halo) * c for r, c in zip(self.rows, self.cols)]

    def starts(self, halo):
        sizes = self.sizes(halo)
        return [sum(sizes[:s]) for s in range(SCALES)]

    def total(self, halo):
        return sum(self.sizes(halo))

    def own(self, halo):
        return [st + halo * c for st, c in zip(self.starts(halo), self.cols)]


def spread_matrix(strip):
    rows, cols = strip.rows[0], strip.cols[0]
    parts = []
    for s in range(1, SCALES):
        mat = np.zeros((rows * cols, strip.rows[s] * strip.cols[s]), np.float32)
        for r in range(rows):
            for c in range(cols):
                mat[r * cols + c, (r >> s) * strip.cols[s] + (c >> s)] = 1.0
        parts.append(mat)
    return np.concatenate(parts, axis=1)


def column_of(strip, scale, count):
    return lax.broadcasted_iota(jnp.int32, (count, 1), 0) % strip.cols[scale]


def shifted_copies(strip, halo, act, wide, depth):
    for s in range(SCALES):
        start, count, cols = strip.starts(halo)[s], strip.sizes(halo)[s], strip.cols[s]
        column = column_of(strip, s, count)
        for k in range(3):
            rows = act[PAD + start + k - 1 : PAD + start + k - 1 + count, :]
            if k == 0:
                rows = jnp.where(column == 0, 0.0, rows)
            if k == 2:
                rows = jnp.where(column == cols - 1, 0.0, rows)
            wide[start : start + count, k * depth : (k + 1) * depth] = rows.astype(bf16)


def patches(strip, halo, wide, cells, depth, flip=False):
    for s in range(SCALES):
        cols = strip.cols[s]
        count = strip.sizes(halo)[s]
        source, target = strip.starts(halo + 1)[s], strip.starts(halo)[s]
        for ky in range(3):
            first = source + (2 - ky if flip else ky) * cols
            for kx in range(3):
                col = (2 - kx if flip else kx) * depth
                tap = 3 * ky + kx
                cells[target : target + count, tap * depth : (tap + 1) * depth] = wide[
                    first : first + count, col : col + depth
                ]


FLIPS = ((1, 2), (2, 1))
TURNS = (0, 1, 3, 2)


def across(place, part, core):
    rank = place[0]
    for bit in range(2):
        if part >> bit & 1:
            rank = rank ^ jnp.where(core == 0, FLIPS[0][bit], FLIPS[1][bit])
    return rank


def load_staged(conv_rows, head_rows, head_cols, place, refs, weights, head_w, small, w_sem, h_sem):
    depth = weights.shape[1]
    layer_rows = weights.shape[0] // LAYERS
    last = [-(-layer_rows * (n + 1) // conv_rows) for n in range(LAYERS)]
    pieces = -(-head_cols // depth)
    for n, turn in enumerate(TURNS):
        for part in range(8):
            ref = refs[5 * n + min(part, 4)]
            if part >= 4:
                ref = ref.at[part - 4]
            core = place[4] if part < 4 else 1 - place[4]
            z = (place[3] + 4 - turn) % 4
            k = (z * 2 + core) * 4 + across(place, part % 4, core)
            layer = sum((k >= n).astype(jnp.int32) for n in last[:-1])
            pltpu.make_async_copy(
                ref.at[pl.ds(0, conv_rows), :],
                weights.at[pl.ds(pl.multiple_of(k * conv_rows, 16), conv_rows), :],
                w_sem.at[layer],
            ).start()
            for piece in range(pieces):
                width = min(depth, head_cols - piece * depth)
                pltpu.make_async_copy(
                    ref.at[pl.ds(conv_rows + piece * head_rows, head_rows), pl.ds(0, width)],
                    head_w.at[pl.ds(pl.multiple_of(k * head_rows, 16), head_rows), pl.ds(piece * depth, width)],
                    h_sem.at[0],
                ).start()
            pltpu.make_async_copy(
                ref.at[pl.ds(conv_rows + (pieces - 1) * head_rows, head_rows), pl.ds(width, depth - width)],
                small.at[pl.ds(pl.multiple_of(k * head_rows, 16), head_rows), :],
                h_sem.at[1],
            ).start()
    waits = []
    before = 0
    for layer in range(LAYERS):
        rows = weights.at[pl.ds(before * conv_rows, (last[layer] - before) * conv_rows), :]
        waits.append(pltpu.make_async_copy(rows, rows, w_sem.at[layer]))
        before = last[layer]
    return waits, [pltpu.make_async_copy(head_w, head_w, h_sem.at[0]), pltpu.make_async_copy(small, small, h_sem.at[1])]


def forward_kernel(strip, depth, staged, *refs):
    taps = 9 * depth
    place, x_ref, scale_ref, shift_ref = refs[:4]
    refs = refs[4:]
    if staged is None:
        w_hbm = refs[0]
        refs = refs[1:]
    else:
        conv_rows, head_rows, head_cols = staged
        blocks, refs = refs[: 5 * len(TURNS)], refs[5 * len(TURNS) :]
    p_refs, c_hbms, a3_ref, refs = refs[:3], refs[3:6], refs[6], refs[7:]
    if staged is not None:
        full_hbm, head_ref, small_ref = refs[:3]
        refs = refs[3:]
    weights, act, wide, cells, w_sem, c_sem = refs[:6]
    if staged is None:
        loads = []
        for layer in range(LAYERS):
            copy = pltpu.make_async_copy(
                w_hbm.at[pl.ds(layer * taps, taps), :], weights.at[pl.ds(layer * taps, taps), :], w_sem.at[layer]
            )
            copy.start()
            loads.append(copy)
    else:
        h_sem, f_sem = refs[6:]
        loads, head_loads = load_staged(
            conv_rows, head_rows, head_cols, place, blocks, weights, head_ref, small_ref, w_sem, h_sem
        )
    here, ranks = place[0], place[1]
    first_in = strip.total(3)
    act[PAD : PAD + first_in, :] = x_ref[...].astype(f32)
    stores = []
    fulls = []
    for layer in range(LAYERS):
        halo = LAYERS - 1 - layer
        count = strip.total(halo)
        shifted_copies(strip, halo + 1, act, wide, depth)
        for copy in stores:
            copy.wait()
        patches(strip, halo, wide, cells, depth)
        stores = []
        own = strip.own(halo)
        flat = strip.starts(0)
        for s in range(SCALES):
            size = strip.sizes(0)[s]
            copy = pltpu.make_async_copy(
                cells.at[pl.ds(own[s], size), :], c_hbms[layer].at[pl.ds(flat[s], size), :], c_sem.at[s]
            )
            copy.start()
            stores.append(copy)
        loads[layer].wait()
        if staged is not None:
            rows = pl.ds(layer * taps, taps)
            copy = pltpu.make_async_copy(weights.at[rows, :], full_hbm.at[rows, :], f_sem.at[layer])
            copy.start()
            fulls.append(copy)
        for half in range(depth // 256):
            lanes = slice(half * 256, (half + 1) * 256)
            z = mm(cells[:count, :], weights[layer * taps : (layer + 1) * taps, lanes])
            p = z * scale_ref[layer : layer + 1, lanes] + shift_ref[layer : layer + 1, lanes]
            a = (p / (1.0 + jnp.exp(-p))).astype(bf16)
            for s in range(SCALES):
                size = strip.sizes(0)[s]
                p_refs[layer][flat[s] : flat[s] + size, lanes] = p[own[s] : own[s] + size]
            if layer == LAYERS - 1:
                a3_ref[:, lanes] = a
            else:
                for s in range(SCALES):
                    start, size = strip.starts(halo)[s], strip.sizes(halo)[s]
                    row = lax.broadcasted_iota(jnp.int32, (size, 1), 0) // strip.cols[s]
                    row = row + here * strip.rows[s] - halo
                    inside = (row >= 0) & (row < ranks * strip.rows[s])
                    act[PAD + start : PAD + start + size, lanes] = jnp.where(
                        inside, a[start : start + size].astype(f32), 0.0
                    )
    for copy in stores + fulls:
        copy.wait()
    if staged is not None:
        for copy in head_loads:
            copy.wait()


def slope(p):
    sigma = 1.0 / (1.0 + jnp.exp(-p))
    return sigma * (1.0 + p * (1.0 - sigma))


def head_kernel(
    strip, place, a3_ref, w_ref, gain_ref, join_ref, cot_ref, share_ref, where_ref, spread_ref, gather_ref,
    scale_ref, p2_ref,
    maps_ref, pool_ref, join_grad_ref, gain_grad_ref, w_grad_ref, dz_ref, *refs
):
    da3 = refs[-1]
    halves = refs[:-1]
    head = pl.program_id(0)
    fine = strip.sizes(0)[0]
    starts, sizes = strip.starts(0), strip.sizes(0)
    a3 = a3_ref[...]
    weight = w_ref[...]
    g = mm(a3, weight)
    inverse = lax.rsqrt(jnp.sum(g * g, axis=-1, keepdims=True) + epsilon)
    unit = g * inverse
    gain = gain_ref[...]
    normed = unit * gain
    join = join_ref[...]
    coarse = jnp.concatenate(
        [normed[starts[s] : starts[s] + sizes[s]] * join[s : s + 1] for s in range(1, SCALES)], axis=0
    )
    joined = normed[:fine] * join[0:1] + split_mm(spread_ref[...], coarse)
    maps_ref[...] = joined.astype(bf16)
    slots = where_ref.shape[1]
    first = place[0] * fine
    pixel = lax.broadcasted_iota(jnp.int32, (fine, slots), 0) + first
    slot = lax.broadcasted_iota(jnp.int32, (fine, slots), 1)
    hits = jnp.where((where_ref[...] == pixel) & (slot < place[2]) & (head == 0), 1.0, 0.0)
    hits = jnp.sum(hits, axis=-1, keepdims=True)

    @pl.when(head == 0)
    def _():
        pool_ref[...] = jnp.sum(joined * hits, axis=0, keepdims=True)

    fused = cot_ref[...].astype(f32) + hits * share_ref[...]
    down_coarse = split_mm(gather_ref[...], fused)
    down = jnp.concatenate([fused, down_coarse], axis=0)
    product = down * normed
    scaled = []
    for s in range(SCALES):
        part = slice(starts[s], starts[s] + sizes[s])
        join_grad_ref[s : s + 1, :] = jnp.sum(product[part], axis=0, keepdims=True)
        scaled.append(down[part] * join[s : s + 1])
    dn = jnp.concatenate(scaled, axis=0)
    gain_grad_ref[...] = jnp.sum(dn * unit, axis=0, keepdims=True)
    du = dn * gain
    dg = (inverse * (du - unit * jnp.sum(du * unit, axis=-1, keepdims=True))).astype(bf16)
    w_grad_ref[...] = dg if halves else mm(a3, dg, TN).astype(w_grad_ref.dtype)
    part = mm(dg, weight, NT)

    @pl.when(head == 0)
    def _():
        da3[...] = part

    @pl.when(head > 0)
    def _():
        da3[...] += part

    @pl.when(head == pl.num_programs(0) - 1)
    def _():
        emit_grad(place, (da3[...] * scale_ref[...] * slope(p2_ref[...])).astype(bf16), dz_ref, halves)


def emit_grad(place, dz, dz_ref, halves):
    dz_ref[...] = dz
    if halves:
        middle = dz.shape[1] // 2
        left, right = dz[:, :middle], dz[:, middle:]
        first = place[4] == 0
        halves[0][...] = jnp.where(first, left, right)
        halves[1][...] = jnp.where(first, right, left)


def store_blocks(place, pieces, block_refs, sem):
    for turn in range(4):
        for part in range(4):
            out = block_refs[4 * turn + part]
            z = (place[3] + turn) % 4
            rank = across(place, part, place[4])
            for core in range(2):
                k = (z * 2 + core) * 4 + rank
                base = core * (out.shape[0] // 2)
                for condition, source, row in pieces(k):
                    copy = pltpu.make_async_copy(source, out.at[pl.ds(base + row, source.shape[0]), :], sem)
                    if condition is None:
                        copy.start()
                    else:
                        pl.when(condition)(copy.start)


def chip_weight_grad_kernel(layer, conv_rows, place, cells_ref, other_ref, keep_ref, got_ref, *refs):
    refs = refs[-(16 + 5) :]
    outs, (cells, result, dz, in_sem, out_sem) = refs[:16], refs[16:]
    own, depth = keep_ref.shape[0], cells.shape[2]
    loads = []
    for tap in range(9):
        lanes = pl.ds(tap * depth, depth)
        pair = [
            pltpu.make_async_copy(src.at[:, lanes], cells.at[tap, pl.ds(n * own, own), :], in_sem.at[tap])
            for n, src in enumerate((cells_ref, other_ref))
        ]
        for copy in pair:
            copy.start()
        loads.append(pltpu.make_async_copy(cells.at[tap], cells.at[tap], in_sem.at[tap]))
    dz[:own, :] = keep_ref[...]
    dz[own:, :] = got_ref[...]
    for tap in range(9):
        loads[tap].wait()
        result[tap * depth : (tap + 1) * depth, :] = mm(cells[tap], dz[...], TN).astype(bf16)
    rows = 9 * depth
    first_row, stop_row = layer * rows, (layer + 1) * rows

    def pieces(k):
        out = []
        inside = (k * conv_rows >= first_row) & ((k + 1) * conv_rows <= stop_row)
        start = jnp.where(inside, k * conv_rows - first_row, 0)
        out.append((inside, result.at[pl.ds(pl.multiple_of(start, 16), conv_rows), :], 0))
        if first_row % conv_rows:
            size = conv_rows - first_row % conv_rows
            out.append((k == first_row // conv_rows, result.at[pl.ds(0, size), :], conv_rows - size))
        if stop_row % conv_rows:
            size = stop_row % conv_rows
            out.append((k == stop_row // conv_rows, result.at[pl.ds(rows - size, size), :], 0))
        return out

    store_blocks(place, pieces, outs, out_sem)
    pltpu.make_async_copy(result, result, out_sem).wait()


def chip_head_grad_kernel(conv_rows, place, a3_ref, other_ref, keep_ref, got_ref, small_ref, *refs):
    refs = refs[-(16 + 4) :]
    outs, (a3, dg, result, out_sem) = refs[:16], refs[16:]
    own = a3_ref.shape[0]
    a3[:own, :] = a3_ref[...]
    a3[own:, :] = other_ref[...]
    dg[:own, :] = keep_ref[...]
    dg[own:, :] = got_ref[...]
    width = result.shape[2]
    cols = dg.shape[1]
    for piece in range(result.shape[0]):
        stop = min(cols, (piece + 1) * width)
        lanes = slice(piece * width, stop)
        result[piece, :, : stop - piece * width] = mm(a3[...], dg[:, lanes], TN).astype(bf16)
    result[result.shape[0] - 1, :, cols % width :] = small_ref[...]
    rows = (outs[0].shape[0] // 2 - conv_rows) // result.shape[0]

    def pieces(k):
        return [
            (None, result.at[piece, pl.ds(pl.multiple_of(k * rows, 16), rows), :], conv_rows + piece * rows)
            for piece in range(result.shape[0])
        ]

    store_blocks(place, pieces, outs, out_sem)
    pltpu.make_async_copy(result, result, out_sem).wait()


def weight_grad_kernel(cells_ref, dz_ref, *refs):
    out_ref = refs[-1]
    out_ref[...] = mm(cells_ref[...], dz_ref[...], TN).astype(out_ref.dtype)


def data_grad_kernel(
    strip, depth, last, place, dz_ref, above_ref, below_ref, w_ref, *refs
):
    refs, (act, wide, cells, total) = refs[:-4], refs[-4:]
    if last:
        spread_ref, out_ref = refs
    else:
        scale_ref, p_ref, out_ref, *halves = refs
    step = pl.program_id(0)

    @pl.when(step == 0)
    def _():
        edge = 0
        for s in range(SCALES):
            start, size, cols = strip.starts(1)[s], strip.sizes(0)[s], strip.cols[s]
            flat = strip.starts(0)[s]
            act[PAD + start : PAD + start + cols, :] = above_ref[edge : edge + cols, :].astype(f32)
            act[PAD + start + cols : PAD + start + cols + size, :] = dz_ref[flat : flat + size, :].astype(f32)
            act[PAD + start + cols + size : PAD + start + 2 * cols + size, :] = below_ref[
                edge : edge + cols, :
            ].astype(f32)
            edge += cols
        shifted_copies(strip, 1, act, wide, depth)
        patches(strip, 0, wide, cells, depth, flip=True)
        total[...] = jnp.zeros(total.shape, f32)

    for ky in range(3):
        @pl.when(step == ky)
        def _():
            value = total[...]
            for kx in range(3):
                tap = 3 * ky + kx
                value += mm(cells[:, tap * depth : (tap + 1) * depth], w_ref[kx * depth : (kx + 1) * depth, :], NT)
            total[...] = value

    @pl.when(step == 2)
    def _():
        if last:
            fine = strip.sizes(0)[0]
            coarse = jnp.concatenate(
                [
                    total[st : st + size, :] * (0.25**s)
                    for s, (st, size) in enumerate(zip(strip.starts(0), strip.sizes(0)))
                    if s
                ],
                axis=0,
            )
            out_ref[...] = total[:fine, :] + split_mm(spread_ref[...], coarse)
        else:
            emit_grad(place, (total[...] * scale_ref[...] * slope(p_ref[...])).astype(bf16), out_ref, halves)


def vmem(shape=None, index=None):
    if shape is None:
        return pl.BlockSpec(memory_space=pltpu.VMEM)
    return pl.BlockSpec(shape, index)


SMEM = pl.BlockSpec(memory_space=pltpu.SMEM)
ANY = pl.BlockSpec(memory_space=pl.ANY)


def params():
    return pltpu.CompilerParams(vmem_limit_bytes=VMEM_LIMIT)


def forward(strip, place, x, conv, scale, shift, head_cols):
    depth = x.shape[1]
    own = strip.total(0)
    wide_rows = strip.total(3)
    rows = LAYERS * 9 * depth
    staged, inputs = None, [conv]
    outs = (
        [jax.ShapeDtypeStruct((own, depth), f32)] * 3
        + [jax.ShapeDtypeStruct((own, 9 * depth), bf16)] * 3
        + [jax.ShapeDtypeStruct((own, depth), bf16)]
    )
    out_specs = [vmem()] * 3 + [ANY] * 3 + [vmem()]
    sems = [pltpu.SemaphoreType.DMA((LAYERS,)), pltpu.SemaphoreType.DMA((SCALES,))]
    if isinstance(conv, tuple):
        staged, inputs = (*conv[0], head_cols), conv[1]
        spare = -head_cols % depth
        outs += [
            jax.ShapeDtypeStruct((rows, depth), bf16),
            jax.ShapeDtypeStruct((depth, head_cols), bf16),
            jax.ShapeDtypeStruct((depth, spare), bf16),
        ]
        out_specs += [ANY, vmem(), vmem()]
        sems += [pltpu.SemaphoreType.DMA((2,)), pltpu.SemaphoreType.DMA((LAYERS,))]
    return pl.pallas_call(
        functools.partial(forward_kernel, strip, depth, staged),
        name="forward",
        out_shape=outs,
        in_specs=[SMEM, vmem(), vmem(), vmem()] + [ANY] * len(inputs),
        out_specs=out_specs,
        scratch_shapes=[
            pltpu.VMEM((rows, depth), bf16),
            pltpu.VMEM((wide_rows + 2 * PAD, depth), f32),
            pltpu.VMEM((wide_rows, 3 * depth), bf16),
            pltpu.VMEM((strip.total(2), 9 * depth), bf16),
        ]
        + sems,
        compiler_params=params(),
    )(place, x, scale, shift, *inputs)


def head(strip, place, a3, weight, gain, join, cot, share, where, spread, scale, p2, staged):
    own, depth = a3.shape
    total = weight.shape[1]
    fine = strip.sizes(0)[0]
    ch = HEAD_CH
    gather = spread.T

    def whole(array):
        return pl.BlockSpec(array.shape, lambda t: (0,) * array.ndim)

    def part(rows):
        return pl.BlockSpec((rows, ch), lambda t: (0, t))

    return pl.pallas_call(
        functools.partial(head_kernel, strip),
        name="heads",
        grid=(total // ch,),
        out_shape=[
            jax.ShapeDtypeStruct((fine, total), bf16),
            jax.ShapeDtypeStruct((1, ch), f32),
            jax.ShapeDtypeStruct((SCALES, total), f32),
            jax.ShapeDtypeStruct((1, total), f32),
            jax.ShapeDtypeStruct((own if staged else depth, total), bf16),
            jax.ShapeDtypeStruct((own, depth), bf16),
        ]
        + [jax.ShapeDtypeStruct((own, depth // 2), bf16)] * (2 * staged),
        in_specs=[
            SMEM, whole(a3), part(depth), part(1), part(SCALES), part(fine), whole(share), whole(where),
            whole(spread), whole(gather), whole(scale), whole(p2),
        ],
        out_specs=[
            part(fine),
            pl.BlockSpec((1, ch), lambda t: (0, 0)),
            part(SCALES),
            part(1),
            part(own if staged else depth),
            pl.BlockSpec((own, depth), lambda t: (0, 0)),
        ]
        + [pl.BlockSpec((own, depth // 2), lambda t: (0, 0))] * (2 * staged),
        scratch_shapes=[pltpu.VMEM((own, depth), f32)],
        compiler_params=params(),
    )(place, a3, weight, gain, join, cot, share, where, spread, gather, scale, p2)


def chip_weight_grad(layer, place, cells, other, keep, got, blocks, rows, conv_rows):
    own, half = keep.shape
    depth = cells.shape[1] // 9
    blocks = blocks or []
    return pl.pallas_call(
        functools.partial(chip_weight_grad_kernel, layer, conv_rows),
        name="chip_weight_grad",
        out_shape=[jax.ShapeDtypeStruct((rows, half), bf16)] * 16,
        in_specs=[SMEM, ANY, ANY, vmem(), vmem()] + [ANY] * len(blocks),
        out_specs=[ANY] * 16,
        scratch_shapes=[
            pltpu.VMEM((9, 2 * own, depth), bf16),
            pltpu.VMEM((9 * depth, half), bf16),
            pltpu.VMEM((2 * own, half), bf16),
            pltpu.SemaphoreType.DMA((9,)),
            pltpu.SemaphoreType.DMA,
        ],
        input_output_aliases={5 + n: n for n in range(len(blocks))},
        compiler_params=params(),
    )(place, cells, other, keep, got, *blocks)


def chip_head_grad(place, a3, other, keep, got, small, blocks, conv_rows):
    own, depth = a3.shape
    half = blocks[0].shape[1]
    pieces = -(-keep.shape[1] // half)
    return pl.pallas_call(
        functools.partial(chip_head_grad_kernel, conv_rows),
        name="chip_head_grad",
        out_shape=[jax.ShapeDtypeStruct(b.shape, bf16) for b in blocks],
        in_specs=[SMEM] + [vmem()] * 5 + [ANY] * 16,
        out_specs=[ANY] * 16,
        scratch_shapes=[
            pltpu.VMEM((2 * own, depth), bf16),
            pltpu.VMEM((2 * own, keep.shape[1]), bf16),
            pltpu.VMEM((pieces, depth, half), bf16),
            pltpu.SemaphoreType.DMA,
        ],
        input_output_aliases={6 + n: n for n in range(16)},
        compiler_params=params(),
    )(place, a3, other, keep, got, small, *blocks)


def weight_grad(layer, cells, dz, into):
    own, depth = dz.shape
    extra = [] if into is None else [into]
    return pl.pallas_call(
        weight_grad_kernel,
        name="weight_grad",
        grid=(9,),
        out_shape=jax.ShapeDtypeStruct((LAYERS * 9 * depth, depth), bf16),
        in_specs=[
            pl.BlockSpec((own, depth), lambda t: (0, t)),
            pl.BlockSpec((own, depth), lambda t: (0, 0)),
        ]
        + [ANY] * len(extra),
        out_specs=pl.BlockSpec((depth, depth), lambda t: (layer * 9 + t, 0)),
        input_output_aliases={} if into is None else {2: 0},
        compiler_params=params(),
    )(cells, dz, *extra)


def data_grad(strip, layer, place, dz, above, below, conv, others, staged):
    own, depth = dz.shape
    last = layer == 0
    split = staged and not last

    def whole(array):
        return pl.BlockSpec(array.shape, lambda t: (0, 0))

    out = (strip.sizes(0)[0], depth) if last else (own, depth)
    return pl.pallas_call(
        functools.partial(data_grad_kernel, strip, depth, last),
        name="data_grad",
        grid=(3,),
        out_shape=[jax.ShapeDtypeStruct(out, f32 if last else bf16)]
        + [jax.ShapeDtypeStruct((own, depth // 2), bf16)] * (2 * split),
        in_specs=[
            SMEM, whole(dz), whole(above), whole(below),
            pl.BlockSpec((3 * depth, depth), lambda t: (layer * 3 + t, 0)),
        ]
        + [whole(o) for o in others],
        out_specs=[pl.BlockSpec(out, lambda t: (0, 0))]
        + [pl.BlockSpec((own, depth // 2), lambda t: (0, 0))] * (2 * split),
        scratch_shapes=[
            pltpu.VMEM((strip.total(1) + 2 * PAD, depth), f32),
            pltpu.VMEM((strip.total(1), 3 * depth), bf16),
            pltpu.VMEM((own, 9 * depth), bf16),
            pltpu.VMEM((own, depth), f32),
        ],
        compiler_params=params(),
    )(place, dz, above, below, conv, *others)


def from_neighbour(cells, distance, axis):
    count = lax.axis_size(axis)
    pairs = [(i, i + distance) for i in range(count) if 0 <= i + distance < count]
    return lax.ppermute(cells, axis, pairs)


def with_rows(strip, levels, axis):
    halo = 3
    above = [[] for _ in levels]
    below = [[] for _ in levels]
    left = [halo] * len(levels)
    distance = 1
    while max(left) > 0:
        take = [min(n, r) for n, r in zip(left, strip.rows)]
        tails = [v[v.shape[0] - t * c :] for v, t, c in zip(levels, take, strip.cols) if t]
        heads = [v[: t * c] for v, t, c in zip(levels, take, strip.cols) if t]
        got_tail = from_neighbour(jnp.concatenate(tails, axis=0), distance, axis)
        got_head = from_neighbour(jnp.concatenate(heads, axis=0), -distance, axis)
        at = 0
        for s, (t, c) in enumerate(zip(take, strip.cols)):
            if t:
                above[s].insert(0, got_tail[at : at + t * c])
                below[s].append(got_head[at : at + t * c])
                at += t * c
        left = [n - t for n, t in zip(left, take)]
        distance += 1
    pieces = []
    for s, v in enumerate(levels):
        pieces += above[s] + [v] + below[s]
    return jnp.concatenate(pieces, axis=0)


def edges(strip, dz, axis):
    starts, sizes = strip.starts(0), strip.sizes(0)
    head_rows = jnp.concatenate([dz[st : st + c] for st, c in zip(starts, strip.cols)], axis=0)
    tail_rows = jnp.concatenate([dz[st + n - c : st + n] for st, n, c in zip(starts, sizes, strip.cols)], axis=0)
    return from_neighbour(tail_rows, 1, axis), from_neighbour(head_rows, -1, axis)


def after(value, *others):
    return lax.optimization_barrier((value,) + others)[0]


def turn_pairs(step):
    return [((z * 2 + c) * 4 + s, (((z + step) % 4) * 2 + c) * 4 + s) for z in range(4) for c in range(2) for s in range(4)]


def flip_pairs(which):
    return [((z * 2 + c) * 4 + s, (z * 2 + c) * 4 + (s ^ FLIPS[c][which])) for z in range(4) for c in range(2) for s in range(4)]


def core_pairs():
    return [((z * 2 + c) * 4 + s, (z * 2 + 1 - c) * 4 + s) for z in range(4) for c in range(2) for s in range(4)]


def staged_gather(every, conv, head_w, small):
    depth = conv.shape[1]
    pieces = [head_w[:, n : n + depth] for n in range(0, head_w.shape[1], depth)]
    spare = depth - pieces[-1].shape[1]
    filler = jnp.pad(small[None], ((0, head_w.shape[0] - 1), (0, spare - small.shape[0])))
    pieces[-1] = jnp.concatenate([pieces[-1], filler], axis=1)
    own = jnp.concatenate([conv] + pieces, axis=0)
    blocks = []
    for turn in TURNS:
        line = own if turn == 0 else lax.ppermute(own, every, turn_pairs(turn))
        one = lax.ppermute(line, every, flip_pairs(0))
        two = lax.ppermute(line, every, flip_pairs(1))
        both = lax.ppermute(one, every, flip_pairs(1))
        mine = [line, one, two, both]
        blocks += mine + [lax.ppermute(jnp.stack(mine), every, core_pairs())]
    return (conv.shape[0], head_w.shape[0]), blocks


def staged_scatter(every, blocks, core, conv_rows):
    def total(*terms):
        return sum((t.astype(f32) for t in terms[1:]), terms[0].astype(f32))

    whole = None
    for turn in TURNS[::-1]:
        mine, one, two, both = blocks[turn]
        both = lax.ppermute(both, every, flip_pairs(1))
        one = total(one, both).astype(bf16)
        two = lax.ppermute(two, every, flip_pairs(1))
        one = lax.ppermute(one, every, flip_pairs(0))
        part = total(mine, two, one)
        if turn:
            part = lax.ppermute(part.astype(bf16), every, turn_pairs(turn)).astype(f32)
        whole = part if whole is None else whole + part
    half = whole.shape[0] // 2
    keep = jnp.where(core == 0, whole[:half], whole[half:])
    give = jnp.where(core == 0, whole[half:], whole[:half])
    got = lax.ppermute(give, every, core_pairs())
    first, second = jnp.where(core == 0, keep, got), jnp.where(core == 0, got, keep)
    conv = jnp.concatenate([first[:conv_rows], second[:conv_rows]], axis=1)
    rows = (half - conv_rows) // 4

    def pieces(side):
        return [side[conv_rows + n * rows : conv_rows + (n + 1) * rows] for n in range(4)]

    left, right = pieces(first), pieces(second)
    lanes = left[3].shape[1] // 2
    heads = jnp.concatenate(left[:3] + [left[3][:, :lanes]] + right[:3] + [right[3][:, :lanes]], axis=1)
    small = left[3][:2, lanes:] + right[3][:2, lanes:]
    return conv, heads, small


def shards(
    features,
    conv_master,
    head_master,
    scale_master,
    join_master,
    affine_scale,
    affine_shift,
    head_cotangent,
    pool_cotangent,
    box_counts,
    proposals,
):
    images, rows, cols, depth = features.shape
    total = head_master.shape[1]
    strip = Strip(rows, cols)
    every = ("dp", "space")
    own_gain = scale_master.shape[0]
    small = jnp.concatenate([scale_master, join_master]).astype(bf16)
    conv_own, head_own = conv_master.astype(bf16), head_master.astype(bf16)
    staged = lax.axis_size("dp") == 8 and lax.axis_size("space") == 4
    line = lax.axis_index("dp")
    place = jnp.stack(
        [lax.axis_index("space"), jnp.int32(lax.axis_size("space")), box_counts[0], line // 2, line % 2]
    ).astype(jnp.int32)
    if staged:
        conv_full = staged_gather(every, conv_own, head_own, small)
    else:
        conv_full = lax.all_gather(conv_own, every, axis=0, tiled=True)
        head_full = lax.all_gather(head_own, every, axis=0, tiled=True)
        small = lax.all_gather(small[None], every, axis=0, tiled=True)
    spread = jnp.asarray(spread_matrix(strip), bf16)
    fine = features.reshape(rows * cols, depth)
    means = []
    for s in range(1, SCALES):
        at = strip.starts(0)[s] - strip.starts(0)[1]
        pick = spread[:, at : at + strip.sizes(0)[s]]
        means.append((mm(pick, fine, TN) * (0.25**s)).astype(bf16))
    levels = [fine] + means
    if staged:
        levels = [after(v, conv_full[1][1]) for v in levels]
    x = with_rows(strip, levels, "space")
    p0, p1, p2, c0, c1, c2, a3, *loaded = forward(strip, place, x, conv_full, affine_scale, affine_shift, total)
    if staged:
        conv_full, head_full, small = loaded
        small = small.reshape(-1, head_own.shape[0], small.shape[1])[:, 0]
    own_small = own_gain + join_master.shape[0]
    gain = small[:, :own_gain].astype(f32).reshape(1, total)
    join = small[:, own_gain:own_small].astype(f32).reshape(SCALES, total)
    pre, cells = (p0, p1, p2), (c0, c1, c2)

    count = box_counts.astype(f32)[:, None]
    share = pool_cotangent / count
    maps, pool, join_grad, gain_grad, head_grad, dz, *halves = head(
        strip, place, a3, head_full, gain, join, head_cotangent.reshape(rows * cols, total), share, proposals,
        spread, affine_scale[2:3], p2, staged,
    )
    pooled = lax.psum(pool, "space") / count
    ranks = lax.axis_size("dp") * lax.axis_size("space")
    small_grad = jnp.concatenate([gain_grad.reshape(ranks, -1), join_grad.reshape(ranks, -1)], axis=1)
    grad = None
    if staged:
        core = place[4]
        swap = functools.partial(lax.ppermute, axis_name=every, perm=core_pairs())
        half_cols = total // 2
        left, right = head_grad[:, :half_cols], head_grad[:, half_cols:]
        dg_keep = jnp.where(core == 0, left, right)
        dg_got = swap(jnp.where(core == 0, right, left))
        a3_got = swap(a3)
        small_rows = jnp.pad(
            small_grad.reshape(ranks, 2, -1),
            ((0, 0), (0, head_own.shape[0] - 2), (0, 128 - small_grad.shape[1] // 2)),
        ).astype(bf16)
        block_rows = 2 * (conv_own.shape[0] + 4 * head_own.shape[0])
    for layer in (2, 1, 0):
        above, below = edges(strip, dz, "space")
        if staged:
            keep, give = halves
            grad = chip_weight_grad(
                layer, place, cells[layer], swap(cells[layer]), keep, swap(give), grad, block_rows, conv_own.shape[0]
            )
            if layer == 2:
                grad = chip_head_grad(
                    place, a3, a3_got, dg_keep, dg_got, small_rows.reshape(-1, 128), grad, conv_own.shape[0]
                )
        else:
            grad = weight_grad(layer, cells[layer], dz, grad)
        others = [affine_scale[layer - 1 : layer], pre[layer - 1]] if layer else [spread]
        dz, *halves = data_grad(strip, layer, place, dz, above, below, conv_full, others, staged)
    input_grad = dz
    if staged:
        conv_grad, head_grad, small_grad = staged_scatter(
            every, [grad[4 * n : 4 * n + 4] for n in range(4)], core, conv_own.shape[0]
        )
        small_grad = small_grad[:, : own_small // 2].reshape(1, -1)
    else:
        conv_grad = lax.psum_scatter(grad, every, scatter_dimension=0, tiled=True).astype(f32)
        head_grad = lax.psum_scatter(head_grad, every, scatter_dimension=0, tiled=True).astype(f32)
        small_grad = lax.psum_scatter(small_grad, every, scatter_dimension=0, tiled=True)
    return (
        maps.reshape(images, rows, cols, total),
        pooled,
        input_grad.reshape(images, rows, cols, depth),
        conv_grad,
        head_grad,
        small_grad[0, :own_gain],
        small_grad[0, own_gain:],
    )


def solution(mesh):
    return jax.shard_map(
        shards,
        mesh=mesh,
        in_specs=(
            P("dp", "space", None, None),
            P(("dp", "space"), None),
            P(("dp", "space"), None),
            P(("dp", "space")),
            P(("dp", "space")),
            P(),
            P(),
            P("dp", "space", None, None),
            P("dp", None),
            P("dp"),
            P("dp", None),
        ),
        out_specs=(
            P("dp", "space", None, None),
            P("dp", None),
            P("dp", "space", None, None),
            P(("dp", "space"), None),
            P(("dp", "space"), None),
            P(("dp", "space")),
            P(("dp", "space")),
        ),
        check_vma=False,
    )
```

```python
import functools

import jax
import jax.numpy as jnp
import numpy as np
from jax import lax
from jax.experimental import pallas as pl
from jax.experimental.pallas import tpu as pltpu
from jax.sharding import PartitionSpec as P

HEAD_CH = 256
TASK_HEADS = 7
SCALES = 3
LAYERS = 3
PAD = 8
VMEM_LIMIT = 56 << 20

epsilon = 1e-06
f32 = jnp.float32
bf16 = jnp.bfloat16
NN = (((1,), (0,)), ((), ()))
NT = (((1,), (1,)), ((), ()))
TN = (((0,), (0,)), ((), ()))


def mm(left, right, dims=NN):
    return lax.dot_general(left, right, dims, preferred_element_type=f32)


def split_mm(left, right):
    high = right.astype(bf16)
    low = (right - high.astype(f32)).astype(bf16)
    return mm(left, high) + mm(left, low)


class Strip:
    def __init__(self, rows, cols):
        self.rows = [rows >> s for s in range(SCALES)]
        self.cols = [cols >> s for s in range(SCALES)]

    def sizes(self, halo):
        return [(r + 2 * halo) * c for r, c in zip(self.rows, self.cols)]

    def starts(self, halo):
        sizes = self.sizes(halo)
        return [sum(sizes[:s]) for s in range(SCALES)]

    def total(self, halo):
        return sum(self.sizes(halo))

    def own(self, halo):
        return [st + halo * c for st, c in zip(self.starts(halo), self.cols)]


def spread_matrix(strip):
    rows, cols = strip.rows[0], strip.cols[0]
    parts = []
    for s in range(1, SCALES):
        mat = np.zeros((rows * cols, strip.rows[s] * strip.cols[s]), np.float32)
        for r in range(rows):
            for c in range(cols):
                mat[r * cols + c, (r >> s) * strip.cols[s] + (c >> s)] = 1.0
        parts.append(mat)
    return np.concatenate(parts, axis=1)


def column_of(strip, scale, count):
    return lax.broadcasted_iota(jnp.int32, (count, 1), 0) % strip.cols[scale]


def shifted_copies(strip, halo, act, wide, depth):
    for s in range(SCALES):
        start, count, cols = strip.starts(halo)[s], strip.sizes(halo)[s], strip.cols[s]
        column = column_of(strip, s, count)
        for k in range(3):
            rows = act[PAD + start + k - 1 : PAD + start + k - 1 + count, :]
            if k == 0:
                rows = jnp.where(column == 0, 0.0, rows)
            if k == 2:
                rows = jnp.where(column == cols - 1, 0.0, rows)
            wide[start : start + count, k * depth : (k + 1) * depth] = rows.astype(bf16)


def patches(strip, halo, wide, cells, depth, flip=False, base=0):
    for s in range(SCALES):
        cols = strip.cols[s]
        count = strip.sizes(halo)[s]
        source, target = strip.starts(halo + 1)[s], strip.starts(halo)[s]
        for ky in range(3):
            first = source + (2 - ky if flip else ky) * cols
            for kx in range(3):
                col = (2 - kx if flip else kx) * depth
                tap = 3 * ky + kx
                cells[base + target : base + target + count, tap * depth : (tap + 1) * depth] = wide[
                    first : first + count, col : col + depth
                ]


FLIPS = ((1, 2), (2, 1))
TURNS = (0, 1, 3, 2)
GROUPS = (((0, 1, 2, 3),),) * 3 + (((0, 1, 2), (3,)),)
ARRIVALS = sum(4 + len(groups) for groups in GROUPS)


def across(place, part, core):
    rank = place[0]
    for bit in range(2):
        if part >> bit & 1:
            rank = rank ^ jnp.where(core == 0, FLIPS[0][bit], FLIPS[1][bit])
    return rank


def load_staged(conv_rows, place, refs, weights, head_w, w_sem, h_sem):
    depth = weights.shape[1]
    layer_rows = weights.shape[0] // LAYERS
    last = [-(-layer_rows * (n + 1) // conv_rows) for n in range(LAYERS)]
    pieces = head_w.shape[0]
    blocks = []
    at = 0
    for turn, groups in zip(TURNS, GROUPS):
        z = (place[3] + 4 - turn) % 4
        for own, parts in [(True, (n,)) for n in range(4)] + [(False, group) for group in groups]:
            core = place[4] if own else 1 - place[4]
            for n, part in enumerate(parts):
                ref = refs[at] if own or len(parts) == 1 else refs[at].at[n]
                blocks.append((ref, (z * 2 + core) * 4 + across(place, part, core)))
            at += 1
    for layer in range(LAYERS):
        for ref, k in blocks:
            copy = pltpu.make_async_copy(
                ref.at[pl.ds(0, conv_rows), :],
                weights.at[pl.ds(pl.multiple_of(k * conv_rows, 16), conv_rows), :],
                w_sem.at[layer],
            )
            inside = k < last[layer]
            if layer:
                inside = inside & (k >= last[layer - 1])
            pl.when(inside)(copy.start)
    head_rows = head_w.shape[1] // len(blocks)
    for ref, k in blocks:
        for piece in range(pieces):
            pltpu.make_async_copy(
                ref.at[pl.ds(conv_rows + piece * head_rows, head_rows), :],
                head_w.at[piece, pl.ds(pl.multiple_of(k * head_rows, 16), head_rows), :],
                h_sem.at[0],
            ).start()
    waits = []
    before = 0
    for layer in range(LAYERS):
        rows = weights.at[pl.ds(before * conv_rows, (last[layer] - before) * conv_rows), :]
        waits.append(pltpu.make_async_copy(rows, rows, w_sem.at[layer]))
        before = last[layer]
    return waits, pltpu.make_async_copy(head_w, head_w, h_sem.at[0])


def pack_kernel(strip, conv_ref, head_ref, gain_ref, join_ref, x_ref, gather_ref, own_ref, wide_ref, top_ref, bottom_ref):
    depth = conv_ref.shape[1]
    at = conv_ref.shape[0]
    rows, head_cols = head_ref.shape
    for ref in (own_ref, wide_ref):
        ref[:at, :] = conv_ref[...].astype(bf16)
    for first in range(0, head_cols, depth):
        width = min(depth, head_cols - first)
        piece = head_ref[:, first : first + width]
        if width < depth:
            small = jnp.concatenate([gain_ref[...], join_ref[...]], axis=1)
            small = jnp.concatenate([small, jnp.zeros((1, depth - width - small.shape[1]), f32)], axis=1)
            row = lax.broadcasted_iota(jnp.int32, (rows, depth - width), 0)
            small = jnp.where(row == 0, jnp.broadcast_to(small, (rows, depth - width)), 0.0)
            piece = jnp.concatenate([piece, small], axis=1)
        for ref in (own_ref, wide_ref):
            ref[at : at + rows, :] = piece.astype(bf16)
        at += rows
    x = x_ref[...]
    sums = mm(gather_ref[...], x)
    for s in range(1, SCALES):
        first = strip.starts(0)[s] - strip.starts(0)[1]
        size = strip.sizes(0)[s]
        wide_ref[at : at + size, :] = (sums[first : first + size] * (0.25**s)).astype(bf16)
        at += size
    edge = 3 * strip.cols[0]
    top_ref[...] = x_ref[:edge, :]
    bottom_ref[...] = x_ref[x.shape[0] - edge :, :]


def forward_kernel(strip, depth, staged, *refs):
    taps = 9 * depth
    place, x_ref, scale_ref, shift_ref = refs[:4]
    refs = refs[4:]
    if staged is None:
        w_hbm = refs[0]
        refs = refs[1:]
    else:
        conv_rows, head_cols = staged
        above_ref, below_ref, place_ref, owner_ref = refs[:4]
        blocks, refs = refs[4 : 4 + ARRIVALS], refs[4 + ARRIVALS :]
    p_refs, acts_ref, a3_ref, refs = refs[:3], refs[3], refs[4], refs[5:]
    if staged is not None:
        full_hbm, head_ref, small_ref = refs[:3]
        refs = refs[3:]
    weights, act, wide, cells, w_sem = refs[:5]
    if staged is None:
        loads = []
        for layer in range(LAYERS):
            copy = pltpu.make_async_copy(
                w_hbm.at[pl.ds(layer * taps, taps), :], weights.at[pl.ds(layer * taps, taps), :], w_sem.at[layer]
            )
            copy.start()
            loads.append(copy)
    else:
        strips, expand, h_sem, f_sem, x_sem = refs[5:]
        strips[...] = jnp.zeros(strips.shape, bf16)
        coarse = strips.shape[1]
        fetches = []
        for part in range(4):
            copy = pltpu.make_async_copy(
                blocks[part].at[pl.ds(blocks[part].shape[0] - coarse, coarse), :],
                strips.at[3 + across(place, part, place[4])],
                x_sem.at[part],
            )
            copy.start()
            fetches.append(copy)
        loads, head_loads = load_staged(
            conv_rows, place, blocks, weights, head_ref, w_sem, h_sem
        )
        expand_load = pltpu.make_async_copy(place_ref, expand, h_sem.at[1])
        expand_load.start()
    here, ranks = place[0], place[1]
    if staged is None:
        act[PAD : PAD + strip.total(3), :] = x_ref[...].astype(f32)
    else:
        at = PAD
        for ref in (above_ref, x_ref, below_ref):
            act[at : at + ref.shape[0], :] = ref[...].astype(f32)
            at += ref.shape[0]
        for copy in fetches:
            copy.wait()
        for s in range(1, SCALES):
            rows, cols = strip.rows[s], strip.cols[s]
            first = strip.starts(0)[s] - strip.starts(0)[1]
            for row in range(-3, rows + 3):
                source = strips[here + 3 + row // rows, first + row % rows * cols : first + (row % rows + 1) * cols, :]
                act[at : at + cols, :] = source.astype(f32)
                at += cols
    for s in range(SCALES):
        start, size = strip.starts(1)[s], strip.sizes(1)[s]
        first = PAD + strip.starts(3)[s] + 2 * strip.cols[s]
        acts_ref[start : start + size, :] = act[first : first + size, :].astype(bf16)
    fulls = []
    for layer in range(LAYERS):
        halo = LAYERS - 1 - layer
        count = strip.total(halo)
        shifted_copies(strip, halo + 1, act, wide, depth)
        patches(strip, halo, wide, cells, depth)
        own = strip.own(halo)
        flat = strip.starts(0)
        loads[layer].wait()
        if staged is not None:
            rows = pl.ds(layer * taps, taps)
            copy = pltpu.make_async_copy(weights.at[rows, :], full_hbm.at[rows, :], f_sem.at[layer])
            copy.start()
            fulls.append(copy)
        for half in range(depth // 256):
            lanes = slice(half * 256, (half + 1) * 256)
            z = mm(cells[:count, :], weights[layer * taps : (layer + 1) * taps, lanes])
            p = z * scale_ref[layer : layer + 1, lanes] + shift_ref[layer : layer + 1, lanes]
            a = (p / (1.0 + jnp.exp(-p))).astype(bf16)
            for s in range(SCALES):
                size = strip.sizes(0)[s]
                p_refs[layer][flat[s] : flat[s] + size, lanes] = p[own[s] : own[s] + size]
            if layer == LAYERS - 1:
                a3_ref[:, lanes] = a
                acts_ref[LAYERS * strip.total(1) :, lanes] = a
            else:
                for s in range(SCALES):
                    start, size = strip.starts(halo)[s], strip.sizes(halo)[s]
                    row = lax.broadcasted_iota(jnp.int32, (size, 1), 0) // strip.cols[s]
                    row = row + here * strip.rows[s] - halo
                    inside = (row >= 0) & (row < ranks * strip.rows[s])
                    kept = jnp.where(inside, a[start : start + size].astype(f32), 0.0)
                    act[PAD + start : PAD + start + size, lanes] = kept
                    edge = (halo - 1) * strip.cols[s]
                    first, size = (layer + 1) * strip.total(1) + strip.starts(1)[s], strip.sizes(1)[s]
                    acts_ref[first : first + size, lanes] = kept[edge : edge + size].astype(bf16)
    for copy in fulls:
        copy.wait()
    if staged is not None:
        head_loads.wait()
        expand_load.wait()
        owners, spare = owner_ref.shape[0], expand.shape[0]
        pieces, depth_rows = head_ref.shape[:2]
        row = lax.broadcasted_iota(jnp.int32, (owners, depth_rows), 0)
        col = lax.broadcasted_iota(jnp.int32, (owners, depth_rows), 1)
        pick = jnp.where(col == row * (depth_rows // owners), 1.0, 0.0).astype(bf16)
        picked = mm(pick, head_ref[pieces - 1, :, depth - spare :]).astype(bf16)
        for n in range(1 + SCALES):
            cols = slice(n * head_cols, (n + 1) * head_cols)
            spread = mm(picked, expand[:, cols]) * owner_ref[:, cols].astype(f32)
            small_ref[n : n + 1, :] = jnp.sum(spread, axis=0, keepdims=True)


def slope(p):
    sigma = 1.0 / (1.0 + jnp.exp(-p))
    return sigma * (1.0 + p * (1.0 - sigma))


def head_kernel(
    strip, split, place, a3_ref, w_ref, small_ref, cot_ref, pool_cot_ref, where_ref, spread_ref, gather_ref,
    scale_ref, p2_ref, maps_ref, pool_ref, sums_ref, *refs,
):
    if split:
        *grads, keep_ref, give_ref, da3, dg_all = refs
    else:
        *grads, w_grad_ref, da3 = refs
    head = pl.program_id(0)
    fine = strip.sizes(0)[0]
    starts, sizes = strip.starts(0), strip.sizes(0)
    a3 = a3_ref[...]
    weight = w_ref[0] if split else w_ref[...]
    g = mm(a3, weight)
    inverse = lax.rsqrt(jnp.sum(g * g, axis=-1, keepdims=True) + epsilon)
    unit = g * inverse
    gain = small_ref[0:1, :]
    normed = unit * gain
    join = small_ref[1:, :]
    coarse = jnp.concatenate(
        [normed[starts[s] : starts[s] + sizes[s]] * join[s : s + 1] for s in range(1, SCALES)], axis=0
    )
    joined = normed[:fine] * join[0:1] + split_mm(spread_ref[...], coarse)
    maps_ref[...] = joined.astype(bf16)
    slots = where_ref.shape[1]
    first = place[0] * fine
    pixel = lax.broadcasted_iota(jnp.int32, (fine, slots), 0) + first
    slot = lax.broadcasted_iota(jnp.int32, (fine, slots), 1)
    hits = jnp.where((where_ref[...] == pixel) & (slot < place[2]) & (head == 0), 1.0, 0.0)
    hits = jnp.sum(hits, axis=-1, keepdims=True)

    @pl.when(head == 0)
    def _():
        pool_ref[...] = jnp.sum(joined * hits, axis=0, keepdims=True)

    share = pool_cot_ref[...] / place[2].astype(f32)
    fused = cot_ref[...].astype(f32) + hits * share
    down_coarse = split_mm(gather_ref[...], fused)
    down = jnp.concatenate([fused, down_coarse], axis=0)
    product = down * normed
    scaled = []
    for s in range(SCALES):
        part = slice(starts[s], starts[s] + sizes[s])
        sums_ref[s + 1 : s + 2, :] = jnp.sum(product[part], axis=0, keepdims=True)
        scaled.append(down[part] * join[s : s + 1])
    dn = jnp.concatenate(scaled, axis=0)
    sums_ref[0:1, :] = jnp.sum(dn * unit, axis=0, keepdims=True)
    du = dn * gain
    dg = (inverse * (du - unit * jnp.sum(du * unit, axis=-1, keepdims=True))).astype(bf16)
    if split:
        dg_all[head] = dg
    else:
        w_grad_ref[...] = mm(a3, dg, TN).astype(w_grad_ref.dtype)
    part = mm(dg, weight, NT)

    @pl.when(head == 0)
    def _():
        da3[...] = part

    @pl.when(head > 0)
    def _():
        da3[...] += part

    @pl.when(head == pl.num_programs(0) - 1)
    def _():
        layer = LAYERS - 1
        dz = da3[...] * scale_ref[layer : layer + 1, :] * slope(p2_ref[...])
        emit_grad(strip, place, dz.astype(bf16), *grads)
        if split:
            heads, _, width = dg_all.shape
            first = place[4] == 0
            half = heads * width // 2
            for start in range(0, half, width // 2):
                left = dg_all[start // width, :, start % width : start % width + width // 2]
                at = half + start
                right = dg_all[at // width, :, at % width : at % width + width // 2]
                keep_ref[:, start : start + width // 2] = jnp.where(first, left, right)
                give_ref[:, start : start + width // 2] = jnp.where(first, right, left)


def emit_grad(strip, place, dz, dz_ref, first_ref, last_ref, keep_ref=None, give_ref=None):
    dz_ref[...] = dz
    edge = 0
    for start, size, cols in zip(strip.starts(0), strip.sizes(0), strip.cols):
        first_ref[edge : edge + cols, :] = dz[start : start + cols]
        last_ref[edge : edge + cols, :] = dz[start + size - cols : start + size]
        edge += cols
    if keep_ref is not None:
        middle = dz.shape[1] // 2
        left, right = dz[:, :middle], dz[:, middle:]
        first = place[4] == 0
        keep_ref[...] = jnp.where(first, left, right)
        give_ref[...] = jnp.where(first, right, left)


def store_blocks(place, pieces, block_refs, sem):
    for turn in range(4):
        for part in range(4):
            out = block_refs[4 * turn + part]
            z = (place[3] + turn) % 4
            rank = across(place, part, place[4])
            for core in range(2):
                k = (z * 2 + core) * 4 + rank
                base = core * (out.shape[0] // 2)
                for condition, source, row in pieces(k):
                    copy = pltpu.make_async_copy(source, out.at[pl.ds(base + row, source.shape[0]), :], sem)
                    if condition is None:
                        copy.start()
                    else:
                        pl.when(condition)(copy.start)


def weight_grad_kernel(strip, depth, layer, images, conv_rows, place, *refs):
    acts, grads = refs[:images], refs[images : 2 * images]
    *outs, token, raw, act, wide, cells, dz, result, sem, in_sem = refs[2 * images :]
    own, count = strip.total(0), strip.total(1)
    loads = []
    for n in range(images):
        copy = pltpu.make_async_copy(acts[n].at[pl.ds(layer * count, count), :], raw.at[n], in_sem.at[n])
        copy.start()
        loads.append(copy)
    for n in range(images):
        loads[n].wait()
        act[PAD : PAD + count, :] = raw[n].astype(f32)
        shifted_copies(strip, 1, act, wide, depth)
        patches(strip, 0, wide, cells, depth, base=n * own)
        dz[n * own : (n + 1) * own, :] = grads[n][...]
    for tap in range(9):
        lanes = slice(tap * depth, (tap + 1) * depth)
        result[lanes, :] = mm(cells[:, lanes], dz[...], TN).astype(bf16)
    rows = 9 * depth
    first_row, stop_row = layer * rows, (layer + 1) * rows
    token[...] = jnp.zeros(token.shape, f32)
    if conv_rows is None:
        copy = pltpu.make_async_copy(result, outs[-1].at[pl.ds(first_row, rows), :], sem)
        copy.start()
        copy.wait()
        return

    def pieces(k):
        out = []
        inside = (k * conv_rows >= first_row) & ((k + 1) * conv_rows <= stop_row)
        start = jnp.where(inside, k * conv_rows - first_row, 0)
        out.append((inside, result.at[pl.ds(pl.multiple_of(start, 16), conv_rows), :], 0))
        if first_row % conv_rows:
            size = conv_rows - first_row % conv_rows
            out.append((k == first_row // conv_rows, result.at[pl.ds(0, size), :], conv_rows - size))
        if stop_row % conv_rows:
            size = stop_row % conv_rows
            out.append((k == stop_row // conv_rows, result.at[pl.ds(rows - size, size), :], 0))
        return out

    store_blocks(place, pieces, outs[-16:], sem)
    pltpu.make_async_copy(result, result, sem).wait()


def chip_head_grad_kernel(conv_rows, place, a3_ref, other_ref, keep_ref, got_ref, *refs):
    refs = refs[-(16 + 4) :]
    outs, (a3, dg, result, out_sem) = refs[:16], refs[16:]
    own = keep_ref.shape[0]
    for n, ref in enumerate((a3_ref, other_ref)):
        pltpu.make_async_copy(ref.at[pl.ds(ref.shape[0] - own, own), :], a3.at[pl.ds(n * own, own), :], out_sem).start()
    pltpu.make_async_copy(a3, a3, out_sem).wait()
    dg[:own, :] = keep_ref[...]
    dg[own:, :] = got_ref[...]
    width = result.shape[2]
    cols = dg.shape[1]
    for piece in range(result.shape[0]):
        stop = min(cols, (piece + 1) * width)
        lanes = slice(piece * width, stop)
        result[piece, :, : stop - piece * width] = mm(a3[...], dg[:, lanes], TN).astype(bf16)
    if cols % width:
        result[result.shape[0] - 1, :, cols % width :] = jnp.zeros((result.shape[1], width - cols % width), bf16)
    rows = (outs[0].shape[0] // 2 - conv_rows) // result.shape[0]

    def pieces(k):
        return [
            (None, result.at[piece, pl.ds(pl.multiple_of(k * rows, 16), rows), :], conv_rows + piece * rows)
            for piece in range(result.shape[0])
        ]

    store_blocks(place, pieces, outs, out_sem)
    pltpu.make_async_copy(result, result, out_sem).wait()


def data_grad_kernel(
    strip, depth, layer, place, dz_ref, above_ref, below_ref, w_ref, _, *refs
):
    refs, (act, wide, cells, total) = refs[:-4], refs[-4:]
    last = layer == 0
    if last:
        spread_ref, out_ref = refs
    else:
        scale_ref, p_ref, *outs = refs
    step = pl.program_id(0)

    @pl.when(step == 0)
    def _():
        edge = 0
        for s in range(SCALES):
            start, size, cols = strip.starts(1)[s], strip.sizes(0)[s], strip.cols[s]
            flat = strip.starts(0)[s]
            act[PAD + start : PAD + start + cols, :] = above_ref[edge : edge + cols, :].astype(f32)
            act[PAD + start + cols : PAD + start + cols + size, :] = dz_ref[flat : flat + size, :].astype(f32)
            act[PAD + start + cols + size : PAD + start + 2 * cols + size, :] = below_ref[
                edge : edge + cols, :
            ].astype(f32)
            edge += cols
        shifted_copies(strip, 1, act, wide, depth)
        patches(strip, 0, wide, cells, depth, flip=True)
        total[...] = jnp.zeros(total.shape, f32)

    for ky in range(3):
        @pl.when(step == ky)
        def _():
            value = total[...]
            for kx in range(3):
                tap = 3 * ky + kx
                value += mm(cells[:, tap * depth : (tap + 1) * depth], w_ref[kx * depth : (kx + 1) * depth, :], NT)
            total[...] = value

    @pl.when(step == 2)
    def _():
        if last:
            fine = strip.sizes(0)[0]
            coarse = jnp.concatenate(
                [
                    total[st : st + size, :] * (0.25**s)
                    for s, (st, size) in enumerate(zip(strip.starts(0), strip.sizes(0)))
                    if s
                ],
                axis=0,
            )
            out_ref[...] = total[:fine, :] + split_mm(spread_ref[...], coarse)
        else:
            dz = total[...] * scale_ref[layer - 1 : layer, :] * slope(p_ref[...])
            emit_grad(strip, place, dz.astype(bf16), *outs)


def vmem(shape=None, index=None):
    if shape is None:
        return pl.BlockSpec(memory_space=pltpu.VMEM)
    return pl.BlockSpec(shape, index)


SMEM = pl.BlockSpec(memory_space=pltpu.SMEM)
ANY = pl.BlockSpec(memory_space=pl.ANY)


def params():
    return pltpu.CompilerParams(vmem_limit_bytes=VMEM_LIMIT)


def small_layout(owners, cols, spare):
    gains = cols // owners
    expand = np.zeros((spare, (1 + SCALES) * cols), np.float32)
    owner = np.zeros((owners, (1 + SCALES) * cols), np.float32)
    for n in range((1 + SCALES) * cols):
        size = gains if n < cols else SCALES * gains
        at = n if n < cols else n - cols
        expand[at % size + (0 if n < cols else gains), n] = 1.0
        owner[at // size, n] = 1.0
    return jnp.asarray(expand, bf16), jnp.asarray(owner, bf16)


def pack(strip, conv, head_w, gain, join, x, gather):
    depth = conv.shape[1]
    rows = conv.shape[0] + head_w.shape[0] * -(-head_w.shape[1] // depth)
    edge = 3 * strip.cols[0]
    return pl.pallas_call(
        functools.partial(pack_kernel, strip),
        name="pack",
        out_shape=[jax.ShapeDtypeStruct((n, depth), bf16) for n in (rows, rows + gather.shape[0], edge, edge)],
        in_specs=[vmem()] * 6,
        out_specs=[vmem()] * 4,
        compiler_params=params(),
    )(conv, head_w, gain[None], join[None], x, gather)


def forward(strip, place, x, conv, scale, shift, head_cols):
    depth = x.shape[1]
    own = strip.total(0)
    wide_rows = strip.total(3)
    rows = LAYERS * 9 * depth
    staged, inputs = None, [conv]
    outs = (
        [jax.ShapeDtypeStruct((own, depth), f32)] * 3
        + [jax.ShapeDtypeStruct((n, depth), bf16) for n in (LAYERS * strip.total(1) + own, own)]
    )
    out_specs = [vmem()] * 5
    sems = [pltpu.SemaphoreType.DMA((LAYERS,))]
    edge_specs = []
    if isinstance(conv, tuple):
        conv_rows, edges, inputs = conv
        staged = (conv_rows, head_cols)
        spare = -head_cols % depth
        owners = rows // conv_rows
        expand, owner = small_layout(owners, head_cols, spare)
        edge_specs = [vmem()] * 2 + [ANY, vmem()]
        pieces = -(-head_cols // depth)
        outs += [
            jax.ShapeDtypeStruct((rows, depth), bf16),
            jax.ShapeDtypeStruct((pieces, depth, depth), bf16),
            jax.ShapeDtypeStruct((1 + SCALES, head_cols), f32),
        ]
        out_specs += [ANY, vmem(), vmem()]
        sems += [
            pltpu.VMEM((6 + owners // 8, strip.total(0) - strip.sizes(0)[0], depth), bf16),
            pltpu.VMEM(expand.shape, bf16),
            pltpu.SemaphoreType.DMA((2,)),
            pltpu.SemaphoreType.DMA((LAYERS,)),
            pltpu.SemaphoreType.DMA((4,)),
        ]
        inputs = edges + [expand, owner] + inputs
    return pl.pallas_call(
        functools.partial(forward_kernel, strip, depth, staged),
        name="forward",
        out_shape=outs,
        in_specs=[SMEM, vmem(), vmem(), vmem()] + edge_specs + [ANY] * (len(inputs) - len(edge_specs)),
        out_specs=out_specs,
        scratch_shapes=[
            pltpu.VMEM((rows, depth), bf16),
            pltpu.VMEM((wide_rows + 2 * PAD, depth), f32),
            pltpu.VMEM((wide_rows, 3 * depth), bf16),
            pltpu.VMEM((strip.total(2), 9 * depth), bf16),
        ]
        + sems,
        compiler_params=params(),
    )(place, x, scale, shift, *inputs)


def head(strip, place, a3, weight, small, cot, pool_cot, where, spread, scale, p2, split):
    own, depth = a3.shape
    total = small.shape[1]
    fine = strip.sizes(0)[0]
    ch = HEAD_CH
    gather = spread.T
    edge = sum(strip.cols)

    def whole(array):
        return pl.BlockSpec(array.shape, lambda t: (0,) * array.ndim)

    def part(rows):
        return pl.BlockSpec((rows, ch), lambda t: (0, t))

    outs = [
        (jax.ShapeDtypeStruct((fine, total), bf16), part(fine)),
        (jax.ShapeDtypeStruct((1, ch), f32), None),
        (jax.ShapeDtypeStruct((1 + SCALES, total), f32), part(1 + SCALES)),
        (jax.ShapeDtypeStruct((own, depth), bf16), None),
        (jax.ShapeDtypeStruct((edge, depth), bf16), None),
        (jax.ShapeDtypeStruct((edge, depth), bf16), None),
    ]
    weight_spec = part(depth)
    if split:
        per = depth // ch
        weight_spec = pl.BlockSpec((1, depth, ch), lambda t: (t // per, 0, t % per))
        outs += [(jax.ShapeDtypeStruct((own, depth // 2), bf16), None)] * 2
        outs += [(jax.ShapeDtypeStruct((own, total // 2), bf16), None)] * 2
    else:
        outs += [(jax.ShapeDtypeStruct((depth, total), bf16), part(depth))]
    return pl.pallas_call(
        functools.partial(head_kernel, strip, split),
        name="heads",
        grid=(total // ch,),
        out_shape=[shape for shape, _ in outs],
        in_specs=[
            SMEM, whole(a3), weight_spec, part(1 + SCALES), part(fine), whole(pool_cot), whole(where),
            whole(spread), whole(gather), whole(scale), whole(p2),
        ],
        out_specs=[spec or whole(shape) for shape, spec in outs],
        scratch_shapes=[pltpu.VMEM((own, depth), f32)] + [pltpu.VMEM((total // ch, own, ch), bf16)] * split,
        compiler_params=params(),
    )(place, a3, weight, small, cot, pool_cot, where, spread, gather, scale, p2)


def weight_grad(strip, layer, place, acts, grads, into, rows, conv_rows):
    own, half = grads[0].shape
    depth = acts[0].shape[1]
    images = len(acts)
    count_here = strip.total(1)
    into = into or []
    count = 1 if conv_rows is None else 16
    return pl.pallas_call(
        functools.partial(weight_grad_kernel, strip, depth, layer, images, conv_rows),
        name="weight_grad",
        out_shape=[jax.ShapeDtypeStruct((rows, half), bf16)] * count + [jax.ShapeDtypeStruct((8, 128), f32)],
        in_specs=[SMEM] + [ANY] * images + [vmem()] * images + [ANY] * len(into),
        out_specs=[ANY] * count + [vmem()],
        scratch_shapes=[
            pltpu.VMEM((images, count_here, depth), bf16),
            pltpu.VMEM((count_here + 2 * PAD, depth), f32),
            pltpu.VMEM((count_here, 3 * depth), bf16),
            pltpu.VMEM((images * own, 9 * depth), bf16),
            pltpu.VMEM((images * own, half), bf16),
            pltpu.VMEM((9 * depth, half), bf16),
            pltpu.SemaphoreType.DMA,
            pltpu.SemaphoreType.DMA((images,)),
        ],
        input_output_aliases={1 + 2 * images + n: n for n in range(len(into))},
        compiler_params=params(),
    )(place, *acts, *grads, *into)


def chip_head_grad(place, a3, other, keep, got, blocks, conv_rows):
    own, depth = keep.shape[0], a3.shape[1]
    half = blocks[0].shape[1]
    pieces = -(-keep.shape[1] // half)
    return pl.pallas_call(
        functools.partial(chip_head_grad_kernel, conv_rows),
        name="chip_head_grad",
        out_shape=[jax.ShapeDtypeStruct(b.shape, bf16) for b in blocks],
        in_specs=[SMEM, ANY, ANY, vmem(), vmem()] + [ANY] * 16,
        out_specs=[ANY] * 16,
        scratch_shapes=[
            pltpu.VMEM((2 * own, depth), bf16),
            pltpu.VMEM((2 * own, keep.shape[1]), bf16),
            pltpu.VMEM((pieces, depth, half), bf16),
            pltpu.SemaphoreType.DMA,
        ],
        input_output_aliases={5 + n: n for n in range(16)},
        compiler_params=params(),
    )(place, a3, other, keep, got, *blocks)


def data_grad(strip, layer, place, dz, above, below, conv, token, others, split):
    own, depth = dz.shape
    last = layer == 0
    edge = sum(strip.cols)

    def whole(array):
        return pl.BlockSpec(array.shape, lambda t: (0, 0))

    if last:
        outs = [jax.ShapeDtypeStruct((strip.sizes(0)[0], depth), f32)]
    else:
        outs = [jax.ShapeDtypeStruct((n, depth), bf16) for n in (own, edge, edge)]
        outs += [jax.ShapeDtypeStruct((own, depth // 2), bf16)] * (2 * split)
    return pl.pallas_call(
        functools.partial(data_grad_kernel, strip, depth, layer),
        name="data_grad",
        grid=(3,),
        out_shape=outs,
        in_specs=[
            SMEM, whole(dz), whole(above), whole(below),
            pl.BlockSpec((3 * depth, depth), lambda t: (layer * 3 + t, 0)), ANY,
        ]
        + [whole(o) for o in others],
        out_specs=[whole(o) for o in outs],
        scratch_shapes=[
            pltpu.VMEM((strip.total(1) + 2 * PAD, depth), f32),
            pltpu.VMEM((strip.total(1), 3 * depth), bf16),
            pltpu.VMEM((own, 9 * depth), bf16),
            pltpu.VMEM((own, depth), f32),
        ],
        compiler_params=params(),
    )(place, dz, above, below, conv, token, *others)


def from_neighbour(cells, distance, axis):
    count = lax.axis_size(axis)
    pairs = [(i, i + distance) for i in range(count) if 0 <= i + distance < count]
    return lax.ppermute(cells, axis, pairs)


def with_rows(strip, levels, axis):
    above = [[] for _ in levels]
    below = [[] for _ in levels]
    left = [3] * len(levels)
    distance = 1
    while max(left) > 0:
        take = [min(n, r) for n, r in zip(left, strip.rows)]
        tails = [v[v.shape[0] - t * c :] for v, t, c in zip(levels, take, strip.cols) if t]
        heads = [v[: t * c] for v, t, c in zip(levels, take, strip.cols) if t]
        got_tail = from_neighbour(jnp.concatenate(tails, axis=0), distance, axis)
        got_head = from_neighbour(jnp.concatenate(heads, axis=0), -distance, axis)
        at = 0
        for s, (t, c) in enumerate(zip(take, strip.cols)):
            if t:
                above[s].insert(0, got_tail[at : at + t * c])
                below[s].append(got_head[at : at + t * c])
                at += t * c
        left = [n - t for n, t in zip(left, take)]
        distance += 1
    return jnp.concatenate([v for s, own in enumerate(levels) for v in above[s] + [own] + below[s]], axis=0)


def after(value, *others):
    return lax.optimization_barrier((value,) + others)[0]


def turn_pairs(step):
    return [((z * 2 + c) * 4 + s, (((z + step) % 4) * 2 + c) * 4 + s) for z in range(4) for c in range(2) for s in range(4)]


def flip_pairs(which):
    return [((z * 2 + c) * 4 + s, (z * 2 + c) * 4 + (s ^ FLIPS[c][which])) for z in range(4) for c in range(2) for s in range(4)]


def core_pairs():
    return [((z * 2 + c) * 4 + s, (z * 2 + 1 - c) * 4 + s) for z in range(4) for c in range(2) for s in range(4)]


def staged_gather(every, own, wide, tops, bottoms):
    def swap(n, parts):
        four = [lines[n], ones[n], twos[n], boths[n]] if len(boths) > n else [lines[n], ones[n], twos[n]]
        chosen = [four[part] for part in parts]
        return lax.ppermute(jnp.stack(chosen) if len(parts) > 1 else chosen[0], every, core_pairs())

    lines, ones, twos, boths, swaps = [wide], [], [], [], [[] for _ in TURNS]
    ends = len(TURNS) - 1
    for turn in range(len(TURNS) + 1):
        fresh = {}
        if turn < len(TURNS):
            fresh["one"] = lax.ppermute(lines[turn], every, flip_pairs(0))
            fresh["two"] = lax.ppermute(lines[turn], every, flip_pairs(1))
        if turn < ends:
            step = TURNS[turn + 1]
            if step == 2:
                fresh["line"] = lax.ppermute(after(lines[1], *ones), every, turn_pairs(1))
            else:
                fresh["line"] = lax.ppermute(after(own, *ones) if ones else own, every, turn_pairs(step))
        if turn:
            fresh["both"] = lax.ppermute(ones[turn - 1], every, flip_pairs(1))
        if turn >= 2:
            fresh["swap"] = swap(turn - 2, GROUPS[turn - 2][0])
        if turn == len(TURNS):
            fresh["early"] = swap(ends, GROUPS[ends][0])
        if not turn:
            fresh["above"] = from_neighbour(bottoms, 1, "space")
            fresh["below"] = from_neighbour(tops, -1, "space")
        fresh = dict(zip(fresh, lax.optimization_barrier(tuple(fresh.values()))))
        if not turn:
            edges = [fresh["above"], fresh["below"]]
        if turn < len(TURNS):
            ones.append(fresh["one"])
            twos.append(fresh["two"])
        if turn < ends:
            lines.append(fresh["line"])
        if turn:
            boths.append(fresh["both"])
        if turn >= 2:
            swaps[turn - 2].append(fresh["swap"])
    swaps[ends] += [fresh["early"], swap(ends, GROUPS[ends][1])]
    return edges, [v for n in range(len(TURNS)) for v in [lines[n], ones[n], twos[n], boths[n]] + swaps[n]]


def total_of(*terms):
    return sum((t.astype(f32) for t in terms[1:]), terms[0].astype(f32))


def staged_scatter(every, blocks, core, conv_rows, extras, input_grad):
    order = TURNS[::-1]
    boths, ones, twos, parts = {}, {}, {}, {}
    along = {}
    for n in range(len(order) + 1):
        fresh = {}
        if n < len(order):
            fresh["both"] = lax.ppermute(blocks[order[n]][3], every, flip_pairs(1))
        if n:
            turn = order[n - 1]
            fresh["two"] = lax.ppermute(blocks[turn][2], every, flip_pairs(1))
            fresh["one"] = lax.ppermute(total_of(blocks[turn][1], boths[turn]).astype(bf16), every, flip_pairs(0))
        if n >= 2:
            turn = order[n - 2]
            terms = [blocks[turn][0], twos[turn], ones[turn]]
            if turn == 1:
                terms.append(along[2])
            fresh["along"] = lax.ppermute(total_of(*terms).astype(bf16), every, turn_pairs(1 if turn == 2 else turn))
        fresh["extra"] = extras[n]()
        if n == 1:
            fresh["extra"].append(input_grad)
        held = list(fresh)
        flat, tree = jax.tree.flatten([fresh[key] for key in held])
        fresh = dict(zip(held, jax.tree.unflatten(tree, lax.optimization_barrier(tuple(flat)))))
        if n == 1:
            input_grad = fresh["extra"].pop()
        extras[n + 1].given = fresh["extra"]
        if n < len(order):
            boths[order[n]] = fresh["both"]
        if n:
            ones[order[n - 1]], twos[order[n - 1]] = fresh["one"], fresh["two"]
        if n >= 2:
            along[order[n - 2]] = fresh["along"]
    whole = total_of(blocks[0][0], twos[0], ones[0], along[1], along[3])
    half = whole.shape[0] // 2
    keep = jnp.where(core == 0, whole[:half], whole[half:])
    give = jnp.where(core == 0, whole[half:], whole[:half])
    got = lax.ppermute(give, every, core_pairs())
    first, second = jnp.where(core == 0, keep, got), jnp.where(core == 0, got, keep)
    conv = jnp.concatenate([first[:conv_rows], second[:conv_rows]], axis=1)
    rows = (half - conv_rows) // 4

    def pieces(side):
        return [side[conv_rows + n * rows : conv_rows + (n + 1) * rows] for n in range(4)]

    left, right = pieces(first), pieces(second)
    lanes = left[3].shape[1] // 2
    heads = jnp.concatenate(left[:3] + [left[3][:, :lanes]] + right[:3] + [right[3][:, :lanes]], axis=1)
    return conv, heads, input_grad


class Summing:
    def __init__(self, every, steps, given=None):
        self.every, self.steps, self.given = every, steps, given

    def __call__(self):
        return [v if pairs is None else v + lax.ppermute(v, self.every, pairs) for v, pairs in zip(self.given, self.steps)]


def line_pairs(bit):
    return [((z * 2 + c) * 4 + s, ((z ^ bit) * 2 + c) * 4 + s) for z in range(4) for c in range(2) for s in range(4)]


def shards(
    features,
    conv_master,
    head_master,
    scale_master,
    join_master,
    affine_scale,
    affine_shift,
    head_cotangent,
    pool_cotangent,
    box_counts,
    proposals,
):
    images, rows, cols, depth = features.shape
    total = head_master.shape[1]
    strip = Strip(rows, cols)
    every = ("dp", "space")
    own_gain, own_join = scale_master.shape[0], join_master.shape[0]
    staged = lax.axis_size("dp") == 8 and lax.axis_size("space") == 4
    line, rank = lax.axis_index("dp"), lax.axis_index("space")
    place = jnp.stack([rank, jnp.int32(lax.axis_size("space")), box_counts[0], line // 2, line % 2]).astype(jnp.int32)
    spread = jnp.asarray(spread_matrix(strip), bf16)
    x = features.reshape(rows * cols, depth)
    if staged:
        packed = pack(strip, conv_master, head_master, scale_master, join_master, x, spread.T)
        conv_full = conv_master.shape[0], *staged_gather(every, *packed)
    else:
        conv_full = lax.all_gather(conv_master.astype(bf16), every, axis=0, tiled=True)
        head_full = lax.all_gather(head_master.astype(bf16), every, axis=0, tiled=True)
        small = jnp.concatenate([scale_master, join_master]).astype(bf16)
        small = lax.all_gather(small[None], every, axis=0, tiled=True).astype(f32)
        small = jnp.concatenate([small[:, :own_gain].reshape(1, total), small[:, own_gain:].reshape(SCALES, total)], axis=0)
        means = []
        for s in range(1, SCALES):
            at = strip.starts(0)[s] - strip.starts(0)[1]
            pick = spread[:, at : at + strip.sizes(0)[s]]
            means.append((mm(pick, x, TN) * (0.25**s)).astype(bf16))
        x = with_rows(strip, [x] + means, "space")
    p0, p1, p2, acts, a3, *loaded = forward(strip, place, x, conv_full, affine_scale, affine_shift, total)
    if staged:
        conv_full, head_full, small = loaded
    pre = p0, p1, p2
    maps, pool, sums, dz, first, final, *halves = head(
        strip, place, a3, head_full, small, head_cotangent.reshape(rows * cols, total), pool_cotangent, proposals,
        spread, affine_scale, p2, staged,
    )
    block_rows = LAYERS * 9 * depth
    conv_rows = None
    if staged:
        swap = functools.partial(lax.ppermute, axis_name=every, perm=core_pairs())
        *halves, dg_keep, dg_give = halves
        others = swap(acts)
        conv_rows = conv_master.shape[0]
        block_rows = packed[0].shape[0] * 2
    else:
        (head_grad,), halves = halves, []
    grad = None
    for layer in (2, 1, 0):
        above, below = from_neighbour(final, 1, "space"), from_neighbour(first, -1, "space")
        if staged:
            keep, give = halves
            pair = [acts, others], [keep, swap(give)]
        else:
            pair = [acts], [dz]
        *grad, token = weight_grad(strip, layer, place, *pair, grad, block_rows, conv_rows)
        if layer == 2 and staged:
            grad = chip_head_grad(place, acts, others, dg_keep, swap(dg_give), grad, conv_rows)
        more = [affine_scale, pre[layer - 1]] if layer else [spread]
        dz, *edge = data_grad(strip, layer, place, dz, above, below, conv_full, token, more, staged)
        if layer:
            first, final, *halves = edge
    input_grad = dz
    me = line * lax.axis_size("space") + rank
    if staged:
        steps = [
            (core_pairs(), flip_pairs(0)),
            (flip_pairs(0), flip_pairs(1)),
            (flip_pairs(1), None),
            (line_pairs(1), None),
            (line_pairs(2), None),
        ]
        extras = [Summing(every, pairs) for pairs in steps] + [Summing(every, ())]
        extras[0].given = [sums, pool]
        conv_grad, head_grad, input_grad = staged_scatter(
            every, [grad[4 * n : 4 * n + 4] for n in range(4)], place[4], conv_rows, extras, input_grad
        )
        sums, pooled = extras[-1].given
    else:
        pooled = lax.psum(pool, "space")
        sums = lax.psum(sums, every)
        conv_grad = lax.psum_scatter(grad[0], every, scatter_dimension=0, tiled=True).astype(f32)
        head_grad = lax.psum_scatter(head_grad, every, scatter_dimension=0, tiled=True).astype(f32)
    return (
        maps.reshape(images, rows, cols, total),
        pooled / box_counts.astype(f32)[:, None],
        input_grad.reshape(images, rows, cols, depth),
        conv_grad,
        head_grad,
        lax.dynamic_slice_in_dim(sums[0], me * own_gain, own_gain),
        lax.dynamic_slice_in_dim(sums[1:].reshape(-1), me * own_join, own_join),
    )


def solution(mesh):
    return jax.shard_map(
        shards,
        mesh=mesh,
        in_specs=(
            P("dp", "space", None, None),
            P(("dp", "space"), None),
            P(("dp", "space"), None),
            P(("dp", "space")),
            P(("dp", "space")),
            P(),
            P(),
            P("dp", "space", None, None),
            P("dp", None),
            P("dp"),
            P("dp", None),
        ),
        out_specs=(
            P("dp", "space", None, None),
            P("dp", None),
            P("dp", "space", None, None),
            P(("dp", "space"), None),
            P(("dp", "space"), None),
            P(("dp", "space")),
            P(("dp", "space")),
        ),
        check_vma=False,
    )
```

```python
import functools

import jax
import jax.numpy as jnp
import numpy as np
from jax import lax
from jax.experimental import pallas as pl
from jax.experimental.pallas import tpu as pltpu
from jax.sharding import PartitionSpec as P

HEAD_CH = 256
TASK_HEADS = 7
SCALES = 3
LAYERS = 3
PAD = 8

epsilon = 1e-06
f32 = jnp.float32
bf16 = jnp.bfloat16
NN = (((1,), (0,)), ((), ()))
NT = (((1,), (1,)), ((), ()))
TN = (((0,), (0,)), ((), ()))


def mm(left, right, dims=NN):
    return lax.dot_general(left, right, dims, preferred_element_type=f32)


def split_mm(left, right):
    high = right.astype(bf16)
    low = (right - high.astype(f32)).astype(bf16)
    return mm(left, high) + mm(left, low)


class Strip:
    def __init__(self, rows, cols):
        self.rows = [rows >> s for s in range(SCALES)]
        self.cols = [cols >> s for s in range(SCALES)]

    def sizes(self, halo):
        return [(r + 2 * halo) * c for r, c in zip(self.rows, self.cols)]

    def starts(self, halo):
        sizes = self.sizes(halo)
        return [sum(sizes[:s]) for s in range(SCALES)]

    def total(self, halo):
        return sum(self.sizes(halo))

    def own(self, halo):
        return [st + halo * c for st, c in zip(self.starts(halo), self.cols)]


def spread_matrix(strip):
    rows, cols = strip.rows[0], strip.cols[0]
    parts = []
    for s in range(1, SCALES):
        mat = np.zeros((rows * cols, strip.rows[s] * strip.cols[s]), np.float32)
        for r in range(rows):
            for c in range(cols):
                mat[r * cols + c, (r >> s) * strip.cols[s] + (c >> s)] = 1.0
        parts.append(mat)
    return np.concatenate(parts, axis=1)


def column_of(strip, scale, count):
    return lax.broadcasted_iota(jnp.int32, (count, 1), 0) % strip.cols[scale]


def shifted_copies(strip, halo, act, wide, depth):
    for s in range(SCALES):
        start, count, cols = strip.starts(halo)[s], strip.sizes(halo)[s], strip.cols[s]
        column = column_of(strip, s, count)
        for k in range(3):
            rows = act[PAD + start + k - 1 : PAD + start + k - 1 + count, :]
            if k == 0:
                rows = jnp.where(column == 0, 0.0, rows)
            if k == 2:
                rows = jnp.where(column == cols - 1, 0.0, rows)
            wide[start : start + count, k * depth : (k + 1) * depth] = rows.astype(bf16)


def patches(strip, halo, wide, cells, depth, flip=False, base=0):
    for s in range(SCALES):
        cols = strip.cols[s]
        count = strip.sizes(halo)[s]
        source, target = strip.starts(halo + 1)[s], strip.starts(halo)[s]
        for ky in range(3):
            first = source + (2 - ky if flip else ky) * cols
            for kx in range(3):
                col = (2 - kx if flip else kx) * depth
                tap = 3 * ky + kx
                cells[base + target : base + target + count, tap * depth : (tap + 1) * depth] = wide[
                    first : first + count, col : col + depth
                ]


FLIPS = ((1, 2), (2, 1))
TURNS = (0, 1, 3, 2)
GROUPS = (((0, 1, 2, 3),),) * 3 + (((0, 1, 2), (3,)),)
ITEMS = tuple(
    item
    for n in range(4)
    for item in [(n, True, (part,)) for part in range(4)] + [(n, False, group) for group in GROUPS[n]]
)


def across(place, part, core):
    rank = place[0]
    for bit in range(2):
        if part >> bit & 1:
            rank = rank ^ jnp.where(core == 0, FLIPS[0][bit], FLIPS[1][bit])
    return rank


def load_blocks(conv_rows, place, refs, weights, head_w, sem):
    depth = weights.shape[1]
    pieces, rows = head_w.shape[:2]
    head_rows = rows * conv_rows // weights.shape[0]
    layer_rows = weights.shape[0] // LAYERS
    last = [-(-layer_rows * (n + 1) // conv_rows) for n in range(LAYERS)]
    blocks = []
    for (n, own, parts), ref in zip(ITEMS, refs):
        core = place[4] if own else 1 - place[4]
        z = (place[3] + 4 - TURNS[n]) % 4
        for at, part in enumerate(parts):
            block = ref if len(parts) == 1 else ref.at[at]
            blocks.append((block, (z * 2 + core) * 4 + across(place, part, core)))
    for layer in range(LAYERS):
        for block, k in blocks:
            copy = pltpu.make_async_copy(
                block.at[pl.ds(0, conv_rows), :],
                weights.at[pl.ds(pl.multiple_of(k * conv_rows, 16), conv_rows), :],
                sem.at[layer],
            )
            inside = k < last[layer]
            if layer:
                inside = inside & (k >= last[layer - 1])
            pl.when(inside)(copy.start)
    for block, k in blocks:
        pltpu.make_async_copy(
            block.at[pl.ds(conv_rows, pieces * head_rows), :].reshape(pieces, head_rows, depth),
            head_w.at[:, pl.ds(pl.multiple_of(k * head_rows, 16), head_rows), :],
            sem.at[LAYERS],
        ).start()
    waits = []
    for first, stop in zip([0] + last, last):
        rows = weights.at[pl.ds(first * conv_rows, (stop - first) * conv_rows), :]
        waits.append(pltpu.make_async_copy(rows, rows, sem.at[len(waits)]))
    return waits + [pltpu.make_async_copy(head_w, head_w, sem.at[LAYERS])]


def prepare_kernel(strip, depth, place, x_ref, above_ref, below_ref, *refs):
    blocks, (cells, acts_ref, token, strips, act, wide, x_sem) = refs[:4], refs[4:]
    strips[...] = jnp.zeros(strips.shape, bf16)
    coarse = strips.shape[1]
    fetches = []
    for part in range(4):
        copy = pltpu.make_async_copy(
            blocks[part].at[pl.ds(blocks[part].shape[0] - coarse, coarse), :],
            strips.at[3 + across(place, part, place[4])],
            x_sem.at[part],
        )
        copy.start()
        fetches.append(copy)
    token[...] = jnp.zeros(token.shape, f32)
    at = PAD
    for ref in (above_ref, x_ref, below_ref):
        act[at : at + ref.shape[0], :] = ref[...].astype(f32)
        at += ref.shape[0]
    for copy in fetches:
        copy.wait()
    for s in range(1, SCALES):
        rows, cols = strip.rows[s], strip.cols[s]
        first = strip.starts(0)[s] - strip.starts(0)[1]
        for row in range(-3, rows + 3):
            source = strips[place[0] + 3 + row // rows, first + row % rows * cols : first + (row % rows + 1) * cols, :]
            act[at : at + cols, :] = source.astype(f32)
            at += cols
    first_patches(strip, depth, act, wide, cells, acts_ref)


def first_patches(strip, depth, act, wide, cells, acts_ref):
    for s in range(SCALES):
        start, size = strip.starts(1)[s], strip.sizes(1)[s]
        first = PAD + strip.starts(3)[s] + 2 * strip.cols[s]
        acts_ref[start : start + size, :] = act[first : first + size, :].astype(bf16)
    shifted_copies(strip, LAYERS, act, wide, depth)
    patches(strip, LAYERS - 1, wide, cells, depth)


def pack_kernel(strip, conv_ref, head_ref, gain_ref, join_ref, x_ref, gather_ref, own_ref, wide_ref, top_ref, bottom_ref):
    depth = conv_ref.shape[1]
    at = conv_ref.shape[0]
    rows, head_cols = head_ref.shape
    for ref in (own_ref, wide_ref):
        ref[:at, :] = conv_ref[...].astype(bf16)
    for first in range(0, head_cols, depth):
        width = min(depth, head_cols - first)
        piece = head_ref[:, first : first + width]
        if width < depth:
            small = jnp.concatenate([gain_ref[...], join_ref[...]], axis=1)
            small = jnp.concatenate([small, jnp.zeros((1, depth - width - small.shape[1]), f32)], axis=1)
            row = lax.broadcasted_iota(jnp.int32, (rows, depth - width), 0)
            small = jnp.where(row == 0, jnp.broadcast_to(small, (rows, depth - width)), 0.0)
            piece = jnp.concatenate([piece, small], axis=1)
        for ref in (own_ref, wide_ref):
            ref[at : at + rows, :] = piece.astype(bf16)
        at += rows
    x = x_ref[...]
    sums = mm(gather_ref[...], x)
    for s in range(1, SCALES):
        first = strip.starts(0)[s] - strip.starts(0)[1]
        size = strip.sizes(0)[s]
        wide_ref[at : at + size, :] = (sums[first : first + size] * (0.25**s)).astype(bf16)
        at += size
    edge = 3 * strip.cols[0]
    top_ref[...] = x_ref[:edge, :]
    bottom_ref[...] = x_ref[x.shape[0] - edge :, :]


def forward_kernel(strip, depth, staged, place, scale_ref, shift_ref, *refs):
    taps = 9 * depth
    halos = [LAYERS - 1 - layer for layer in range(LAYERS)]
    if staged:
        conv_rows, head_cols = staged
        expand_hbm, owner_ref, first_cells, *refs = refs
        blocks, refs = refs[: len(ITEMS)], refs[len(ITEMS) :]
        first_acts, refs = refs[0], refs[1:]
        p_refs, refs = refs[:3], refs[3:]
        a3_ref, small_ref, weights, head_ref, acts_ref, act, wide, cells, expand, sem = refs
        loads = load_blocks(conv_rows, place, blocks, weights, head_ref, sem)
        expand_load = pltpu.make_async_copy(expand_hbm, expand, sem.at[LAYERS + 1])
        expand_load.start()
        acts_ref[: first_acts.shape[0], :] = first_acts[...]
    else:
        x_ref, w_hbm, *refs = refs
        p_refs, refs = refs[:3], refs[3:]
        a3_ref, acts_ref, weights, act, wide, cells, sem = refs
        load = pltpu.make_async_copy(w_hbm, weights, sem.at[0])
        load.start()
        act[PAD : PAD + strip.total(3), :] = x_ref[...].astype(f32)
        first_cells = cells
        first_patches(strip, depth, act, wide, cells, acts_ref)
        load.wait()
    here, ranks = place[0], place[1]
    flat = strip.starts(0)
    for layer, halo in enumerate(halos):
        count = strip.total(halo)
        if layer:
            shifted_copies(strip, halo + 1, act, wide, depth)
            patches(strip, halo, wide, cells, depth)
        used = cells if layer else first_cells
        own = strip.own(halo)
        if staged:
            loads[layer].wait()
        for half in range(depth // 256):
            lanes = slice(half * 256, (half + 1) * 256)
            z = mm(used[:count, :], weights[layer * taps : (layer + 1) * taps, lanes])
            p = z * scale_ref[layer : layer + 1, lanes] + shift_ref[layer : layer + 1, lanes]
            a = (p / (1.0 + jnp.exp(-p))).astype(bf16)
            for s in range(SCALES):
                size = strip.sizes(0)[s]
                p_refs[layer][flat[s] : flat[s] + size, lanes] = p[own[s] : own[s] + size]
            if layer == LAYERS - 1:
                a3_ref[:, lanes] = a
                acts_ref[LAYERS * strip.total(1) :, lanes] = a
            else:
                for s in range(SCALES):
                    start, size = strip.starts(halo)[s], strip.sizes(halo)[s]
                    row = lax.broadcasted_iota(jnp.int32, (size, 1), 0) // strip.cols[s]
                    row = row + here * strip.rows[s] - halo
                    inside = (row >= 0) & (row < ranks * strip.rows[s])
                    kept = jnp.where(inside, a[start : start + size].astype(f32), 0.0)
                    act[PAD + start : PAD + start + size, lanes] = kept
                    edge = (halo - 1) * strip.cols[s]
                    first, size = (layer + 1) * strip.total(1) + strip.starts(1)[s], strip.sizes(1)[s]
                    acts_ref[first : first + size, lanes] = kept[edge : edge + size].astype(bf16)
    if staged:
        loads[LAYERS].wait()
        expand_load.wait()
        owners, spare = owner_ref.shape[0], expand.shape[0]
        pieces, depth_rows = head_ref.shape[:2]
        row = lax.broadcasted_iota(jnp.int32, (owners, depth_rows), 0)
        col = lax.broadcasted_iota(jnp.int32, (owners, depth_rows), 1)
        pick = jnp.where(col == row * (depth_rows // owners), 1.0, 0.0).astype(bf16)
        picked = mm(pick, head_ref[pieces - 1, :, depth - spare :]).astype(bf16)
        for n in range(1 + SCALES):
            cols = slice(n * head_cols, (n + 1) * head_cols)
            spread = mm(picked, expand[:, cols]) * owner_ref[:, cols].astype(f32)
            small_ref[n : n + 1, :] = jnp.sum(spread, axis=0, keepdims=True)


def slope(p):
    sigma = 1.0 / (1.0 + jnp.exp(-p))
    return sigma * (1.0 + p * (1.0 - sigma))


def head_kernel(
    strip, split, place, a3_ref, w_ref, small_ref, cot_ref, pool_cot_ref, where_ref, spread_ref, gather_ref,
    scale_ref, p2_ref, maps_ref, pool_ref, sums_ref, *refs,
):
    if split:
        *grads, keep_ref, give_ref, dg_all = refs
    else:
        *grads, w_grad_ref, dg_all = refs
    fine = strip.sizes(0)[0]
    starts, sizes = strip.starts(0), strip.sizes(0)
    parts = [slice(starts[s], starts[s] + sizes[s]) for s in range(SCALES)]
    slots = where_ref.shape[1]
    pixel = lax.broadcasted_iota(jnp.int32, (fine, slots), 0) + place[0] * fine
    slot = lax.broadcasted_iota(jnp.int32, (fine, slots), 1)
    hits = jnp.where((where_ref[...] == pixel) & (slot < place[2]), 1.0, 0.0)
    hits = jnp.sum(hits, axis=-1, keepdims=True)
    share = pool_cot_ref[...] / place[2].astype(f32)
    heads = maps_ref.shape[1] // HEAD_CH
    depth = a3_ref.shape[1]
    per = depth // HEAD_CH
    da3 = None
    for head in range(heads):
        lanes = slice(head * HEAD_CH, (head + 1) * HEAD_CH)
        if split:
            weight = w_ref[head // per, :, head % per * HEAD_CH : (head % per + 1) * HEAD_CH]
        else:
            weight = w_ref[:, lanes]
        g = mm(a3_ref[...], weight)
        inverse = lax.rsqrt(jnp.sum(g * g, axis=-1, keepdims=True) + epsilon)
        unit = g * inverse
        gain = small_ref[0:1, lanes]
        join = [small_ref[1 + s : 2 + s, lanes] for s in range(SCALES)]
        normed = unit * gain
        coarse = jnp.concatenate([normed[parts[s]] * join[s] for s in range(1, SCALES)], axis=0)
        joined = normed[:fine] * join[0] + split_mm(spread_ref[...], coarse)
        maps_ref[:, lanes] = joined.astype(bf16)
        fused = cot_ref[:, lanes]
        if head == 0:
            pool_ref[...] = jnp.sum(joined * hits, axis=0, keepdims=True)
            fused = fused.astype(f32) + hits * share
            down_coarse = split_mm(gather_ref[...], fused)
        else:
            down_coarse = mm(gather_ref[...], fused)
        down = jnp.concatenate([fused.astype(f32), down_coarse], axis=0)
        product = down * normed
        scaled = []
        for s in range(SCALES):
            sums_ref[s + 1 : s + 2, lanes] = jnp.sum(product[parts[s]], axis=0, keepdims=True)
            scaled.append(down[parts[s]] * join[s])
        dn = jnp.concatenate(scaled, axis=0)
        sums_ref[0:1, lanes] = jnp.sum(dn * unit, axis=0, keepdims=True)
        du = dn * gain
        dg = (inverse * (du - unit * jnp.sum(du * unit, axis=-1, keepdims=True))).astype(bf16)
        dg_all[head] = dg
        if not split:
            w_grad_ref[:, lanes] = mm(a3_ref[...], dg, TN).astype(bf16)
        part = mm(dg, weight, NT)
        da3 = part if da3 is None else da3 + part
    layer = LAYERS - 1
    dz = da3 * scale_ref[layer : layer + 1, :] * slope(p2_ref[...])
    emit_grad(strip, place, dz.astype(bf16), *grads)
    if split:
        width = HEAD_CH
        first = place[4] == 0
        half = heads * width // 2
        for start in range(0, half, width // 2):
            left = dg_all[start // width, :, start % width : start % width + width // 2]
            at = half + start
            right = dg_all[at // width, :, at % width : at % width + width // 2]
            keep_ref[:, start : start + width // 2] = jnp.where(first, left, right)
            give_ref[:, start : start + width // 2] = jnp.where(first, right, left)


def emit_grad(strip, place, dz, dz_ref, first_ref, last_ref, keep_ref=None, give_ref=None):
    dz_ref[...] = dz
    edge = 0
    for start, size, cols in zip(strip.starts(0), strip.sizes(0), strip.cols):
        first_ref[edge : edge + cols, :] = dz[start : start + cols]
        last_ref[edge : edge + cols, :] = dz[start + size - cols : start + size]
        edge += cols
    if keep_ref is not None:
        middle = dz.shape[1] // 2
        left, right = dz[:, :middle], dz[:, middle:]
        first = place[4] == 0
        keep_ref[...] = jnp.where(first, left, right)
        give_ref[...] = jnp.where(first, right, left)


def store_blocks(place, pieces, block_refs, sem):
    for turn in range(4):
        for part in range(4):
            out = block_refs[4 * turn + part]
            z = (place[3] + turn) % 4
            rank = across(place, part, place[4])
            for core in range(2):
                k = (z * 2 + core) * 4 + rank
                base = core * (out.shape[0] // 2)
                for condition, source, row in pieces(k):
                    copy = pltpu.make_async_copy(source, out.at[pl.ds(base + row, source.shape[0]), :], sem)
                    if condition is None:
                        copy.start()
                    else:
                        pl.when(condition)(copy.start)


def weight_grad_kernel(strip, depth, layer, images, conv_rows, place, *refs):
    acts, grads = refs[:images], refs[images : 2 * images]
    *outs, token, act, wide, cells, dz, result, sem = refs[2 * images :]
    own, count = strip.total(0), strip.total(1)
    for n in range(images):
        act[PAD : PAD + count, :] = acts[n][layer * count : (layer + 1) * count, :].astype(f32)
        shifted_copies(strip, 1, act, wide, depth)
        patches(strip, 0, wide, cells, depth, base=n * own)
        dz[n * own : (n + 1) * own, :] = grads[n][...]
    for tap in range(9):
        lanes = slice(tap * depth, (tap + 1) * depth)
        result[lanes, :] = mm(cells[:, lanes], dz[...], TN).astype(bf16)
    rows = 9 * depth
    first_row, stop_row = layer * rows, (layer + 1) * rows
    token[...] = jnp.zeros(token.shape, f32)
    if conv_rows is None:
        copy = pltpu.make_async_copy(result, outs[-1].at[pl.ds(first_row, rows), :], sem)
        copy.start()
        copy.wait()
        return

    def pieces(k):
        out = []
        inside = (k * conv_rows >= first_row) & ((k + 1) * conv_rows <= stop_row)
        start = jnp.where(inside, k * conv_rows - first_row, 0)
        out.append((inside, result.at[pl.ds(pl.multiple_of(start, 16), conv_rows), :], 0))
        if first_row % conv_rows:
            size = conv_rows - first_row % conv_rows
            out.append((k == first_row // conv_rows, result.at[pl.ds(0, size), :], conv_rows - size))
        if stop_row % conv_rows:
            size = stop_row % conv_rows
            out.append((k == stop_row // conv_rows, result.at[pl.ds(rows - size, size), :], 0))
        return out

    store_blocks(place, pieces, outs[-16:], sem)
    pltpu.make_async_copy(result, result, sem).wait()


def chip_head_grad_kernel(conv_rows, place, a3_ref, other_ref, keep_ref, got_ref, *refs):
    refs = refs[-(16 + 4) :]
    outs, (a3, dg, result, out_sem) = refs[:16], refs[16:]
    own = keep_ref.shape[0]
    for n, ref in enumerate((a3_ref, other_ref)):
        pltpu.make_async_copy(ref.at[pl.ds(ref.shape[0] - own, own), :], a3.at[pl.ds(n * own, own), :], out_sem).start()
    pltpu.make_async_copy(a3, a3, out_sem).wait()
    dg[:own, :] = keep_ref[...]
    dg[own:, :] = got_ref[...]
    width = result.shape[2]
    cols = dg.shape[1]
    for piece in range(result.shape[0]):
        stop = min(cols, (piece + 1) * width)
        lanes = slice(piece * width, stop)
        result[piece, :, : stop - piece * width] = mm(a3[...], dg[:, lanes], TN).astype(bf16)
    if cols % width:
        result[result.shape[0] - 1, :, cols % width :] = jnp.zeros((result.shape[1], width - cols % width), bf16)
    rows = (outs[0].shape[0] // 2 - conv_rows) // result.shape[0]

    def pieces(k):
        return [
            (None, result.at[piece, pl.ds(pl.multiple_of(k * rows, 16), rows), :], conv_rows + piece * rows)
            for piece in range(result.shape[0])
        ]

    store_blocks(place, pieces, outs, out_sem)
    pltpu.make_async_copy(result, result, out_sem).wait()


def data_grad_kernel(
    strip, depth, layer, place, dz_ref, above_ref, below_ref, w_ref, _, *refs
):
    refs, (act, wide, cells) = refs[:-3], refs[-3:]
    last = layer == 0
    if last:
        spread_ref, out_ref = refs
    else:
        scale_ref, p_ref, *outs = refs
    edge = 0
    for s in range(SCALES):
        start, size, cols = strip.starts(1)[s], strip.sizes(0)[s], strip.cols[s]
        flat = strip.starts(0)[s]
        act[PAD + start : PAD + start + cols, :] = above_ref[edge : edge + cols, :].astype(f32)
        act[PAD + start + cols : PAD + start + cols + size, :] = dz_ref[flat : flat + size, :].astype(f32)
        act[PAD + start + cols + size : PAD + start + 2 * cols + size, :] = below_ref[edge : edge + cols, :].astype(f32)
        edge += cols
    shifted_copies(strip, 1, act, wide, depth)
    patches(strip, 0, wide, cells, depth, flip=True)
    base = layer * 9 * depth
    value = None
    for tap in range(9):
        term = mm(
            cells[:, tap * depth : (tap + 1) * depth], w_ref[base + tap * depth : base + (tap + 1) * depth, :], NT
        )
        value = term if value is None else value + term
    if last:
        fine = strip.sizes(0)[0]
        coarse = jnp.concatenate(
            [
                value[st : st + size] * (0.25**s)
                for s, (st, size) in enumerate(zip(strip.starts(0), strip.sizes(0)))
                if s
            ],
            axis=0,
        )
        out_ref[...] = value[:fine] + split_mm(spread_ref[...], coarse)
    else:
        dz = value * scale_ref[layer - 1 : layer, :] * slope(p_ref[...])
        emit_grad(strip, place, dz.astype(bf16), *outs)


def vmem(shape=None, index=None):
    if shape is None:
        return pl.BlockSpec(memory_space=pltpu.VMEM)
    return pl.BlockSpec(shape, index)


SMEM = pl.BlockSpec(memory_space=pltpu.SMEM)
ANY = pl.BlockSpec(memory_space=pl.ANY)


def params(mebibytes):
    return pltpu.CompilerParams(vmem_limit_bytes=mebibytes << 20)


def small_layout(owners, cols, spare):
    gains = cols // owners
    expand = np.zeros((spare, (1 + SCALES) * cols), np.float32)
    owner = np.zeros((owners, (1 + SCALES) * cols), np.float32)
    for n in range((1 + SCALES) * cols):
        size = gains if n < cols else SCALES * gains
        at = n if n < cols else n - cols
        expand[at % size + (0 if n < cols else gains), n] = 1.0
        owner[at // size, n] = 1.0
    return jnp.asarray(expand, bf16), jnp.asarray(owner, bf16)


def pack(strip, conv, head_w, gain, join, x, gather):
    depth = conv.shape[1]
    rows = conv.shape[0] + head_w.shape[0] * -(-head_w.shape[1] // depth)
    edge = 3 * strip.cols[0]
    return pl.pallas_call(
        functools.partial(pack_kernel, strip),
        name="pack",
        out_shape=[jax.ShapeDtypeStruct((n, depth), bf16) for n in (rows, rows + gather.shape[0], edge, edge)],
        in_specs=[vmem()] * 6,
        out_specs=[vmem()] * 4,
        compiler_params=params(60),
    )(conv, head_w, gain[None], join[None], x, gather)


def on_chip(values):
    return [pltpu.with_memory_space_constraint(v, pltpu.MemorySpace.VMEM) for v in values]


def off_chip(values):
    return [pltpu.with_memory_space_constraint(v, pltpu.MemorySpace.HBM) for v in values]


def forward_scratch(strip, depth, halo):
    return [
        pltpu.VMEM((strip.total(halo) + 2 * PAD, depth), f32),
        pltpu.VMEM((strip.total(halo), 3 * depth), bf16),
    ]


def prepare(strip, place, x, edges, blocks, owners):
    depth = x.shape[1]
    coarse = strip.total(0) - strip.sizes(0)[0]
    return pl.pallas_call(
        functools.partial(prepare_kernel, strip, depth),
        name="prepare",
        out_shape=[
            pltpu.VMEM((strip.total(LAYERS - 1), 9 * depth), bf16),
            pltpu.VMEM((strip.total(1), depth), bf16),
            jax.ShapeDtypeStruct((8, 128), f32),
        ],
        in_specs=[SMEM] + [vmem()] * 3 + [ANY] * len(blocks),
        out_specs=[vmem()] * 3,
        scratch_shapes=[pltpu.VMEM((6 + owners // 8, coarse, depth), bf16)]
        + forward_scratch(strip, depth, LAYERS)
        + [pltpu.SemaphoreType.DMA((4,))],
        compiler_params=params(10),
    )(place, x, *edges, *off_chip(blocks))


def forward(strip, place, x, conv, scale, shift, head_cols):
    depth = scale.shape[1]
    own = strip.total(0)
    rows = LAYERS * 9 * depth
    acts = (LAYERS * strip.total(1) + own, depth)
    staged = isinstance(conv, tuple)
    cells = pltpu.VMEM((strip.total(1 if staged else LAYERS - 1), 9 * depth), bf16)
    if staged:
        conv_rows, prepared, blocks = conv
        expand, owner = small_layout(rows // conv_rows, head_cols, -head_cols % depth)
        first_cells, first_acts = on_chip(prepared)
        inputs = [expand, owner, first_cells, *off_chip(blocks), first_acts]
        in_specs = [ANY, vmem(), vmem()] + [ANY] * len(blocks) + [vmem()]
        outs = [pltpu.VMEM((own, depth), f32)] * 3 + [
            pltpu.VMEM((own, depth), bf16),
            pltpu.VMEM((1 + SCALES, head_cols), f32),
            pltpu.VMEM((rows, depth), bf16),
            pltpu.VMEM((-(-head_cols // depth), depth, depth), bf16),
            pltpu.VMEM(acts, bf16),
        ]
        scratch = forward_scratch(strip, depth, LAYERS - 1)
        scratch += [cells, pltpu.VMEM(expand.shape, bf16), pltpu.SemaphoreType.DMA((LAYERS + 2,))]
    else:
        inputs, in_specs = [x, conv], [vmem(), ANY]
        outs = [jax.ShapeDtypeStruct((own, depth), f32)] * 3
        outs += [jax.ShapeDtypeStruct(shape, bf16) for shape in ((own, depth), acts)]
        scratch = [pltpu.VMEM((rows, depth), bf16)] + forward_scratch(strip, depth, LAYERS)
        scratch += [cells, pltpu.SemaphoreType.DMA((1,))]
    return pl.pallas_call(
        functools.partial(forward_kernel, strip, depth, (conv_rows, head_cols) if staged else None),
        name="forward",
        out_shape=outs,
        in_specs=[SMEM, vmem(), vmem()] + in_specs,
        out_specs=[vmem()] * len(outs),
        scratch_shapes=scratch,
        compiler_params=params(28 if staged else 54),
    )(place, scale, shift, *inputs)


def head(strip, place, a3, weight, small, cot, pool_cot, where, spread, scale, p2, split):
    own, depth = a3.shape
    total = small.shape[1]
    fine = strip.sizes(0)[0]
    edge = sum(strip.cols)
    outs = [
        jax.ShapeDtypeStruct((fine, total), bf16),
        jax.ShapeDtypeStruct((1, HEAD_CH), f32),
        jax.ShapeDtypeStruct((1 + SCALES, total), f32),
    ]
    outs += [jax.ShapeDtypeStruct((n, depth), bf16) for n in (own, edge, edge)]
    if split:
        outs += [jax.ShapeDtypeStruct((own, n // 2), bf16) for n in (depth, depth, total, total)]
    else:
        outs += [jax.ShapeDtypeStruct((depth, total), bf16)]
    return pl.pallas_call(
        functools.partial(head_kernel, strip, split),
        name="heads",
        out_shape=outs,
        in_specs=[SMEM] + [vmem()] * 10,
        out_specs=[vmem()] * len(outs),
        scratch_shapes=[pltpu.VMEM((total // HEAD_CH, own, HEAD_CH), bf16)],
        compiler_params=params(24),
    )(place, a3, weight, small, cot, pool_cot, where, spread, spread.T, scale, p2)


def weight_grad(strip, layer, place, acts, grads, into, rows, conv_rows):
    own, half = grads[0].shape
    depth = acts[0].shape[1]
    images = len(acts)
    count_here = strip.total(1)
    into = into or []
    count = 1 if conv_rows is None else 16
    return pl.pallas_call(
        functools.partial(weight_grad_kernel, strip, depth, layer, images, conv_rows),
        name="weight_grad",
        out_shape=[pltpu.HBM((rows, half), bf16)] * count + [jax.ShapeDtypeStruct((8, 128), f32)],
        in_specs=[SMEM] + [vmem()] * (2 * images) + [ANY] * len(into),
        out_specs=[ANY] * count + [vmem()],
        scratch_shapes=[
            pltpu.VMEM((count_here + 2 * PAD, depth), f32),
            pltpu.VMEM((count_here, 3 * depth), bf16),
            pltpu.VMEM((images * own, 9 * depth), bf16),
            pltpu.VMEM((images * own, half), bf16),
            pltpu.VMEM((9 * depth, half), bf16),
            pltpu.SemaphoreType.DMA,
        ],
        input_output_aliases={1 + 2 * images + n: n for n in range(len(into))},
        compiler_params=params(22),
    )(place, *acts, *grads, *off_chip(into))


def chip_head_grad(place, a3, other, keep, got, blocks, conv_rows):
    own, depth = keep.shape[0], a3.shape[1]
    half = blocks[0].shape[1]
    pieces = -(-keep.shape[1] // half)
    return pl.pallas_call(
        functools.partial(chip_head_grad_kernel, conv_rows),
        name="chip_head_grad",
        out_shape=[pltpu.HBM(b.shape, bf16) for b in blocks],
        in_specs=[SMEM, ANY, ANY, vmem(), vmem()] + [ANY] * 16,
        out_specs=[ANY] * 16,
        scratch_shapes=[
            pltpu.VMEM((2 * own, depth), bf16),
            pltpu.VMEM((2 * own, keep.shape[1]), bf16),
            pltpu.VMEM((pieces, depth, half), bf16),
            pltpu.SemaphoreType.DMA,
        ],
        input_output_aliases={5 + n: n for n in range(16)},
        compiler_params=params(10),
    )(place, a3, other, keep, got, *off_chip(blocks))


def data_grad(strip, layer, place, dz, above, below, conv, token, others, split):
    if split:
        conv = pltpu.with_memory_space_constraint(conv, pltpu.MemorySpace.VMEM)
    own, depth = dz.shape
    last = layer == 0
    edge = sum(strip.cols)

    if last:
        outs = [jax.ShapeDtypeStruct((strip.sizes(0)[0], depth), f32)]
    else:
        outs = [jax.ShapeDtypeStruct((n, depth), bf16) for n in (own, edge, edge)]
        outs += [jax.ShapeDtypeStruct((own, depth // 2), bf16)] * (2 * split)
    return pl.pallas_call(
        functools.partial(data_grad_kernel, strip, depth, layer),
        name="data_grad",
        out_shape=outs,
        in_specs=[SMEM] + [vmem()] * 4 + [ANY] + [vmem()] * len(others),
        out_specs=[vmem()] * len(outs),
        scratch_shapes=[
            pltpu.VMEM((strip.total(1) + 2 * PAD, depth), f32),
            pltpu.VMEM((strip.total(1), 3 * depth), bf16),
            pltpu.VMEM((own, 9 * depth), bf16),
        ],
        compiler_params=params(14 if split else 32),
    )(place, dz, above, below, conv, token, *others)


def from_neighbour(cells, distance, axis):
    count = lax.axis_size(axis)
    pairs = [(i, i + distance) for i in range(count) if 0 <= i + distance < count]
    return lax.ppermute(cells, axis, pairs)


def with_rows(strip, levels, axis):
    above = [[] for _ in levels]
    below = [[] for _ in levels]
    left = [3] * len(levels)
    distance = 1
    while max(left) > 0:
        take = [min(n, r) for n, r in zip(left, strip.rows)]
        tails = [v[v.shape[0] - t * c :] for v, t, c in zip(levels, take, strip.cols) if t]
        heads = [v[: t * c] for v, t, c in zip(levels, take, strip.cols) if t]
        got_tail = from_neighbour(jnp.concatenate(tails, axis=0), distance, axis)
        got_head = from_neighbour(jnp.concatenate(heads, axis=0), -distance, axis)
        at = 0
        for s, (t, c) in enumerate(zip(take, strip.cols)):
            if t:
                above[s].insert(0, got_tail[at : at + t * c])
                below[s].append(got_head[at : at + t * c])
                at += t * c
        left = [n - t for n, t in zip(left, take)]
        distance += 1
    return jnp.concatenate([v for s, own in enumerate(levels) for v in above[s] + [own] + below[s]], axis=0)


def after(value, *others):
    return lax.optimization_barrier((value,) + others)[0]


def turn_pairs(step):
    return [((z * 2 + c) * 4 + s, (((z + step) % 4) * 2 + c) * 4 + s) for z in range(4) for c in range(2) for s in range(4)]


def flip_pairs(which):
    return [((z * 2 + c) * 4 + s, (z * 2 + c) * 4 + (s ^ FLIPS[c][which])) for z in range(4) for c in range(2) for s in range(4)]


def core_pairs():
    return [((z * 2 + c) * 4 + s, (z * 2 + 1 - c) * 4 + s) for z in range(4) for c in range(2) for s in range(4)]


def staged_gather(every, own, wide, tops, bottoms, begin):
    def swap(n, parts):
        four = [lines[n], ones[n], twos[n], boths[n]] if len(boths) > n else [lines[n], ones[n], twos[n]]
        chosen = [four[part] for part in parts]
        return lax.ppermute(jnp.stack(chosen) if len(parts) > 1 else chosen[0], every, core_pairs())

    lines, ones, twos, boths, swaps = [wide], [], [], [], [[] for _ in TURNS]
    ends = len(TURNS) - 1
    for turn in range(len(TURNS) + 1):
        fresh = {}
        if turn < len(TURNS):
            fresh["one"] = lax.ppermute(lines[turn], every, flip_pairs(0))
            fresh["two"] = lax.ppermute(lines[turn], every, flip_pairs(1))
        if turn < ends:
            step = TURNS[turn + 1]
            if step == 2:
                fresh["line"] = lax.ppermute(after(lines[1], *ones), every, turn_pairs(1))
            else:
                fresh["line"] = lax.ppermute(after(own, *ones) if ones else own, every, turn_pairs(step))
        if turn:
            fresh["both"] = lax.ppermute(ones[turn - 1], every, flip_pairs(1))
        if turn >= 2:
            fresh["swap"] = swap(turn - 2, GROUPS[turn - 2][0])
        if turn == ends:
            *prepared, fresh["token"] = begin(edges, [lines[0], ones[0], twos[0], boths[0]])
        if turn == len(TURNS):
            fresh["early"] = swap(ends, GROUPS[ends][0])
        if not turn:
            fresh["above"] = from_neighbour(bottoms, 1, "space")
            fresh["below"] = from_neighbour(tops, -1, "space")
        fresh = dict(zip(fresh, lax.optimization_barrier(tuple(fresh.values()))))
        if not turn:
            edges = [fresh["above"], fresh["below"]]
        if turn < len(TURNS):
            ones.append(fresh["one"])
            twos.append(fresh["two"])
        if turn < ends:
            lines.append(fresh["line"])
        if turn:
            boths.append(fresh["both"])
        if turn >= 2:
            swaps[turn - 2].append(fresh["swap"])
    swaps[ends] += [fresh["early"], swap(ends, GROUPS[ends][1])]
    mine = [lines, ones, twos, boths]
    groups = {(n, group): array for n in range(len(TURNS)) for group, array in zip(GROUPS[n], swaps[n])}
    return prepared, [mine[parts[0]][n] if own_side else groups[n, parts] for n, own_side, parts in ITEMS]


def total_of(*terms):
    return sum((t.astype(f32) for t in terms[1:]), terms[0].astype(f32))


def staged_scatter(every, blocks, core, conv_rows, extras, input_grad, *hold):
    order = TURNS[::-1]
    boths, ones, twos, parts = {}, {}, {}, {}
    along = {}
    for n in range(len(order) + 1):
        fresh = {}
        if n < len(order):
            both = blocks[order[n]][3]
            fresh["both"] = lax.ppermute(both if n else after(both, *hold), every, flip_pairs(1))
        if n:
            turn = order[n - 1]
            fresh["two"] = lax.ppermute(blocks[turn][2], every, flip_pairs(1))
            fresh["one"] = lax.ppermute(total_of(blocks[turn][1], boths[turn]).astype(bf16), every, flip_pairs(0))
        if n >= 2:
            turn = order[n - 2]
            terms = [blocks[turn][0], twos[turn], ones[turn]]
            if turn == 1:
                terms.append(along[2])
            fresh["along"] = lax.ppermute(total_of(*terms).astype(bf16), every, turn_pairs(1 if turn == 2 else turn))
        fresh["extra"] = extras[n]()
        if n == 1:
            fresh["extra"].append(input_grad)
        held = list(fresh)
        flat, tree = jax.tree.flatten([fresh[key] for key in held])
        fresh = dict(zip(held, jax.tree.unflatten(tree, lax.optimization_barrier(tuple(flat)))))
        if n == 1:
            input_grad = fresh["extra"].pop()
        extras[n + 1].given = fresh["extra"]
        if n < len(order):
            boths[order[n]] = fresh["both"]
        if n:
            ones[order[n - 1]], twos[order[n - 1]] = fresh["one"], fresh["two"]
        if n >= 2:
            along[order[n - 2]] = fresh["along"]
    whole = total_of(blocks[0][0], twos[0], ones[0], along[1], along[3])
    half = whole.shape[0] // 2
    keep = jnp.where(core == 0, whole[:half], whole[half:])
    give = jnp.where(core == 0, whole[half:], whole[:half])
    got = lax.ppermute(give, every, core_pairs())
    first, second = jnp.where(core == 0, keep, got), jnp.where(core == 0, got, keep)
    conv = jnp.concatenate([first[:conv_rows], second[:conv_rows]], axis=1)
    rows = (half - conv_rows) // 4

    def pieces(side):
        return [side[conv_rows + n * rows : conv_rows + (n + 1) * rows] for n in range(4)]

    left, right = pieces(first), pieces(second)
    lanes = left[3].shape[1] // 2
    heads = jnp.concatenate(left[:3] + [left[3][:, :lanes]] + right[:3] + [right[3][:, :lanes]], axis=1)
    return conv, heads, input_grad


class Summing:
    def __init__(self, every, steps, given=None):
        self.every, self.steps, self.given = every, steps, given

    def __call__(self):
        return [v if pairs is None else v + lax.ppermute(v, self.every, pairs) for v, pairs in zip(self.given, self.steps)]


def line_pairs(bit):
    return [((z * 2 + c) * 4 + s, ((z ^ bit) * 2 + c) * 4 + s) for z in range(4) for c in range(2) for s in range(4)]


def shards(
    features,
    conv_master,
    head_master,
    scale_master,
    join_master,
    affine_scale,
    affine_shift,
    head_cotangent,
    pool_cotangent,
    box_counts,
    proposals,
):
    images, rows, cols, depth = features.shape
    total = head_master.shape[1]
    strip = Strip(rows, cols)
    every = ("dp", "space")
    own_gain, own_join = scale_master.shape[0], join_master.shape[0]
    staged = lax.axis_size("dp") == 8 and lax.axis_size("space") == 4
    line, rank = lax.axis_index("dp"), lax.axis_index("space")
    place = jnp.stack([rank, jnp.int32(lax.axis_size("space")), box_counts[0], line // 2, line % 2]).astype(jnp.int32)
    spread = jnp.asarray(spread_matrix(strip), bf16)
    x = features.reshape(rows * cols, depth)
    if staged:
        packed = pack(strip, conv_master, head_master, scale_master, join_master, x, spread.T)
        conv_rows = conv_master.shape[0]

        def begin(edges, blocks):
            return prepare(strip, place, x, edges, blocks, LAYERS * 9 * depth // conv_rows)

        conv_full = conv_rows, *staged_gather(every, *packed, begin)
    else:
        conv_full = lax.all_gather(conv_master.astype(bf16), every, axis=0, tiled=True)
        head_full = lax.all_gather(head_master.astype(bf16), every, axis=0, tiled=True)
        small = jnp.concatenate([scale_master, join_master]).astype(bf16)
        small = lax.all_gather(small[None], every, axis=0, tiled=True).astype(f32)
        small = jnp.concatenate([small[:, :own_gain].reshape(1, total), small[:, own_gain:].reshape(SCALES, total)], axis=0)
        means = []
        for s in range(1, SCALES):
            at = strip.starts(0)[s] - strip.starts(0)[1]
            pick = spread[:, at : at + strip.sizes(0)[s]]
            means.append((mm(pick, x, TN) * (0.25**s)).astype(bf16))
        x = with_rows(strip, [x] + means, "space")
    results = forward(strip, place, x, conv_full, affine_scale, affine_shift, total)
    if staged:
        p0, p1, p2, a3, small, conv_full, head_full, acts = results
    else:
        p0, p1, p2, a3, acts = results
    pre = p0, p1, p2
    maps, pool, sums, dz, first, final, *halves = head(
        strip, place, a3, head_full, small, head_cotangent.reshape(rows * cols, total), pool_cotangent, proposals,
        spread, affine_scale, p2, staged,
    )
    block_rows = LAYERS * 9 * depth
    if staged:
        swap = functools.partial(lax.ppermute, axis_name=every, perm=core_pairs())
        *halves, dg_keep, dg_give = halves
        others = swap(acts)
        block_rows = packed[0].shape[0] * 2
    else:
        (head_grad,), halves = halves, []
        conv_rows = None
    grad = None
    for layer in (2, 1, 0):
        above, below = from_neighbour(final, 1, "space"), from_neighbour(first, -1, "space")
        if staged:
            keep, give = halves
            pair = [acts, others], [keep, swap(give)]
        else:
            pair = [acts], [dz]
        *grad, token = weight_grad(strip, layer, place, *pair, grad, block_rows, conv_rows)
        if layer == 2 and staged:
            grad = chip_head_grad(place, acts, others, dg_keep, swap(dg_give), grad, conv_rows)
        more = [affine_scale, pre[layer - 1]] if layer else [spread]
        dz, *edge = data_grad(strip, layer, place, dz, above, below, conv_full, token, more, staged)
        if layer:
            first, final, *halves = edge
    input_grad = dz
    me = line * lax.axis_size("space") + rank
    if staged:
        steps = [
            (core_pairs(), flip_pairs(0)),
            (flip_pairs(0), flip_pairs(1)),
            (flip_pairs(1), None),
            (line_pairs(1), None),
            (line_pairs(2), None),
        ]
        extras = [Summing(every, pairs) for pairs in steps] + [Summing(every, ())]
        extras[0].given = [sums, pool]
        conv_grad, head_grad, input_grad = staged_scatter(
            every, [grad[4 * n : 4 * n + 4] for n in range(4)], place[4], conv_rows, extras, input_grad, above, below
        )
        sums, pooled = extras[-1].given
    else:
        pooled = lax.psum(pool, "space")
        sums = lax.psum(sums, every)
        conv_grad = lax.psum_scatter(grad[0], every, scatter_dimension=0, tiled=True).astype(f32)
        head_grad = lax.psum_scatter(head_grad, every, scatter_dimension=0, tiled=True).astype(f32)
    return (
        maps.reshape(images, rows, cols, total),
        pooled / box_counts.astype(f32)[:, None],
        input_grad.reshape(images, rows, cols, depth),
        conv_grad,
        head_grad,
        lax.dynamic_slice_in_dim(sums[0], me * own_gain, own_gain),
        lax.dynamic_slice_in_dim(sums[1:].reshape(-1), me * own_join, own_join),
    )


def solution(mesh):
    return jax.shard_map(
        shards,
        mesh=mesh,
        in_specs=(
            P("dp", "space", None, None),
            P(("dp", "space"), None),
            P(("dp", "space"), None),
            P(("dp", "space")),
            P(("dp", "space")),
            P(),
            P(),
            P("dp", "space", None, None),
            P("dp", None),
            P("dp"),
            P("dp", None),
        ),
        out_specs=(
            P("dp", "space", None, None),
            P("dp", None),
            P("dp", "space", None, None),
            P(("dp", "space"), None),
            P(("dp", "space"), None),
            P(("dp", "space")),
            P(("dp", "space")),
        ),
        check_vma=False,
    )
```

```python
import functools

import jax
import jax.numpy as jnp
import numpy as np
from jax import lax
from jax.experimental import pallas as pl
from jax.experimental.pallas import tpu as pltpu
from jax.sharding import PartitionSpec as P

HEAD_CH = 256
TASK_HEADS = 7
SCALES = 3
LAYERS = 3
PAD = 8

epsilon = 1e-06
f32 = jnp.float32
bf16 = jnp.bfloat16
NN = (((1,), (0,)), ((), ()))
NT = (((1,), (1,)), ((), ()))
TN = (((0,), (0,)), ((), ()))


def mm(left, right, dims=NN):
    return lax.dot_general(left, right, dims, preferred_element_type=f32)


def split_mm(left, right):
    high = right.astype(bf16)
    low = (right - high.astype(f32)).astype(bf16)
    return mm(left, high) + mm(left, low)


class Strip:
    def __init__(self, rows, cols):
        self.rows = [rows >> s for s in range(SCALES)]
        self.cols = [cols >> s for s in range(SCALES)]

    def sizes(self, halo):
        return [(r + 2 * halo) * c for r, c in zip(self.rows, self.cols)]

    def starts(self, halo):
        sizes = self.sizes(halo)
        return [sum(sizes[:s]) for s in range(SCALES)]

    def total(self, halo):
        return sum(self.sizes(halo))

    def own(self, halo):
        return [st + halo * c for st, c in zip(self.starts(halo), self.cols)]


def spread_matrix(strip):
    rows, cols = strip.rows[0], strip.cols[0]
    parts = []
    for s in range(1, SCALES):
        mat = np.zeros((rows * cols, strip.rows[s] * strip.cols[s]), np.float32)
        for r in range(rows):
            for c in range(cols):
                mat[r * cols + c, (r >> s) * strip.cols[s] + (c >> s)] = 1.0
        parts.append(mat)
    return np.concatenate(parts, axis=1)


def column_of(strip, scale, count):
    return lax.broadcasted_iota(jnp.int32, (count, 1), 0) % strip.cols[scale]


def shifted_copies(strip, halo, act, wide, depth):
    for s in range(SCALES):
        start, count, cols = strip.starts(halo)[s], strip.sizes(halo)[s], strip.cols[s]
        column = column_of(strip, s, count)
        for k in range(3):
            rows = act[PAD + start + k - 1 : PAD + start + k - 1 + count, :]
            if k == 0:
                rows = jnp.where(column == 0, 0.0, rows)
            if k == 2:
                rows = jnp.where(column == cols - 1, 0.0, rows)
            wide[start : start + count, k * depth : (k + 1) * depth] = rows.astype(bf16)


def patches(strip, halo, wide, cells, depth, flip=False, base=0):
    for s in range(SCALES):
        cols = strip.cols[s]
        count = strip.sizes(halo)[s]
        source, target = strip.starts(halo + 1)[s], strip.starts(halo)[s]
        for ky in range(3):
            first = source + (2 - ky if flip else ky) * cols
            for kx in range(3):
                col = (2 - kx if flip else kx) * depth
                tap = 3 * ky + kx
                cells[base + target : base + target + count, tap * depth : (tap + 1) * depth] = wide[
                    first : first + count, col : col + depth
                ]


FLIPS = ((1, 2), (2, 1))
TURNS = (0, 1, 3, 2)
GROUPS = (((0, 1, 2, 3),),) * 3 + (((0, 1, 2), (3,)),)
ITEMS = tuple(
    item
    for n in range(4)
    for item in [(n, True, (part,)) for part in range(4)] + [(n, False, group) for group in GROUPS[n]]
)


def across(place, part, core):
    rank = place[0]
    for bit in range(2):
        if part >> bit & 1:
            rank = rank ^ jnp.where(core == 0, FLIPS[0][bit], FLIPS[1][bit])
    return rank


def load_blocks(conv_rows, place, refs, weights, head_w, sem):
    depth = weights.shape[1]
    pieces, rows = head_w.shape[:2]
    head_rows = rows * conv_rows // weights.shape[0]
    layer_rows = weights.shape[0] // LAYERS
    last = [-(-layer_rows * (n + 1) // conv_rows) for n in range(LAYERS)]
    blocks = []
    for (n, own, parts), ref in zip(ITEMS, refs):
        core = place[4] if own else 1 - place[4]
        z = (place[3] + 4 - TURNS[n]) % 4
        for at, part in enumerate(parts):
            block = ref if len(parts) == 1 else ref.at[at]
            blocks.append((block, (z * 2 + core) * 4 + across(place, part, core)))
    for layer in range(LAYERS):
        for block, k in blocks:
            copy = pltpu.make_async_copy(
                block.at[pl.ds(0, conv_rows), :],
                weights.at[pl.ds(pl.multiple_of(k * conv_rows, 16), conv_rows), :],
                sem.at[layer],
            )
            inside = k < last[layer]
            if layer:
                inside = inside & (k >= last[layer - 1])
            pl.when(inside)(copy.start)
    for block, k in blocks:
        pltpu.make_async_copy(
            block.at[pl.ds(conv_rows, pieces * head_rows), :].reshape(pieces, head_rows, depth),
            head_w.at[:, pl.ds(pl.multiple_of(k * head_rows, 16), head_rows), :],
            sem.at[LAYERS],
        ).start()
    waits = []
    for first, stop in zip([0] + last, last):
        rows = weights.at[pl.ds(first * conv_rows, (stop - first) * conv_rows), :]
        waits.append(pltpu.make_async_copy(rows, rows, sem.at[len(waits)]))
    return waits + [pltpu.make_async_copy(head_w, head_w, sem.at[LAYERS])]


def prepare_kernel(strip, depth, place, x_ref, above_ref, below_ref, *refs):
    blocks, (cells, acts_ref, token, strips, act, wide, x_sem) = refs[:4], refs[4:]
    strips[...] = jnp.zeros(strips.shape, bf16)
    coarse = strips.shape[1]
    fetches = []
    for part in range(4):
        copy = pltpu.make_async_copy(
            blocks[part].at[pl.ds(blocks[part].shape[0] - coarse, coarse), :],
            strips.at[3 + across(place, part, place[4])],
            x_sem.at[part],
        )
        copy.start()
        fetches.append(copy)
    token[...] = jnp.zeros(token.shape, f32)
    at = PAD
    for ref in (above_ref, x_ref, below_ref):
        act[at : at + ref.shape[0], :] = ref[...].astype(f32)
        at += ref.shape[0]
    for copy in fetches:
        copy.wait()
    for s in range(1, SCALES):
        rows, cols = strip.rows[s], strip.cols[s]
        first = strip.starts(0)[s] - strip.starts(0)[1]
        for row in range(-3, rows + 3):
            source = strips[place[0] + 3 + row // rows, first + row % rows * cols : first + (row % rows + 1) * cols, :]
            act[at : at + cols, :] = source.astype(f32)
            at += cols
    first_patches(strip, depth, act, wide, cells, acts_ref)


def first_patches(strip, depth, act, wide, cells, acts_ref):
    for s in range(SCALES):
        start, size = strip.starts(1)[s], strip.sizes(1)[s]
        first = PAD + strip.starts(3)[s] + 2 * strip.cols[s]
        acts_ref[start : start + size, :] = act[first : first + size, :].astype(bf16)
    shifted_copies(strip, LAYERS, act, wide, depth)
    patches(strip, LAYERS - 1, wide, cells, depth)


def pack_kernel(strip, conv_ref, head_ref, gain_ref, join_ref, x_ref, gather_ref, own_ref, wide_ref, top_ref, bottom_ref):
    depth = conv_ref.shape[1]
    at = conv_ref.shape[0]
    rows, head_cols = head_ref.shape
    for ref in (own_ref, wide_ref):
        ref[:at, :] = conv_ref[...].astype(bf16)
    for first in range(0, head_cols, depth):
        width = min(depth, head_cols - first)
        piece = head_ref[:, first : first + width]
        if width < depth:
            small = jnp.concatenate([gain_ref[...], join_ref[...]], axis=1)
            small = jnp.concatenate([small, jnp.zeros((1, depth - width - small.shape[1]), f32)], axis=1)
            row = lax.broadcasted_iota(jnp.int32, (rows, depth - width), 0)
            small = jnp.where(row == 0, jnp.broadcast_to(small, (rows, depth - width)), 0.0)
            piece = jnp.concatenate([piece, small], axis=1)
        for ref in (own_ref, wide_ref):
            ref[at : at + rows, :] = piece.astype(bf16)
        at += rows
    x = x_ref[...]
    sums = mm(gather_ref[...], x)
    for s in range(1, SCALES):
        first = strip.starts(0)[s] - strip.starts(0)[1]
        size = strip.sizes(0)[s]
        wide_ref[at : at + size, :] = (sums[first : first + size] * (0.25**s)).astype(bf16)
        at += size
    edge = 3 * strip.cols[0]
    top_ref[...] = x_ref[:edge, :]
    bottom_ref[...] = x_ref[x.shape[0] - edge :, :]


def forward_kernel(strip, depth, staged, place, scale_ref, shift_ref, *refs):
    taps = 9 * depth
    halos = [LAYERS - 1 - layer for layer in range(LAYERS)]
    if staged:
        conv_rows, head_cols = staged
        expand_hbm, owner_ref, first_cells, *refs = refs
        blocks, refs = refs[: len(ITEMS)], refs[len(ITEMS) :]
        first_acts, refs = refs[0], refs[1:]
        p_refs, refs = refs[:3], refs[3:]
        a3_ref, small_ref, weights, head_ref, acts_ref, act, wide, cells, expand, sem = refs
        loads = load_blocks(conv_rows, place, blocks, weights, head_ref, sem)
        expand_load = pltpu.make_async_copy(expand_hbm, expand, sem.at[LAYERS + 1])
        expand_load.start()
        acts_ref[: first_acts.shape[0], :] = first_acts[...]
    else:
        x_ref, w_hbm, *refs = refs
        p_refs, refs = refs[:3], refs[3:]
        a3_ref, acts_ref, weights, act, wide, cells, sem = refs
        load = pltpu.make_async_copy(w_hbm, weights, sem.at[0])
        load.start()
        act[PAD : PAD + strip.total(3), :] = x_ref[...].astype(f32)
        first_cells = cells
        first_patches(strip, depth, act, wide, cells, acts_ref)
        load.wait()
    here, ranks = place[0], place[1]
    flat = strip.starts(0)
    for layer, halo in enumerate(halos):
        count = strip.total(halo)
        if layer:
            shifted_copies(strip, halo + 1, act, wide, depth)
            patches(strip, halo, wide, cells, depth)
        used = cells if layer else first_cells
        own = strip.own(halo)
        if staged:
            loads[layer].wait()
        for half in range(depth // 256):
            lanes = slice(half * 256, (half + 1) * 256)
            z = mm(used[:count, :], weights[layer * taps : (layer + 1) * taps, lanes])
            p = z * scale_ref[layer : layer + 1, lanes] + shift_ref[layer : layer + 1, lanes]
            a = (p / (1.0 + jnp.exp(-p))).astype(bf16)
            for s in range(SCALES):
                size = strip.sizes(0)[s]
                p_refs[layer][flat[s] : flat[s] + size, lanes] = p[own[s] : own[s] + size]
            if layer == LAYERS - 1:
                a3_ref[:, lanes] = a
                acts_ref[LAYERS * strip.total(1) :, lanes] = a
            else:
                for s in range(SCALES):
                    start, size = strip.starts(halo)[s], strip.sizes(halo)[s]
                    row = lax.broadcasted_iota(jnp.int32, (size, 1), 0) // strip.cols[s]
                    row = row + here * strip.rows[s] - halo
                    inside = (row >= 0) & (row < ranks * strip.rows[s])
                    kept = jnp.where(inside, a[start : start + size].astype(f32), 0.0)
                    act[PAD + start : PAD + start + size, lanes] = kept
                    edge = (halo - 1) * strip.cols[s]
                    first, size = (layer + 1) * strip.total(1) + strip.starts(1)[s], strip.sizes(1)[s]
                    acts_ref[first : first + size, lanes] = kept[edge : edge + size].astype(bf16)
    if staged:
        loads[LAYERS].wait()
        expand_load.wait()
        owners, spare = owner_ref.shape[0], expand.shape[0]
        pieces, depth_rows = head_ref.shape[:2]
        row = lax.broadcasted_iota(jnp.int32, (owners, depth_rows), 0)
        col = lax.broadcasted_iota(jnp.int32, (owners, depth_rows), 1)
        pick = jnp.where(col == row * (depth_rows // owners), 1.0, 0.0).astype(bf16)
        picked = mm(pick, head_ref[pieces - 1, :, depth - spare :]).astype(bf16)
        for n in range(1 + SCALES):
            cols = slice(n * head_cols, (n + 1) * head_cols)
            spread = mm(picked, expand[:, cols]) * owner_ref[:, cols].astype(f32)
            small_ref[n : n + 1, :] = jnp.sum(spread, axis=0, keepdims=True)


def slope(p):
    sigma = 1.0 / (1.0 + jnp.exp(-p))
    return sigma * (1.0 + p * (1.0 - sigma))


def head_kernel(
    strip, split, place, a3_ref, w_ref, small_ref, cot_ref, pool_cot_ref, where_ref, spread_ref, gather_ref,
    scale_ref, p2_ref, maps_ref, pool_ref, sums_ref, *refs,
):
    if split:
        *grads, keep_ref, give_ref, dg_all = refs
    else:
        *grads, w_grad_ref, dg_all = refs
    fine = strip.sizes(0)[0]
    starts, sizes = strip.starts(0), strip.sizes(0)
    parts = [slice(starts[s], starts[s] + sizes[s]) for s in range(SCALES)]
    slots = where_ref.shape[1]
    pixel = lax.broadcasted_iota(jnp.int32, (fine, slots), 0) + place[0] * fine
    slot = lax.broadcasted_iota(jnp.int32, (fine, slots), 1)
    hits = jnp.where((where_ref[...] == pixel) & (slot < place[2]), 1.0, 0.0)
    hits = jnp.sum(hits, axis=-1, keepdims=True)
    share = pool_cot_ref[...] / place[2].astype(f32)
    heads = maps_ref.shape[1] // HEAD_CH
    depth = a3_ref.shape[1]
    per = depth // HEAD_CH
    da3 = None
    for head in range(heads):
        lanes = slice(head * HEAD_CH, (head + 1) * HEAD_CH)
        if split:
            weight = w_ref[head // per, :, head % per * HEAD_CH : (head % per + 1) * HEAD_CH]
        else:
            weight = w_ref[:, lanes]
        g = mm(a3_ref[...], weight)
        inverse = lax.rsqrt(jnp.sum(g * g, axis=-1, keepdims=True) + epsilon)
        unit = g * inverse
        gain = small_ref[0:1, lanes]
        join = [small_ref[1 + s : 2 + s, lanes] for s in range(SCALES)]
        normed = unit * gain
        coarse = jnp.concatenate([normed[parts[s]] * join[s] for s in range(1, SCALES)], axis=0)
        joined = normed[:fine] * join[0] + split_mm(spread_ref[...], coarse)
        maps_ref[:, lanes] = joined.astype(bf16)
        fused = cot_ref[:, lanes]
        if head == 0:
            pool_ref[...] = jnp.sum(joined * hits, axis=0, keepdims=True)
            fused = fused.astype(f32) + hits * share
            down_coarse = split_mm(gather_ref[...], fused)
        else:
            down_coarse = mm(gather_ref[...], fused)
        down = jnp.concatenate([fused.astype(f32), down_coarse], axis=0)
        product = down * normed
        scaled = []
        for s in range(SCALES):
            sums_ref[s + 1 : s + 2, lanes] = jnp.sum(product[parts[s]], axis=0, keepdims=True)
            scaled.append(down[parts[s]] * join[s])
        dn = jnp.concatenate(scaled, axis=0)
        sums_ref[0:1, lanes] = jnp.sum(dn * unit, axis=0, keepdims=True)
        du = dn * gain
        dg = (inverse * (du - unit * jnp.sum(du * unit, axis=-1, keepdims=True))).astype(bf16)
        dg_all[head] = dg
        if not split:
            w_grad_ref[:, lanes] = mm(a3_ref[...], dg, TN).astype(bf16)
        part = mm(dg, weight, NT)
        da3 = part if da3 is None else da3 + part
    layer = LAYERS - 1
    dz = da3 * scale_ref[layer : layer + 1, :] * slope(p2_ref[...])
    emit_grad(strip, place, dz.astype(bf16), *grads)
    if split:
        width = HEAD_CH
        first = place[4] == 0
        half = heads * width // 2
        for start in range(0, half, width // 2):
            left = dg_all[start // width, :, start % width : start % width + width // 2]
            at = half + start
            right = dg_all[at // width, :, at % width : at % width + width // 2]
            keep_ref[:, start : start + width // 2] = jnp.where(first, left, right)
            give_ref[:, start : start + width // 2] = jnp.where(first, right, left)


def emit_grad(strip, place, dz, dz_ref, first_ref, last_ref, keep_ref=None, give_ref=None):
    dz_ref[...] = dz
    edge = 0
    for start, size, cols in zip(strip.starts(0), strip.sizes(0), strip.cols):
        first_ref[edge : edge + cols, :] = dz[start : start + cols]
        last_ref[edge : edge + cols, :] = dz[start + size - cols : start + size]
        edge += cols
    if keep_ref is not None:
        middle = dz.shape[1] // 2
        left, right = dz[:, :middle], dz[:, middle:]
        first = place[4] == 0
        keep_ref[...] = jnp.where(first, left, right)
        give_ref[...] = jnp.where(first, right, left)


def store_blocks(place, pieces, block_refs, sem):
    for turn in range(4):
        for part in range(4):
            out = block_refs[4 * turn + part]
            z = (place[3] + turn) % 4
            rank = across(place, part, place[4])
            for core in range(2):
                k = (z * 2 + core) * 4 + rank
                base = core * (out.shape[0] // 2)
                for condition, source, row in pieces(k):
                    copy = pltpu.make_async_copy(source, out.at[pl.ds(base + row, source.shape[0]), :], sem)
                    if condition is None:
                        copy.start()
                    else:
                        pl.when(condition)(copy.start)


def weight_grad_kernel(strip, depth, layer, images, conv_rows, place, *refs):
    acts, grads = refs[:images], refs[images : 2 * images]
    *outs, token, act, wide, cells, dz, result, sem = refs[2 * images :]
    own, count = strip.total(0), strip.total(1)
    for n in range(images):
        act[PAD : PAD + count, :] = acts[n][layer * count : (layer + 1) * count, :].astype(f32)
        shifted_copies(strip, 1, act, wide, depth)
        patches(strip, 0, wide, cells, depth, base=n * own)
        dz[n * own : (n + 1) * own, :] = grads[n][...]
    for tap in range(9):
        lanes = slice(tap * depth, (tap + 1) * depth)
        result[lanes, :] = mm(cells[:, lanes], dz[...], TN).astype(bf16)
    rows = 9 * depth
    first_row, stop_row = layer * rows, (layer + 1) * rows
    token[...] = jnp.zeros(token.shape, f32)
    if conv_rows is None:
        copy = pltpu.make_async_copy(result, outs[-1].at[pl.ds(first_row, rows), :], sem)
        copy.start()
        copy.wait()
        return

    def pieces(k):
        out = []
        inside = (k * conv_rows >= first_row) & ((k + 1) * conv_rows <= stop_row)
        start = jnp.where(inside, k * conv_rows - first_row, 0)
        out.append((inside, result.at[pl.ds(pl.multiple_of(start, 16), conv_rows), :], 0))
        if first_row % conv_rows:
            size = conv_rows - first_row % conv_rows
            out.append((k == first_row // conv_rows, result.at[pl.ds(0, size), :], conv_rows - size))
        if stop_row % conv_rows:
            size = stop_row % conv_rows
            out.append((k == stop_row // conv_rows, result.at[pl.ds(rows - size, size), :], 0))
        return out

    store_blocks(place, pieces, outs[-16:], sem)
    pltpu.make_async_copy(result, result, sem).wait()


def chip_head_grad_kernel(conv_rows, place, a3_ref, other_ref, keep_ref, got_ref, sums_ref, pool_ref, owner_ref, expand, *refs):
    refs = refs[-(16 + 4) :]
    outs, (a3, dg, result, out_sem) = refs[:16], refs[16:]
    own = keep_ref.shape[0]
    for n, ref in enumerate((a3_ref, other_ref)):
        pltpu.make_async_copy(ref.at[pl.ds(ref.shape[0] - own, own), :], a3.at[pl.ds(n * own, own), :], out_sem).start()
    pltpu.make_async_copy(a3, a3, out_sem).wait()
    dg[:own, :] = keep_ref[...]
    dg[own:, :] = got_ref[...]
    width = result.shape[2]
    cols = dg.shape[1]
    for piece in range(result.shape[0]):
        stop = min(cols, (piece + 1) * width)
        lanes = slice(piece * width, stop)
        result[piece, :, : stop - piece * width] = mm(a3[...], dg[:, lanes], TN).astype(bf16)
    owners, depth_rows, spare = owner_ref.shape[0], result.shape[1], width - cols % width
    small = None
    for n in range(sums_ref.shape[0]):
        lanes = slice(n * sums_ref.shape[1], (n + 1) * sums_ref.shape[1])
        each = (sums_ref[n : n + 1, :] * owner_ref[:, lanes].astype(f32)).astype(bf16)
        term = mm(each, expand[:, lanes], NT)
        small = term if small is None else small + term
    row = lax.broadcasted_iota(jnp.int32, (depth_rows, owners), 0)
    col = lax.broadcasted_iota(jnp.int32, (depth_rows, owners), 1)
    tail = None
    for n in range(small.shape[1] // spare):
        pick = jnp.where(row == col * (depth_rows // owners) + n, 1.0, 0.0).astype(bf16)
        term = mm(pick, small[:, n * spare : (n + 1) * spare].astype(bf16))
        tail = term if tail is None else tail + term
    row = lax.broadcasted_iota(jnp.int32, (depth_rows, spare), 0)
    each = depth_rows // owners
    mine = row // (each * 4) == place[3] * 2 + place[4]
    for n in range(2):
        here = mine & (row % each == 2 + 2 * place[0] + n)
        tail = jnp.where(here, pool_ref[:, n * spare : (n + 1) * spare], tail)
    result[result.shape[0] - 1, :, cols % width :] = tail.astype(bf16)
    rows = (outs[0].shape[0] // 2 - conv_rows) // result.shape[0]

    def pieces(k):
        return [
            (None, result.at[piece, pl.ds(pl.multiple_of(k * rows, 16), rows), :], conv_rows + piece * rows)
            for piece in range(result.shape[0])
        ]

    store_blocks(place, pieces, outs, out_sem)
    pltpu.make_async_copy(result, result, out_sem).wait()


def halves_kernel(place, *refs):
    *terms, keep_ref, give_ref = refs
    whole = total_of(*[t[...] for t in terms])
    half = keep_ref.shape[0]
    first = place[4] == 0
    keep_ref[...] = jnp.where(first, whole[:half], whole[half:])
    give_ref[...] = jnp.where(first, whole[half:], whole[:half])


def deliver_kernel(place, keep_ref, got_ref, conv_ref, head_ref, gain_ref, join_ref, pool_ref):
    first = place[4] == 0
    keep, got = keep_ref[...], got_ref[...]
    width = keep.shape[1]
    rows = head_ref.shape[0]
    half = head_ref.shape[1] // 2
    for n, side in enumerate((jnp.where(first, keep, got), jnp.where(first, got, keep))):
        conv_ref[:, n * width : (n + 1) * width] = side[: conv_ref.shape[0]]
        at = conv_ref.shape[0]
        for col in range(0, half, width):
            size = min(width, half - col)
            head_ref[:, n * half + col : n * half + col + size] = side[at : at + rows, :size]
            at += rows
    lanes = half % width
    small = (keep + got)[at - rows : at, lanes:]
    pooled = None
    for s in range(4):
        term = jnp.concatenate([small[2 + 2 * s : 3 + 2 * s], small[3 + 2 * s : 4 + 2 * s]], axis=1)
        pooled = term if pooled is None else pooled + term
    pool_ref[...] = pooled / place[2].astype(f32)
    small = jnp.concatenate([small[n : n + 1] for n in range(2)], axis=1)
    gains = gain_ref.shape[1]
    gain_ref[...] = small[:, :gains]
    join_ref[...] = small[:, gains : gains + join_ref.shape[1]]


def data_grad_kernel(
    strip, depth, layer, place, dz_ref, above_ref, below_ref, w_ref, _, *refs
):
    refs, (act, wide, cells) = refs[:-3], refs[-3:]
    last = layer == 0
    if last:
        spread_ref, out_ref = refs
    else:
        scale_ref, p_ref, *outs = refs
    edge = 0
    for s in range(SCALES):
        start, size, cols = strip.starts(1)[s], strip.sizes(0)[s], strip.cols[s]
        flat = strip.starts(0)[s]
        act[PAD + start : PAD + start + cols, :] = above_ref[edge : edge + cols, :].astype(f32)
        act[PAD + start + cols : PAD + start + cols + size, :] = dz_ref[flat : flat + size, :].astype(f32)
        act[PAD + start + cols + size : PAD + start + 2 * cols + size, :] = below_ref[edge : edge + cols, :].astype(f32)
        edge += cols
    shifted_copies(strip, 1, act, wide, depth)
    patches(strip, 0, wide, cells, depth, flip=True)
    base = layer * 9 * depth
    value = None
    for tap in range(9):
        term = mm(
            cells[:, tap * depth : (tap + 1) * depth], w_ref[base + tap * depth : base + (tap + 1) * depth, :], NT
        )
        value = term if value is None else value + term
    if last:
        fine = strip.sizes(0)[0]
        coarse = jnp.concatenate(
            [
                value[st : st + size] * (0.25**s)
                for s, (st, size) in enumerate(zip(strip.starts(0), strip.sizes(0)))
                if s
            ],
            axis=0,
        )
        out_ref[...] = value[:fine] + split_mm(spread_ref[...], coarse)
    else:
        dz = value * scale_ref[layer - 1 : layer, :] * slope(p_ref[...])
        emit_grad(strip, place, dz.astype(bf16), *outs)


def vmem(shape=None, index=None):
    if shape is None:
        return pl.BlockSpec(memory_space=pltpu.VMEM)
    return pl.BlockSpec(shape, index)


SMEM = pl.BlockSpec(memory_space=pltpu.SMEM)
ANY = pl.BlockSpec(memory_space=pl.ANY)


def params(mebibytes):
    return pltpu.CompilerParams(vmem_limit_bytes=mebibytes << 20)


def small_layout(owners, cols, spare):
    gains = cols // owners
    expand = np.zeros((spare, (1 + SCALES) * cols), np.float32)
    owner = np.zeros((owners, (1 + SCALES) * cols), np.float32)
    for n in range((1 + SCALES) * cols):
        size = gains if n < cols else SCALES * gains
        at = n if n < cols else n - cols
        expand[at % size + (0 if n < cols else gains), n] = 1.0
        owner[at // size, n] = 1.0
    return jnp.asarray(expand, bf16), jnp.asarray(owner, bf16)


def pack(strip, conv, head_w, gain, join, x, gather):
    depth = conv.shape[1]
    rows = conv.shape[0] + head_w.shape[0] * -(-head_w.shape[1] // depth)
    edge = 3 * strip.cols[0]
    return pl.pallas_call(
        functools.partial(pack_kernel, strip),
        name="pack",
        out_shape=[jax.ShapeDtypeStruct((n, depth), bf16) for n in (rows, rows + gather.shape[0], edge, edge)],
        in_specs=[vmem()] * 6,
        out_specs=[vmem()] * 4,
        compiler_params=params(60),
    )(conv, head_w, gain[None], join[None], x, gather)


def on_chip(values):
    return [pltpu.with_memory_space_constraint(v, pltpu.MemorySpace.VMEM) for v in values]


def off_chip(values):
    return [pltpu.with_memory_space_constraint(v, pltpu.MemorySpace.HBM) for v in values]


def forward_scratch(strip, depth, halo):
    return [
        pltpu.VMEM((strip.total(halo) + 2 * PAD, depth), f32),
        pltpu.VMEM((strip.total(halo), 3 * depth), bf16),
    ]


def prepare(strip, place, x, edges, blocks, owners):
    depth = x.shape[1]
    coarse = strip.total(0) - strip.sizes(0)[0]
    return pl.pallas_call(
        functools.partial(prepare_kernel, strip, depth),
        name="prepare",
        out_shape=[
            pltpu.VMEM((strip.total(LAYERS - 1), 9 * depth), bf16),
            pltpu.VMEM((strip.total(1), depth), bf16),
            jax.ShapeDtypeStruct((8, 128), f32),
        ],
        in_specs=[SMEM] + [vmem()] * 3 + [ANY] * len(blocks),
        out_specs=[vmem()] * 3,
        scratch_shapes=[pltpu.VMEM((6 + owners // 8, coarse, depth), bf16)]
        + forward_scratch(strip, depth, LAYERS)
        + [pltpu.SemaphoreType.DMA((4,))],
        compiler_params=params(10),
    )(place, x, *edges, *off_chip(blocks))


def forward(strip, place, x, conv, scale, shift, head_cols):
    depth = scale.shape[1]
    own = strip.total(0)
    rows = LAYERS * 9 * depth
    acts = (LAYERS * strip.total(1) + own, depth)
    staged = isinstance(conv, tuple)
    cells = pltpu.VMEM((strip.total(1 if staged else LAYERS - 1), 9 * depth), bf16)
    if staged:
        conv_rows, prepared, blocks = conv
        expand, owner = small_layout(rows // conv_rows, head_cols, -head_cols % depth)
        first_cells, first_acts = on_chip(prepared)
        inputs = [expand, owner, first_cells, *off_chip(blocks), first_acts]
        in_specs = [ANY, vmem(), vmem()] + [ANY] * len(blocks) + [vmem()]
        outs = [pltpu.VMEM((own, depth), f32)] * 3 + [
            pltpu.VMEM((own, depth), bf16),
            pltpu.VMEM((1 + SCALES, head_cols), f32),
            pltpu.VMEM((rows, depth), bf16),
            pltpu.VMEM((-(-head_cols // depth), depth, depth), bf16),
            pltpu.VMEM(acts, bf16),
        ]
        scratch = forward_scratch(strip, depth, LAYERS - 1)
        scratch += [cells, pltpu.VMEM(expand.shape, bf16), pltpu.SemaphoreType.DMA((LAYERS + 2,))]
    else:
        inputs, in_specs = [x, conv], [vmem(), ANY]
        outs = [jax.ShapeDtypeStruct((own, depth), f32)] * 3
        outs += [jax.ShapeDtypeStruct(shape, bf16) for shape in ((own, depth), acts)]
        scratch = [pltpu.VMEM((rows, depth), bf16)] + forward_scratch(strip, depth, LAYERS)
        scratch += [cells, pltpu.SemaphoreType.DMA((1,))]
    return pl.pallas_call(
        functools.partial(forward_kernel, strip, depth, (conv_rows, head_cols) if staged else None),
        name="forward",
        out_shape=outs,
        in_specs=[SMEM, vmem(), vmem()] + in_specs,
        out_specs=[vmem()] * len(outs),
        scratch_shapes=scratch,
        compiler_params=params(28 if staged else 54),
    )(place, scale, shift, *inputs)


def head(strip, place, a3, weight, small, cot, pool_cot, where, spread, scale, p2, split):
    own, depth = a3.shape
    total = small.shape[1]
    fine = strip.sizes(0)[0]
    edge = sum(strip.cols)
    outs = [
        jax.ShapeDtypeStruct((fine, total), bf16),
        jax.ShapeDtypeStruct((1, HEAD_CH), f32),
        jax.ShapeDtypeStruct((1 + SCALES, total), f32),
    ]
    outs += [jax.ShapeDtypeStruct((n, depth), bf16) for n in (own, edge, edge)]
    if split:
        outs += [jax.ShapeDtypeStruct((own, n // 2), bf16) for n in (depth, depth, total, total)]
    else:
        outs += [jax.ShapeDtypeStruct((depth, total), bf16)]
    return pl.pallas_call(
        functools.partial(head_kernel, strip, split),
        name="heads",
        out_shape=outs,
        in_specs=[SMEM] + [vmem()] * 10,
        out_specs=[vmem()] * len(outs),
        scratch_shapes=[pltpu.VMEM((total // HEAD_CH, own, HEAD_CH), bf16)],
        compiler_params=params(24),
    )(place, a3, weight, small, cot, pool_cot, where, spread, spread.T, scale, p2)


def weight_grad(strip, layer, place, acts, grads, into, rows, conv_rows):
    own, half = grads[0].shape
    depth = acts[0].shape[1]
    images = len(acts)
    count_here = strip.total(1)
    into = into or []
    count = 1 if conv_rows is None else 16
    return pl.pallas_call(
        functools.partial(weight_grad_kernel, strip, depth, layer, images, conv_rows),
        name="weight_grad",
        out_shape=[pltpu.HBM((rows, half), bf16)] * count + [jax.ShapeDtypeStruct((8, 128), f32)],
        in_specs=[SMEM] + [vmem()] * (2 * images) + [ANY] * len(into),
        out_specs=[ANY] * count + [vmem()],
        scratch_shapes=[
            pltpu.VMEM((count_here + 2 * PAD, depth), f32),
            pltpu.VMEM((count_here, 3 * depth), bf16),
            pltpu.VMEM((images * own, 9 * depth), bf16),
            pltpu.VMEM((images * own, half), bf16),
            pltpu.VMEM((9 * depth, half), bf16),
            pltpu.SemaphoreType.DMA,
        ],
        input_output_aliases={1 + 2 * images + n: n for n in range(len(into))},
        compiler_params=params(22),
    )(place, *acts, *grads, *off_chip(into))


def chip_head_grad(place, a3, other, keep, got, sums, pool, blocks, conv_rows):
    own, depth = keep.shape[0], a3.shape[1]
    half = blocks[0].shape[1]
    expand, owner = small_layout(LAYERS * 9 * depth // conv_rows, sums.shape[1], -sums.shape[1] % depth)
    pieces = -(-keep.shape[1] // half)
    return pl.pallas_call(
        functools.partial(chip_head_grad_kernel, conv_rows),
        name="chip_head_grad",
        out_shape=[pltpu.HBM(b.shape, bf16) for b in blocks],
        in_specs=[SMEM, ANY, ANY] + [vmem()] * 6 + [ANY] * 16,
        out_specs=[ANY] * 16,
        scratch_shapes=[
            pltpu.VMEM((2 * own, depth), bf16),
            pltpu.VMEM((2 * own, keep.shape[1]), bf16),
            pltpu.VMEM((pieces, depth, half), bf16),
            pltpu.SemaphoreType.DMA,
        ],
        input_output_aliases={9 + n: n for n in range(16)},
        compiler_params=params(14),
    )(place, a3, other, keep, got, sums, pool, owner, expand, *off_chip(blocks))


def data_grad(strip, layer, place, dz, above, below, conv, token, others, split):
    if split:
        conv = pltpu.with_memory_space_constraint(conv, pltpu.MemorySpace.VMEM)
    own, depth = dz.shape
    last = layer == 0
    edge = sum(strip.cols)

    if last:
        outs = [jax.ShapeDtypeStruct((strip.sizes(0)[0], depth), f32)]
    else:
        outs = [jax.ShapeDtypeStruct((n, depth), bf16) for n in (own, edge, edge)]
        outs += [jax.ShapeDtypeStruct((own, depth // 2), bf16)] * (2 * split)
    return pl.pallas_call(
        functools.partial(data_grad_kernel, strip, depth, layer),
        name="data_grad",
        out_shape=outs,
        in_specs=[SMEM] + [vmem()] * 4 + [ANY] + [vmem()] * len(others),
        out_specs=[vmem()] * len(outs),
        scratch_shapes=[
            pltpu.VMEM((strip.total(1) + 2 * PAD, depth), f32),
            pltpu.VMEM((strip.total(1), 3 * depth), bf16),
            pltpu.VMEM((own, 9 * depth), bf16),
        ],
        compiler_params=params(14 if split else 32),
    )(place, dz, above, below, conv, token, *others)


def halves(place, *terms):
    rows, width = terms[0].shape
    return pl.pallas_call(
        halves_kernel,
        name="halves",
        out_shape=[jax.ShapeDtypeStruct((rows // 2, width), f32)] * 2,
        in_specs=[SMEM] + [vmem()] * len(terms),
        out_specs=[vmem()] * 2,
        compiler_params=params(16),
    )(place, *terms)


def deliver(place, keep, got, conv_rows, head_cols, gains):
    width = keep.shape[1]
    head_rows = (keep.shape[0] - conv_rows) // -(-(head_cols // 2) // width)
    return pl.pallas_call(
        deliver_kernel,
        name="deliver",
        out_shape=[
            jax.ShapeDtypeStruct((conv_rows, 2 * width), f32),
            jax.ShapeDtypeStruct((head_rows, head_cols), f32),
            jax.ShapeDtypeStruct((1, gains), f32),
            jax.ShapeDtypeStruct((1, SCALES * gains), f32),
            jax.ShapeDtypeStruct((1, HEAD_CH), f32),
        ],
        in_specs=[SMEM] + [vmem()] * 2,
        out_specs=[vmem()] * 5,
        compiler_params=params(8),
    )(place, keep, got)


def from_neighbour(cells, distance, axis):
    count = lax.axis_size(axis)
    pairs = [(i, i + distance) for i in range(count) if 0 <= i + distance < count]
    return lax.ppermute(cells, axis, pairs)


def with_rows(strip, levels, axis):
    above = [[] for _ in levels]
    below = [[] for _ in levels]
    left = [3] * len(levels)
    distance = 1
    while max(left) > 0:
        take = [min(n, r) for n, r in zip(left, strip.rows)]
        tails = [v[v.shape[0] - t * c :] for v, t, c in zip(levels, take, strip.cols) if t]
        heads = [v[: t * c] for v, t, c in zip(levels, take, strip.cols) if t]
        got_tail = from_neighbour(jnp.concatenate(tails, axis=0), distance, axis)
        got_head = from_neighbour(jnp.concatenate(heads, axis=0), -distance, axis)
        at = 0
        for s, (t, c) in enumerate(zip(take, strip.cols)):
            if t:
                above[s].insert(0, got_tail[at : at + t * c])
                below[s].append(got_head[at : at + t * c])
                at += t * c
        left = [n - t for n, t in zip(left, take)]
        distance += 1
    return jnp.concatenate([v for s, own in enumerate(levels) for v in above[s] + [own] + below[s]], axis=0)


def after(value, *others):
    return lax.optimization_barrier((value,) + others)[0]


def turn_pairs(step):
    return [((z * 2 + c) * 4 + s, (((z + step) % 4) * 2 + c) * 4 + s) for z in range(4) for c in range(2) for s in range(4)]


def flip_pairs(which):
    return [((z * 2 + c) * 4 + s, (z * 2 + c) * 4 + (s ^ FLIPS[c][which])) for z in range(4) for c in range(2) for s in range(4)]


def core_pairs():
    return [((z * 2 + c) * 4 + s, (z * 2 + 1 - c) * 4 + s) for z in range(4) for c in range(2) for s in range(4)]


def staged_gather(every, own, wide, tops, bottoms, begin):
    def swap(n, parts):
        four = [lines[n], ones[n], twos[n], boths[n]] if len(boths) > n else [lines[n], ones[n], twos[n]]
        chosen = [four[part] for part in parts]
        return lax.ppermute(jnp.stack(chosen) if len(parts) > 1 else chosen[0], every, core_pairs())

    lines, ones, twos, boths, swaps = [wide], [], [], [], [[] for _ in TURNS]
    ends = len(TURNS) - 1
    for turn in range(len(TURNS) + 1):
        fresh = {}
        if turn < len(TURNS):
            fresh["one"] = lax.ppermute(lines[turn], every, flip_pairs(0))
            fresh["two"] = lax.ppermute(lines[turn], every, flip_pairs(1))
        if turn < ends:
            step = TURNS[turn + 1]
            if step == 2:
                fresh["line"] = lax.ppermute(after(lines[1], *ones), every, turn_pairs(1))
            else:
                fresh["line"] = lax.ppermute(after(own, *ones) if ones else own, every, turn_pairs(step))
        if turn:
            fresh["both"] = lax.ppermute(ones[turn - 1], every, flip_pairs(1))
        if turn >= 2:
            fresh["swap"] = swap(turn - 2, GROUPS[turn - 2][0])
        if turn == ends:
            *prepared, fresh["token"] = begin(edges, [lines[0], ones[0], twos[0], boths[0]])
        if turn == len(TURNS):
            fresh["early"] = swap(ends, GROUPS[ends][0])
        if not turn:
            fresh["above"] = from_neighbour(bottoms, 1, "space")
            fresh["below"] = from_neighbour(tops, -1, "space")
        loose = {key: fresh.pop(key) for key in ("swap", "early") if key in fresh}
        fresh = dict(zip(fresh, lax.optimization_barrier(tuple(fresh.values())))) | loose
        if not turn:
            edges = [fresh["above"], fresh["below"]]
        if turn < len(TURNS):
            ones.append(fresh["one"])
            twos.append(fresh["two"])
        if turn < ends:
            lines.append(fresh["line"])
        if turn:
            boths.append(fresh["both"])
        if turn >= 2:
            swaps[turn - 2].append(fresh["swap"])
    swaps[ends] += [fresh["early"], swap(ends, GROUPS[ends][1])]
    mine = [lines, ones, twos, boths]
    groups = {(n, group): array for n in range(len(TURNS)) for group, array in zip(GROUPS[n], swaps[n])}
    return prepared, [mine[parts[0]][n] if own_side else groups[n, parts] for n, own_side, parts in ITEMS]


def total_of(*terms):
    return sum((t.astype(f32) for t in terms[1:]), terms[0].astype(f32))


def staged_scatter(every, blocks, place, conv_rows, head_cols, gains, input_grad, *hold):
    order = TURNS[::-1]
    boths, ones, twos, parts = {}, {}, {}, {}
    along = {}
    for n in range(len(order) + 1):
        fresh = {}
        if n < len(order):
            both = blocks[order[n]][3]
            fresh["both"] = lax.ppermute(both if n else after(both, *hold), every, flip_pairs(1))
        if n:
            turn = order[n - 1]
            fresh["two"] = lax.ppermute(blocks[turn][2], every, flip_pairs(1))
            fresh["one"] = lax.ppermute(total_of(blocks[turn][1], boths[turn]).astype(bf16), every, flip_pairs(0))
        if n >= 2:
            turn = order[n - 2]
            terms = [blocks[turn][0], twos[turn], ones[turn]]
            if turn == 1:
                terms.append(along[2])
            fresh["along"] = lax.ppermute(total_of(*terms).astype(bf16), every, turn_pairs(1 if turn == 2 else turn))
        if n == 1:
            fresh["input"] = input_grad
        fresh = dict(zip(fresh, lax.optimization_barrier(tuple(fresh.values()))))
        input_grad = fresh.get("input", input_grad)
        if n < len(order):
            boths[order[n]] = fresh["both"]
        if n:
            ones[order[n - 1]], twos[order[n - 1]] = fresh["one"], fresh["two"]
        if n >= 2:
            along[order[n - 2]] = fresh["along"]
    terms = blocks[0][0], twos[0], ones[0], along[1], along[3]
    keep, give = halves(place, *terms)
    return *deliver(place, keep, lax.ppermute(give, every, core_pairs()), conv_rows, head_cols, gains), input_grad


def shards(
    features,
    conv_master,
    head_master,
    scale_master,
    join_master,
    affine_scale,
    affine_shift,
    head_cotangent,
    pool_cotangent,
    box_counts,
    proposals,
):
    images, rows, cols, depth = features.shape
    total = head_master.shape[1]
    strip = Strip(rows, cols)
    every = ("dp", "space")
    own_gain, own_join = scale_master.shape[0], join_master.shape[0]
    staged = lax.axis_size("dp") == 8 and lax.axis_size("space") == 4
    line, rank = lax.axis_index("dp"), lax.axis_index("space")
    place = jnp.stack([rank, jnp.int32(lax.axis_size("space")), box_counts[0], line // 2, line % 2]).astype(jnp.int32)
    spread = jnp.asarray(spread_matrix(strip), bf16)
    x = features.reshape(rows * cols, depth)
    if staged:
        packed = pack(strip, conv_master, head_master, scale_master, join_master, x, spread.T)
        conv_rows = conv_master.shape[0]

        def begin(edges, blocks):
            return prepare(strip, place, x, edges, blocks, LAYERS * 9 * depth // conv_rows)

        conv_full = conv_rows, *staged_gather(every, *packed, begin)
    else:
        conv_full = lax.all_gather(conv_master.astype(bf16), every, axis=0, tiled=True)
        head_full = lax.all_gather(head_master.astype(bf16), every, axis=0, tiled=True)
        small = jnp.concatenate([scale_master, join_master]).astype(bf16)
        small = lax.all_gather(small[None], every, axis=0, tiled=True).astype(f32)
        small = jnp.concatenate([small[:, :own_gain].reshape(1, total), small[:, own_gain:].reshape(SCALES, total)], axis=0)
        means = []
        for s in range(1, SCALES):
            at = strip.starts(0)[s] - strip.starts(0)[1]
            pick = spread[:, at : at + strip.sizes(0)[s]]
            means.append((mm(pick, x, TN) * (0.25**s)).astype(bf16))
        x = with_rows(strip, [x] + means, "space")
    results = forward(strip, place, x, conv_full, affine_scale, affine_shift, total)
    if staged:
        p0, p1, p2, a3, small, conv_full, head_full, acts = results
    else:
        p0, p1, p2, a3, acts = results
    pre = p0, p1, p2
    maps, pool, sums, dz, first, final, *halves = head(
        strip, place, a3, head_full, small, head_cotangent.reshape(rows * cols, total), pool_cotangent, proposals,
        spread, affine_scale, p2, staged,
    )
    block_rows = LAYERS * 9 * depth
    if staged:
        swap = functools.partial(lax.ppermute, axis_name=every, perm=core_pairs())
        *halves, dg_keep, dg_give = halves
        others = swap(acts)
        block_rows = packed[0].shape[0] * 2
    else:
        (head_grad,), halves = halves, []
        conv_rows = None
    grad = None
    for layer in (2, 1, 0):
        above, below = from_neighbour(final, 1, "space"), from_neighbour(first, -1, "space")
        if staged:
            keep, give = halves
            pair = [acts, others], [keep, swap(give)]
        else:
            pair = [acts], [dz]
        *grad, token = weight_grad(strip, layer, place, *pair, grad, block_rows, conv_rows)
        if layer == 2 and staged:
            grad = chip_head_grad(place, acts, others, dg_keep, swap(dg_give), sums, pool, grad, conv_rows)
        more = [affine_scale, pre[layer - 1]] if layer else [spread]
        dz, *edge = data_grad(strip, layer, place, dz, above, below, conv_full, token, more, staged)
        if layer:
            first, final, *halves = edge
    input_grad = dz
    me = line * lax.axis_size("space") + rank
    if staged:
        conv_grad, head_grad, gain_grad, join_grad, pooled, input_grad = staged_scatter(
            every, [grad[4 * n : 4 * n + 4] for n in range(4)], place, conv_rows, total, own_gain, input_grad, above, below
        )
    else:
        pooled = lax.psum(pool, "space") / box_counts.astype(f32)[:, None]
        sums = lax.psum(sums, every)
        gain_grad = lax.dynamic_slice_in_dim(sums[0], me * own_gain, own_gain)
        join_grad = lax.dynamic_slice_in_dim(sums[1:].reshape(-1), me * own_join, own_join)
        conv_grad = lax.psum_scatter(grad[0], every, scatter_dimension=0, tiled=True).astype(f32)
        head_grad = lax.psum_scatter(head_grad, every, scatter_dimension=0, tiled=True).astype(f32)
    return (
        maps.reshape(images, rows, cols, total),
        pooled,
        input_grad.reshape(images, rows, cols, depth),
        conv_grad,
        head_grad,
        gain_grad.reshape(-1),
        join_grad.reshape(-1),
    )


def solution(mesh):
    return jax.shard_map(
        shards,
        mesh=mesh,
        in_specs=(
            P("dp", "space", None, None),
            P(("dp", "space"), None),
            P(("dp", "space"), None),
            P(("dp", "space")),
            P(("dp", "space")),
            P(),
            P(),
            P("dp", "space", None, None),
            P("dp", None),
            P("dp"),
            P("dp", None),
        ),
        out_specs=(
            P("dp", "space", None, None),
            P("dp", None),
            P("dp", "space", None, None),
            P(("dp", "space"), None),
            P(("dp", "space"), None),
            P(("dp", "space")),
            P(("dp", "space")),
        ),
        check_vma=False,
    )
```

```python
import functools
import math

import jax
import jax.numpy as jnp
import numpy as np
from jax import lax
from jax.experimental import pallas as pl
from jax.experimental.pallas import tpu as pltpu
from jax.sharding import PartitionSpec as P

HEAD_CH = 256
TASK_HEADS = 7
SCALES = 3
LAYERS = 3
PAD = 8

epsilon = 1e-06
f32 = jnp.float32
bf16 = jnp.bfloat16
NN = (((1,), (0,)), ((), ()))
NT = (((1,), (1,)), ((), ()))
TN = (((0,), (0,)), ((), ()))


def mm(left, right, dims=NN):
    return lax.dot_general(left, right, dims, preferred_element_type=f32)


def split_mm(left, right):
    high = right.astype(bf16)
    low = (right - high.astype(f32)).astype(bf16)
    return mm(left, high) + mm(left, low)


class Strip:
    def __init__(self, rows, cols):
        self.rows = [rows >> s for s in range(SCALES)]
        self.cols = [cols >> s for s in range(SCALES)]

    def sizes(self, halo):
        return [(r + 2 * halo) * c for r, c in zip(self.rows, self.cols)]

    def starts(self, halo):
        sizes = self.sizes(halo)
        return [sum(sizes[:s]) for s in range(SCALES)]

    def total(self, halo):
        return sum(self.sizes(halo))

    def own(self, halo):
        return [st + halo * c for st, c in zip(self.starts(halo), self.cols)]


def spread_matrix(strip):
    rows, cols = strip.rows[0], strip.cols[0]
    parts = []
    for s in range(1, SCALES):
        mat = np.zeros((rows * cols, strip.rows[s] * strip.cols[s]), np.float32)
        for r in range(rows):
            for c in range(cols):
                mat[r * cols + c, (r >> s) * strip.cols[s] + (c >> s)] = 1.0
        parts.append(mat)
    return np.concatenate(parts, axis=1)


def column_of(strip, scale, count):
    return lax.broadcasted_iota(jnp.int32, (count, 1), 0) % strip.cols[scale]


def shifted_copies(strip, halo, act, wide, depth):
    for s in range(SCALES):
        start, count, cols = strip.starts(halo)[s], strip.sizes(halo)[s], strip.cols[s]
        column = column_of(strip, s, count)
        for k in range(3):
            rows = act[PAD + start + k - 1 : PAD + start + k - 1 + count, :]
            if k == 0:
                rows = jnp.where(column == 0, 0.0, rows)
            if k == 2:
                rows = jnp.where(column == cols - 1, 0.0, rows)
            wide[start : start + count, k * depth : (k + 1) * depth] = rows.astype(bf16)


def patches(strip, halo, wide, cells, depth, flip=False, base=0):
    for s in range(SCALES):
        cols = strip.cols[s]
        count = strip.sizes(halo)[s]
        source, target = strip.starts(halo + 1)[s], strip.starts(halo)[s]
        for ky in range(3):
            first = source + (2 - ky if flip else ky) * cols
            for kx in range(3):
                col = (2 - kx if flip else kx) * depth
                tap = 3 * ky + kx
                cells[base + target : base + target + count, tap * depth : (tap + 1) * depth] = wide[
                    first : first + count, col : col + depth
                ]


FLIPS = ((1, 2), (2, 1))
TURNS = (0, 1, 3, 2)
GROUPS = (((0, 1, 2, 3),),) * 2 + (((0, 1, 2), (3,)), ((0,), (1,), (2,), (3,)))
SWAPS = {2: ((0, GROUPS[0][0]),), 3: ((1, GROUPS[1][0]), (2, GROUPS[2][0]), (3, GROUPS[3][0])), 4: ((2, GROUPS[2][1]), (3, GROUPS[3][1]), (3, GROUPS[3][2]))}
ITEMS = tuple(
    item
    for n in range(4)
    for item in [(n, True, (part,)) for part in range(4)] + [(n, False, group) for group in GROUPS[n]]
)


def across(place, part, core):
    rank = place[0]
    for bit in range(2):
        if part >> bit & 1:
            rank = rank ^ jnp.where(core == 0, FLIPS[0][bit], FLIPS[1][bit])
    return rank


def load_blocks(conv_rows, place, refs, weights, head_w, sem):
    depth = weights.shape[1]
    pieces, rows = head_w.shape[:2]
    head_rows = rows * conv_rows // weights.shape[0]
    layer_rows = weights.shape[0] // LAYERS
    last = [-(-layer_rows * (n + 1) // conv_rows) for n in range(LAYERS)]
    blocks = []
    for (n, own, parts), ref in zip(ITEMS, refs):
        core = place[4] if own else 1 - place[4]
        z = (place[3] + 4 - TURNS[n]) % 4
        for at, part in enumerate(parts):
            block = ref if len(parts) == 1 else ref.at[at]
            blocks.append((block, (z * 2 + core) * 4 + across(place, part, core)))
    for layer in range(LAYERS):
        for block, k in blocks:
            copy = pltpu.make_async_copy(
                block.at[pl.ds(0, conv_rows), :],
                weights.at[pl.ds(pl.multiple_of(k * conv_rows, 16), conv_rows), :],
                sem.at[layer],
            )
            inside = k < last[layer]
            if layer:
                inside = inside & (k >= last[layer - 1])
            pl.when(inside)(copy.start)
    for block, k in blocks:
        pltpu.make_async_copy(
            block.at[pl.ds(conv_rows, pieces * head_rows), :].reshape(pieces, head_rows, depth),
            head_w.at[:, pl.ds(pl.multiple_of(k * head_rows, 16), head_rows), :],
            sem.at[LAYERS],
        ).start()
    waits = []
    for first, stop in zip([0] + last, last):
        rows = weights.at[pl.ds(first * conv_rows, (stop - first) * conv_rows), :]
        waits.append(pltpu.make_async_copy(rows, rows, sem.at[len(waits)]))
    return waits + [pltpu.make_async_copy(head_w, head_w, sem.at[LAYERS])]


def prepare_kernel(strip, depth, place, x_ref, above_ref, below_ref, *refs):
    blocks, (cells, acts_ref, token, strips, act, wide, x_sem) = refs[:4], refs[4:]
    strips[...] = jnp.zeros(strips.shape, bf16)
    coarse = strips.shape[1]
    fetches = []
    for part in range(4):
        copy = pltpu.make_async_copy(
            blocks[part].at[pl.ds(blocks[part].shape[0] - coarse, coarse), :],
            strips.at[3 + across(place, part, place[4])],
            x_sem.at[part],
        )
        copy.start()
        fetches.append(copy)
    token[...] = jnp.zeros(token.shape, f32)
    at = PAD
    for ref in (above_ref, x_ref, below_ref):
        act[at : at + ref.shape[0], :] = ref[...].astype(f32)
        at += ref.shape[0]
    for copy in fetches:
        copy.wait()
    for s in range(1, SCALES):
        rows, cols = strip.rows[s], strip.cols[s]
        first = strip.starts(0)[s] - strip.starts(0)[1]
        for row in range(-3, rows + 3):
            source = strips[place[0] + 3 + row // rows, first + row % rows * cols : first + (row % rows + 1) * cols, :]
            act[at : at + cols, :] = source.astype(f32)
            at += cols
    first_patches(strip, depth, act, wide, cells, acts_ref)


def first_patches(strip, depth, act, wide, cells, acts_ref):
    for s in range(SCALES):
        start, size = strip.starts(1)[s], strip.sizes(1)[s]
        first = PAD + strip.starts(3)[s] + 2 * strip.cols[s]
        acts_ref[start : start + size, :] = act[first : first + size, :].astype(bf16)
    shifted_copies(strip, LAYERS, act, wide, depth)
    patches(strip, LAYERS - 1, wide, cells, depth)


def pack_kernel(strip, conv_ref, head_ref, gain_ref, join_ref, x_ref, gather_ref, own_ref, wide_ref, top_ref, bottom_ref):
    depth = conv_ref.shape[1]
    at = conv_ref.shape[0]
    rows, head_cols = head_ref.shape
    for ref in (own_ref, wide_ref):
        ref[:at, :] = conv_ref[...].astype(bf16)
    for first in range(0, head_cols, depth):
        width = min(depth, head_cols - first)
        piece = head_ref[:, first : first + width]
        if width < depth:
            small = jnp.concatenate([gain_ref[...], join_ref[...]], axis=1)
            small = jnp.concatenate([small, jnp.zeros((1, depth - width - small.shape[1]), f32)], axis=1)
            row = lax.broadcasted_iota(jnp.int32, (rows, depth - width), 0)
            small = jnp.where(row == 0, jnp.broadcast_to(small, (rows, depth - width)), 0.0)
            piece = jnp.concatenate([piece, small], axis=1)
        for ref in (own_ref, wide_ref):
            ref[at : at + rows, :] = piece.astype(bf16)
        at += rows
    x = x_ref[...]
    sums = mm(gather_ref[...], x)
    for s in range(1, SCALES):
        first = strip.starts(0)[s] - strip.starts(0)[1]
        size = strip.sizes(0)[s]
        wide_ref[at : at + size, :] = (sums[first : first + size] * (0.25**s)).astype(bf16)
        at += size
    edge = 3 * strip.cols[0]
    top_ref[...] = x_ref[:edge, :]
    bottom_ref[...] = x_ref[x.shape[0] - edge :, :]


def forward_kernel(strip, depth, staged, place, scale_ref, shift_ref, *refs):
    taps = 9 * depth
    halos = [LAYERS - 1 - layer for layer in range(LAYERS)]
    if staged:
        conv_rows, head_cols = staged
        expand_hbm, owner_ref, first_cells, *refs = refs
        blocks, refs = refs[: len(ITEMS)], refs[len(ITEMS) :]
        first_acts, refs = refs[0], refs[1:]
        p_refs, refs = refs[:3], refs[3:]
        a3_ref, small_ref, weights, head_ref, acts_ref, act, wide, cells, expand, sem = refs
        loads = load_blocks(conv_rows, place, blocks, weights, head_ref, sem)
        expand_load = pltpu.make_async_copy(expand_hbm, expand, sem.at[LAYERS + 1])
        expand_load.start()
        acts_ref[: first_acts.shape[0], :] = first_acts[...]
    else:
        x_ref, w_hbm, *refs = refs
        p_refs, refs = refs[:3], refs[3:]
        a3_ref, acts_ref, weights, act, wide, cells, sem = refs
        load = pltpu.make_async_copy(w_hbm, weights, sem.at[0])
        load.start()
        act[PAD : PAD + strip.total(3), :] = x_ref[...].astype(f32)
        first_cells = cells
        first_patches(strip, depth, act, wide, cells, acts_ref)
        load.wait()
    here, ranks = place[0], place[1]
    flat = strip.starts(0)
    for layer, halo in enumerate(halos):
        count = strip.total(halo)
        if layer:
            shifted_copies(strip, halo + 1, act, wide, depth)
            patches(strip, halo, wide, cells, depth)
        used = cells if layer else first_cells
        own = strip.own(halo)
        if staged:
            loads[layer].wait()
        for half in range(depth // 256):
            lanes = slice(half * 256, (half + 1) * 256)
            z = mm(used[:count, :], weights[layer * taps : (layer + 1) * taps, lanes])
            p = z * scale_ref[layer : layer + 1, lanes] + shift_ref[layer : layer + 1, lanes]
            a = (p / (1.0 + jnp.exp(-p))).astype(bf16)
            for s in range(SCALES):
                size = strip.sizes(0)[s]
                p_refs[layer][flat[s] : flat[s] + size, lanes] = p[own[s] : own[s] + size]
            if layer == LAYERS - 1:
                a3_ref[:, lanes] = a
                acts_ref[LAYERS * strip.total(1) :, lanes] = a
            else:
                for s in range(SCALES):
                    start, size = strip.starts(halo)[s], strip.sizes(halo)[s]
                    row = lax.broadcasted_iota(jnp.int32, (size, 1), 0) // strip.cols[s]
                    row = row + here * strip.rows[s] - halo
                    inside = (row >= 0) & (row < ranks * strip.rows[s])
                    kept = jnp.where(inside, a[start : start + size].astype(f32), 0.0)
                    act[PAD + start : PAD + start + size, lanes] = kept
                    edge = (halo - 1) * strip.cols[s]
                    first, size = (layer + 1) * strip.total(1) + strip.starts(1)[s], strip.sizes(1)[s]
                    acts_ref[first : first + size, lanes] = kept[edge : edge + size].astype(bf16)
    if staged:
        loads[LAYERS].wait()
        expand_load.wait()
        owners, spare = owner_ref.shape[0], expand.shape[0]
        pieces, depth_rows = head_ref.shape[:2]
        row = lax.broadcasted_iota(jnp.int32, (owners, depth_rows), 0)
        col = lax.broadcasted_iota(jnp.int32, (owners, depth_rows), 1)
        pick = jnp.where(col == row * (depth_rows // owners), 1.0, 0.0).astype(bf16)
        picked = mm(pick, head_ref[pieces - 1, :, depth - spare :]).astype(bf16)
        for n in range(1 + SCALES):
            cols = slice(n * head_cols, (n + 1) * head_cols)
            spread = mm(picked, expand[:, cols]) * owner_ref[:, cols].astype(f32)
            small_ref[n : n + 1, :] = jnp.sum(spread, axis=0, keepdims=True)


def slope(p):
    sigma = 1.0 / (1.0 + jnp.exp(-p))
    return sigma * (1.0 + p * (1.0 - sigma))


def head_kernel(
    strip, split, place, a3_ref, w_ref, small_ref, cot_ref, pool_cot_ref, where_ref, spread_ref, gather_ref,
    scale_ref, p2_ref, maps_ref, pool_ref, sums_ref, *refs,
):
    if split:
        *grads, keep_ref, give_ref, dg_all = refs
    else:
        *grads, w_grad_ref, dg_all = refs
    fine = strip.sizes(0)[0]
    starts, sizes = strip.starts(0), strip.sizes(0)
    parts = [slice(starts[s], starts[s] + sizes[s]) for s in range(SCALES)]
    slots = where_ref.shape[1]
    pixel = lax.broadcasted_iota(jnp.int32, (fine, slots), 0) + place[0] * fine
    slot = lax.broadcasted_iota(jnp.int32, (fine, slots), 1)
    hits = jnp.where((where_ref[...] == pixel) & (slot < place[2]), 1.0, 0.0)
    hits = jnp.sum(hits, axis=-1, keepdims=True)
    share = pool_cot_ref[...] / place[2].astype(f32)
    heads = maps_ref.shape[1] // HEAD_CH
    depth = a3_ref.shape[1]
    per = depth // HEAD_CH
    da3 = None
    for head in range(heads):
        lanes = slice(head * HEAD_CH, (head + 1) * HEAD_CH)
        if split:
            weight = w_ref[head // per, :, head % per * HEAD_CH : (head % per + 1) * HEAD_CH]
        else:
            weight = w_ref[:, lanes]
        g = mm(a3_ref[...], weight)
        inverse = lax.rsqrt(jnp.sum(g * g, axis=-1, keepdims=True) + epsilon)
        unit = g * inverse
        gain = small_ref[0:1, lanes]
        join = [small_ref[1 + s : 2 + s, lanes] for s in range(SCALES)]
        normed = unit * gain
        coarse = jnp.concatenate([normed[parts[s]] * join[s] for s in range(1, SCALES)], axis=0)
        joined = normed[:fine] * join[0] + split_mm(spread_ref[...], coarse)
        maps_ref[:, lanes] = joined.astype(bf16)
        fused = cot_ref[:, lanes]
        if head == 0:
            pool_ref[...] = jnp.sum(joined * hits, axis=0, keepdims=True)
            fused = fused.astype(f32) + hits * share
            down_coarse = split_mm(gather_ref[...], fused)
        else:
            down_coarse = mm(gather_ref[...], fused)
        down = jnp.concatenate([fused.astype(f32), down_coarse], axis=0)
        product = down * normed
        scaled = []
        for s in range(SCALES):
            sums_ref[s + 1 : s + 2, lanes] = jnp.sum(product[parts[s]], axis=0, keepdims=True)
            scaled.append(down[parts[s]] * join[s])
        dn = jnp.concatenate(scaled, axis=0)
        sums_ref[0:1, lanes] = jnp.sum(dn * unit, axis=0, keepdims=True)
        du = dn * gain
        dg = (inverse * (du - unit * jnp.sum(du * unit, axis=-1, keepdims=True))).astype(bf16)
        dg_all[head] = dg
        if not split:
            w_grad_ref[:, lanes] = mm(a3_ref[...], dg, TN).astype(bf16)
        part = mm(dg, weight, NT)
        da3 = part if da3 is None else da3 + part
    layer = LAYERS - 1
    dz = da3 * scale_ref[layer : layer + 1, :] * slope(p2_ref[...])
    emit_grad(strip, place, dz.astype(bf16), *grads)
    if split:
        width = HEAD_CH
        first = place[4] == 0
        half = heads * width // 2
        for start in range(0, half, width // 2):
            left = dg_all[start // width, :, start % width : start % width + width // 2]
            at = half + start
            right = dg_all[at // width, :, at % width : at % width + width // 2]
            keep_ref[:, start : start + width // 2] = jnp.where(first, left, right)
            give_ref[:, start : start + width // 2] = jnp.where(first, right, left)


def emit_grad(strip, place, dz, dz_ref, first_ref, last_ref, keep_ref=None, give_ref=None):
    dz_ref[...] = dz
    edge = 0
    for start, size, cols in zip(strip.starts(0), strip.sizes(0), strip.cols):
        first_ref[edge : edge + cols, :] = dz[start : start + cols]
        last_ref[edge : edge + cols, :] = dz[start + size - cols : start + size]
        edge += cols
    if keep_ref is not None:
        middle = dz.shape[1] // 2
        left, right = dz[:, :middle], dz[:, middle:]
        first = place[4] == 0
        keep_ref[...] = jnp.where(first, left, right)
        give_ref[...] = jnp.where(first, right, left)


def store_blocks(place, pieces, block_refs, sem):
    for turn in range(4):
        for part in range(4):
            out = block_refs[4 * turn + part]
            z = (place[3] + turn) % 4
            rank = across(place, part, place[4])
            for core in range(2):
                k = (z * 2 + core) * 4 + rank
                base = core * (out.shape[0] // 2)
                for condition, source, row in pieces(k):
                    target = out.at[pl.ds(base + row, math.prod(source.shape[:-1])), :]
                    if len(source.shape) > 2:
                        target = target.reshape(source.shape)
                    copy = pltpu.make_async_copy(source, target, sem)
                    if condition is None:
                        copy.start()
                    else:
                        pl.when(condition)(copy.start)


def weight_grad_kernel(strip, depth, layer, images, conv_rows, place, *refs):
    acts, grads = refs[:images], refs[images : 2 * images]
    *outs, token, act, wide, cells, dz, result, sem = refs[2 * images :]
    own, count = strip.total(0), strip.total(1)
    for n in range(images):
        act[PAD : PAD + count, :] = acts[n][layer * count : (layer + 1) * count, :].astype(f32)
        shifted_copies(strip, 1, act, wide, depth)
        patches(strip, 0, wide, cells, depth, base=n * own)
        dz[n * own : (n + 1) * own, :] = grads[n][...]
    for tap in range(9):
        lanes = slice(tap * depth, (tap + 1) * depth)
        result[lanes, :] = mm(cells[:, lanes], dz[...], TN).astype(bf16)
    rows = 9 * depth
    first_row, stop_row = layer * rows, (layer + 1) * rows
    token[...] = jnp.zeros(token.shape, f32)
    if conv_rows is None:
        copy = pltpu.make_async_copy(result, outs[-1].at[pl.ds(first_row, rows), :], sem)
        copy.start()
        copy.wait()
        return

    def pieces(k):
        out = []
        inside = (k * conv_rows >= first_row) & ((k + 1) * conv_rows <= stop_row)
        start = jnp.where(inside, k * conv_rows - first_row, 0)
        out.append((inside, result.at[pl.ds(pl.multiple_of(start, 16), conv_rows), :], 0))
        if first_row % conv_rows:
            size = conv_rows - first_row % conv_rows
            out.append((k == first_row // conv_rows, result.at[pl.ds(0, size), :], conv_rows - size))
        if stop_row % conv_rows:
            size = stop_row % conv_rows
            out.append((k == stop_row // conv_rows, result.at[pl.ds(rows - size, size), :], 0))
        return out

    store_blocks(place, pieces, outs[-16:], sem)
    pltpu.make_async_copy(result, result, sem).wait()


def chip_head_grad_kernel(conv_rows, place, a3_ref, other_ref, keep_ref, got_ref, sums_ref, pool_ref, owner_ref, expand, *refs):
    refs = refs[-(16 + 4) :]
    outs, (a3, dg, result, out_sem) = refs[:16], refs[16:]
    own = keep_ref.shape[0]
    for n, ref in enumerate((a3_ref, other_ref)):
        pltpu.make_async_copy(ref.at[pl.ds(ref.shape[0] - own, own), :], a3.at[pl.ds(n * own, own), :], out_sem).start()
    pltpu.make_async_copy(a3, a3, out_sem).wait()
    dg[:own, :] = keep_ref[...]
    dg[own:, :] = got_ref[...]
    width = result.shape[2]
    cols = dg.shape[1]
    for piece in range(result.shape[0]):
        stop = min(cols, (piece + 1) * width)
        lanes = slice(piece * width, stop)
        result[piece, :, : stop - piece * width] = mm(a3[...], dg[:, lanes], TN).astype(bf16)
    owners, depth_rows, spare = owner_ref.shape[0], result.shape[1], width - cols % width
    small = None
    for n in range(sums_ref.shape[0]):
        lanes = slice(n * sums_ref.shape[1], (n + 1) * sums_ref.shape[1])
        each = (sums_ref[n : n + 1, :] * owner_ref[:, lanes].astype(f32)).astype(bf16)
        term = mm(each, expand[:, lanes], NT)
        small = term if small is None else small + term
    row = lax.broadcasted_iota(jnp.int32, (depth_rows, owners), 0)
    col = lax.broadcasted_iota(jnp.int32, (depth_rows, owners), 1)
    tail = None
    for n in range(small.shape[1] // spare):
        pick = jnp.where(row == col * (depth_rows // owners) + n, 1.0, 0.0).astype(bf16)
        term = mm(pick, small[:, n * spare : (n + 1) * spare].astype(bf16))
        tail = term if tail is None else tail + term
    row = lax.broadcasted_iota(jnp.int32, (depth_rows, spare), 0)
    each = depth_rows // owners
    mine = row // (each * 4) == place[3] * 2 + place[4]
    for n in range(2):
        here = mine & (row % each == 2 + 2 * place[0] + n)
        tail = jnp.where(here, pool_ref[:, n * spare : (n + 1) * spare], tail)
    result[result.shape[0] - 1, :, cols % width :] = tail.astype(bf16)
    rows = (outs[0].shape[0] // 2 - conv_rows) // result.shape[0]

    def pieces(k):
        return [(None, result.at[:, pl.ds(pl.multiple_of(k * rows, 16), rows), :], conv_rows)]

    store_blocks(place, pieces, outs, out_sem)
    pltpu.make_async_copy(result, result, out_sem).wait()


def halves_kernel(place, *refs):
    *terms, keep_ref, give_ref = refs
    whole = total_of(*[t[...] for t in terms])
    half = keep_ref.shape[0]
    first = place[4] == 0
    keep_ref[...] = jnp.where(first, whole[:half], whole[half:])
    give_ref[...] = jnp.where(first, whole[half:], whole[:half])


def deliver_kernel(place, keep_ref, got_ref, conv_ref, head_ref, gain_ref, join_ref, pool_ref):
    first = place[4] == 0
    keep, got = keep_ref[...], got_ref[...]
    width = keep.shape[1]
    rows = head_ref.shape[0]
    half = head_ref.shape[1] // 2
    for n, side in enumerate((jnp.where(first, keep, got), jnp.where(first, got, keep))):
        conv_ref[:, n * width : (n + 1) * width] = side[: conv_ref.shape[0]]
        at = conv_ref.shape[0]
        for col in range(0, half, width):
            size = min(width, half - col)
            head_ref[:, n * half + col : n * half + col + size] = side[at : at + rows, :size]
            at += rows
    lanes = half % width
    small = (keep + got)[at - rows : at, lanes:]
    pooled = None
    for s in range(4):
        term = jnp.concatenate([small[2 + 2 * s : 3 + 2 * s], small[3 + 2 * s : 4 + 2 * s]], axis=1)
        pooled = term if pooled is None else pooled + term
    pool_ref[...] = pooled / place[2].astype(f32)
    small = jnp.concatenate([small[n : n + 1] for n in range(2)], axis=1)
    gains = gain_ref.shape[1]
    gain_ref[...] = small[:, :gains]
    join_ref[...] = small[:, gains : gains + join_ref.shape[1]]


def data_grad_kernel(
    strip, depth, layer, place, dz_ref, above_ref, below_ref, w_ref, _, *refs
):
    refs, (act, wide, cells) = refs[:-3], refs[-3:]
    last = layer == 0
    if last:
        spread_ref, out_ref = refs
    else:
        scale_ref, p_ref, *outs = refs
    edge = 0
    for s in range(SCALES):
        start, size, cols = strip.starts(1)[s], strip.sizes(0)[s], strip.cols[s]
        flat = strip.starts(0)[s]
        act[PAD + start : PAD + start + cols, :] = above_ref[edge : edge + cols, :].astype(f32)
        act[PAD + start + cols : PAD + start + cols + size, :] = dz_ref[flat : flat + size, :].astype(f32)
        act[PAD + start + cols + size : PAD + start + 2 * cols + size, :] = below_ref[edge : edge + cols, :].astype(f32)
        edge += cols
    shifted_copies(strip, 1, act, wide, depth)
    patches(strip, 0, wide, cells, depth, flip=True)
    base = layer * 9 * depth
    value = None
    for tap in range(9):
        term = mm(
            cells[:, tap * depth : (tap + 1) * depth], w_ref[base + tap * depth : base + (tap + 1) * depth, :], NT
        )
        value = term if value is None else value + term
    if last:
        fine = strip.sizes(0)[0]
        coarse = jnp.concatenate(
            [
                value[st : st + size] * (0.25**s)
                for s, (st, size) in enumerate(zip(strip.starts(0), strip.sizes(0)))
                if s
            ],
            axis=0,
        )
        out_ref[...] = value[:fine] + split_mm(spread_ref[...], coarse)
    else:
        dz = value * scale_ref[layer - 1 : layer, :] * slope(p_ref[...])
        emit_grad(strip, place, dz.astype(bf16), *outs)


def vmem(shape=None, index=None):
    if shape is None:
        return pl.BlockSpec(memory_space=pltpu.VMEM)
    return pl.BlockSpec(shape, index)


SMEM = pl.BlockSpec(memory_space=pltpu.SMEM)
ANY = pl.BlockSpec(memory_space=pl.ANY)


def params(mebibytes):
    return pltpu.CompilerParams(vmem_limit_bytes=mebibytes << 20)


def small_layout(owners, cols, spare):
    gains = cols // owners
    expand = np.zeros((spare, (1 + SCALES) * cols), np.float32)
    owner = np.zeros((owners, (1 + SCALES) * cols), np.float32)
    for n in range((1 + SCALES) * cols):
        size = gains if n < cols else SCALES * gains
        at = n if n < cols else n - cols
        expand[at % size + (0 if n < cols else gains), n] = 1.0
        owner[at // size, n] = 1.0
    return jnp.asarray(expand, bf16), jnp.asarray(owner, bf16)


def pack(strip, conv, head_w, gain, join, x, gather):
    depth = conv.shape[1]
    rows = conv.shape[0] + head_w.shape[0] * -(-head_w.shape[1] // depth)
    edge = 3 * strip.cols[0]
    return pl.pallas_call(
        functools.partial(pack_kernel, strip),
        name="pack",
        out_shape=[jax.ShapeDtypeStruct((n, depth), bf16) for n in (rows, rows + gather.shape[0], edge, edge)],
        in_specs=[vmem()] * 6,
        out_specs=[vmem()] * 4,
        compiler_params=params(60),
    )(conv, head_w, gain[None], join[None], x, gather)


def on_chip(values):
    return [pltpu.with_memory_space_constraint(v, pltpu.MemorySpace.VMEM) for v in values]


def off_chip(values):
    return [pltpu.with_memory_space_constraint(v, pltpu.MemorySpace.HBM) for v in values]


def forward_scratch(strip, depth, halo):
    return [
        pltpu.VMEM((strip.total(halo) + 2 * PAD, depth), f32),
        pltpu.VMEM((strip.total(halo), 3 * depth), bf16),
    ]


def prepare(strip, place, x, edges, blocks, owners):
    depth = x.shape[1]
    coarse = strip.total(0) - strip.sizes(0)[0]
    return pl.pallas_call(
        functools.partial(prepare_kernel, strip, depth),
        name="prepare",
        out_shape=[
            pltpu.VMEM((strip.total(LAYERS - 1), 9 * depth), bf16),
            pltpu.VMEM((strip.total(1), depth), bf16),
            jax.ShapeDtypeStruct((8, 128), f32),
        ],
        in_specs=[SMEM] + [vmem()] * 3 + [ANY] * len(blocks),
        out_specs=[vmem()] * 3,
        scratch_shapes=[pltpu.VMEM((6 + owners // 8, coarse, depth), bf16)]
        + forward_scratch(strip, depth, LAYERS)
        + [pltpu.SemaphoreType.DMA((4,))],
        compiler_params=params(10),
    )(place, x, *edges, *off_chip(blocks))


def forward(strip, place, x, conv, scale, shift, head_cols):
    depth = scale.shape[1]
    own = strip.total(0)
    rows = LAYERS * 9 * depth
    acts = (LAYERS * strip.total(1) + own, depth)
    staged = isinstance(conv, tuple)
    cells = pltpu.VMEM((strip.total(1 if staged else LAYERS - 1), 9 * depth), bf16)
    if staged:
        conv_rows, prepared, blocks = conv
        expand, owner = small_layout(rows // conv_rows, head_cols, -head_cols % depth)
        first_cells, first_acts = on_chip(prepared)
        inputs = [expand, owner, first_cells, *off_chip(blocks), first_acts]
        in_specs = [ANY, vmem(), vmem()] + [ANY] * len(blocks) + [vmem()]
        outs = [pltpu.VMEM((own, depth), f32)] * 3 + [
            pltpu.VMEM((own, depth), bf16),
            pltpu.VMEM((1 + SCALES, head_cols), f32),
            pltpu.VMEM((rows, depth), bf16),
            pltpu.VMEM((-(-head_cols // depth), depth, depth), bf16),
            pltpu.VMEM(acts, bf16),
        ]
        scratch = forward_scratch(strip, depth, LAYERS - 1)
        scratch += [cells, pltpu.VMEM(expand.shape, bf16), pltpu.SemaphoreType.DMA((LAYERS + 2,))]
    else:
        inputs, in_specs = [x, conv], [vmem(), ANY]
        outs = [jax.ShapeDtypeStruct((own, depth), f32)] * 3
        outs += [jax.ShapeDtypeStruct(shape, bf16) for shape in ((own, depth), acts)]
        scratch = [pltpu.VMEM((rows, depth), bf16)] + forward_scratch(strip, depth, LAYERS)
        scratch += [cells, pltpu.SemaphoreType.DMA((1,))]
    return pl.pallas_call(
        functools.partial(forward_kernel, strip, depth, (conv_rows, head_cols) if staged else None),
        name="forward",
        out_shape=outs,
        in_specs=[SMEM, vmem(), vmem()] + in_specs,
        out_specs=[vmem()] * len(outs),
        scratch_shapes=scratch,
        compiler_params=params(28 if staged else 54),
    )(place, scale, shift, *inputs)


def head(strip, place, a3, weight, small, cot, pool_cot, where, spread, scale, p2, split):
    own, depth = a3.shape
    total = small.shape[1]
    fine = strip.sizes(0)[0]
    edge = sum(strip.cols)
    outs = [
        jax.ShapeDtypeStruct((fine, total), bf16),
        jax.ShapeDtypeStruct((1, HEAD_CH), f32),
        jax.ShapeDtypeStruct((1 + SCALES, total), f32),
    ]
    outs += [jax.ShapeDtypeStruct((n, depth), bf16) for n in (own, edge, edge)]
    if split:
        outs += [jax.ShapeDtypeStruct((own, n // 2), bf16) for n in (depth, depth, total, total)]
    else:
        outs += [jax.ShapeDtypeStruct((depth, total), bf16)]
    return pl.pallas_call(
        functools.partial(head_kernel, strip, split),
        name="heads",
        out_shape=outs,
        in_specs=[SMEM] + [vmem()] * 10,
        out_specs=[vmem()] * len(outs),
        scratch_shapes=[pltpu.VMEM((total // HEAD_CH, own, HEAD_CH), bf16)],
        compiler_params=params(24),
    )(place, a3, weight, small, cot, pool_cot, where, spread, spread.T, scale, p2)


def weight_grad(strip, layer, place, acts, grads, into, rows, conv_rows):
    own, half = grads[0].shape
    depth = acts[0].shape[1]
    images = len(acts)
    count_here = strip.total(1)
    into = into or []
    count = 1 if conv_rows is None else 16
    return pl.pallas_call(
        functools.partial(weight_grad_kernel, strip, depth, layer, images, conv_rows),
        name="weight_grad",
        out_shape=[pltpu.HBM((rows, half), bf16)] * count + [jax.ShapeDtypeStruct((8, 128), f32)],
        in_specs=[SMEM] + [vmem()] * (2 * images) + [ANY] * len(into),
        out_specs=[ANY] * count + [vmem()],
        scratch_shapes=[
            pltpu.VMEM((count_here + 2 * PAD, depth), f32),
            pltpu.VMEM((count_here, 3 * depth), bf16),
            pltpu.VMEM((images * own, 9 * depth), bf16),
            pltpu.VMEM((images * own, half), bf16),
            pltpu.VMEM((9 * depth, half), bf16),
            pltpu.SemaphoreType.DMA,
        ],
        input_output_aliases={1 + 2 * images + n: n for n in range(len(into))},
        compiler_params=params(22),
    )(place, *acts, *grads, *off_chip(into))


def chip_head_grad(place, a3, other, keep, got, sums, pool, blocks, conv_rows):
    own, depth = keep.shape[0], a3.shape[1]
    half = blocks[0].shape[1]
    expand, owner = small_layout(LAYERS * 9 * depth // conv_rows, sums.shape[1], -sums.shape[1] % depth)
    pieces = -(-keep.shape[1] // half)
    return pl.pallas_call(
        functools.partial(chip_head_grad_kernel, conv_rows),
        name="chip_head_grad",
        out_shape=[pltpu.HBM(b.shape, bf16) for b in blocks],
        in_specs=[SMEM, ANY, ANY] + [vmem()] * 6 + [ANY] * 16,
        out_specs=[ANY] * 16,
        scratch_shapes=[
            pltpu.VMEM((2 * own, depth), bf16),
            pltpu.VMEM((2 * own, keep.shape[1]), bf16),
            pltpu.VMEM((pieces, depth, half), bf16),
            pltpu.SemaphoreType.DMA,
        ],
        input_output_aliases={9 + n: n for n in range(16)},
        compiler_params=params(14),
    )(place, a3, other, keep, got, sums, pool, owner, expand, *off_chip(blocks))


def data_grad(strip, layer, place, dz, above, below, conv, token, others, split):
    if split:
        conv = pltpu.with_memory_space_constraint(conv, pltpu.MemorySpace.VMEM)
    own, depth = dz.shape
    last = layer == 0
    edge = sum(strip.cols)

    if last:
        outs = [jax.ShapeDtypeStruct((strip.sizes(0)[0], depth), f32)]
    else:
        outs = [jax.ShapeDtypeStruct((n, depth), bf16) for n in (own, edge, edge)]
        outs += [jax.ShapeDtypeStruct((own, depth // 2), bf16)] * (2 * split)
    return pl.pallas_call(
        functools.partial(data_grad_kernel, strip, depth, layer),
        name="data_grad",
        out_shape=outs,
        in_specs=[SMEM] + [vmem()] * 4 + [ANY] + [vmem()] * len(others),
        out_specs=[vmem()] * len(outs),
        scratch_shapes=[
            pltpu.VMEM((strip.total(1) + 2 * PAD, depth), f32),
            pltpu.VMEM((strip.total(1), 3 * depth), bf16),
            pltpu.VMEM((own, 9 * depth), bf16),
        ],
        compiler_params=params(14 if split else 32),
    )(place, dz, above, below, conv, token, *others)


def halves(place, *terms):
    rows, width = terms[0].shape
    return pl.pallas_call(
        halves_kernel,
        name="halves",
        out_shape=[jax.ShapeDtypeStruct((rows // 2, width), f32)] * 2,
        in_specs=[SMEM] + [vmem()] * len(terms),
        out_specs=[vmem()] * 2,
        compiler_params=params(16),
    )(place, *terms)


def deliver(place, keep, got, conv_rows, head_cols, gains):
    width = keep.shape[1]
    head_rows = (keep.shape[0] - conv_rows) // -(-(head_cols // 2) // width)
    return pl.pallas_call(
        deliver_kernel,
        name="deliver",
        out_shape=[
            jax.ShapeDtypeStruct((conv_rows, 2 * width), f32),
            jax.ShapeDtypeStruct((head_rows, head_cols), f32),
            jax.ShapeDtypeStruct((1, gains), f32),
            jax.ShapeDtypeStruct((1, SCALES * gains), f32),
            jax.ShapeDtypeStruct((1, HEAD_CH), f32),
        ],
        in_specs=[SMEM] + [vmem()] * 2,
        out_specs=[vmem()] * 5,
        compiler_params=params(8),
    )(place, keep, got)


def from_neighbour(cells, distance, axis):
    count = lax.axis_size(axis)
    pairs = [(i, i + distance) for i in range(count) if 0 <= i + distance < count]
    return lax.ppermute(cells, axis, pairs)


def with_rows(strip, levels, axis):
    above = [[] for _ in levels]
    below = [[] for _ in levels]
    left = [3] * len(levels)
    distance = 1
    while max(left) > 0:
        take = [min(n, r) for n, r in zip(left, strip.rows)]
        tails = [v[v.shape[0] - t * c :] for v, t, c in zip(levels, take, strip.cols) if t]
        heads = [v[: t * c] for v, t, c in zip(levels, take, strip.cols) if t]
        got_tail = from_neighbour(jnp.concatenate(tails, axis=0), distance, axis)
        got_head = from_neighbour(jnp.concatenate(heads, axis=0), -distance, axis)
        at = 0
        for s, (t, c) in enumerate(zip(take, strip.cols)):
            if t:
                above[s].insert(0, got_tail[at : at + t * c])
                below[s].append(got_head[at : at + t * c])
                at += t * c
        left = [n - t for n, t in zip(left, take)]
        distance += 1
    return jnp.concatenate([v for s, own in enumerate(levels) for v in above[s] + [own] + below[s]], axis=0)


def after(value, *others):
    return lax.optimization_barrier((value,) + others)[0]


def turn_pairs(step):
    return [((z * 2 + c) * 4 + s, (((z + step) % 4) * 2 + c) * 4 + s) for z in range(4) for c in range(2) for s in range(4)]


def flip_pairs(which):
    return [((z * 2 + c) * 4 + s, (z * 2 + c) * 4 + (s ^ FLIPS[c][which])) for z in range(4) for c in range(2) for s in range(4)]


def core_pairs():
    return [((z * 2 + c) * 4 + s, (z * 2 + 1 - c) * 4 + s) for z in range(4) for c in range(2) for s in range(4)]


def staged_gather(every, own, wide, tops, bottoms, begin):
    def swap(n, parts):
        mine = lines, ones, twos, boths
        chosen = [mine[part][n] for part in parts]
        return lax.ppermute(jnp.stack(chosen) if len(parts) > 1 else chosen[0], every, core_pairs())

    lines, ones, twos, boths, swaps = [wide], [], [], [], [[] for _ in TURNS]
    ends = len(TURNS) - 1
    for turn in range(len(TURNS) + 1):
        fresh = {}
        if turn < len(TURNS):
            fresh["one"] = lax.ppermute(lines[turn], every, flip_pairs(0))
            fresh["two"] = lax.ppermute(lines[turn], every, flip_pairs(1))
        if turn < ends:
            step = TURNS[turn + 1]
            if step == 2:
                fresh["line"] = lax.ppermute(after(lines[1], *ones), every, turn_pairs(1))
            else:
                fresh["line"] = lax.ppermute(after(own, *ones) if ones else own, every, turn_pairs(step))
        if turn:
            fresh["both"] = lax.ppermute(ones[turn - 1], every, flip_pairs(1))
        for n, parts in SWAPS.get(turn, ()):
            swaps[n].append(swap(n, parts))
        if turn == ends:
            *prepared, fresh["token"] = begin(edges, [lines[0], ones[0], twos[0], boths[0]])
        if not turn:
            fresh["above"] = from_neighbour(bottoms, 1, "space")
            fresh["below"] = from_neighbour(tops, -1, "space")
        fresh = dict(zip(fresh, lax.optimization_barrier(tuple(fresh.values()))))
        if not turn:
            edges = [fresh["above"], fresh["below"]]
        if turn < len(TURNS):
            ones.append(fresh["one"])
            twos.append(fresh["two"])
        if turn < ends:
            lines.append(fresh["line"])
        if turn:
            boths.append(fresh["both"])
    swaps[ends].append(swap(ends, GROUPS[ends][-1]))
    mine = [lines, ones, twos, boths]
    groups = {(n, group): array for n in range(len(TURNS)) for group, array in zip(GROUPS[n], swaps[n])}
    return prepared, [mine[parts[0]][n] if own_side else groups[n, parts] for n, own_side, parts in ITEMS]


def total_of(*terms):
    return sum((t.astype(f32) for t in terms[1:]), terms[0].astype(f32))


def staged_scatter(every, blocks, place, conv_rows, head_cols, gains, input_grad, *hold):
    order = TURNS[::-1]
    boths, ones, twos, parts = {}, {}, {}, {}
    along = {}
    for n in range(len(order) + 1):
        fresh = {}
        if n < len(order):
            both = blocks[order[n]][3]
            fresh["both"] = lax.ppermute(both if n else after(both, *hold), every, flip_pairs(1))
        if n:
            turn = order[n - 1]
            fresh["two"] = lax.ppermute(blocks[turn][2], every, flip_pairs(1))
            fresh["one"] = lax.ppermute(total_of(blocks[turn][1], boths[turn]).astype(bf16), every, flip_pairs(0))
        if n >= 2:
            turn = order[n - 2]
            terms = [blocks[turn][0], twos[turn], ones[turn]]
            if turn == 1:
                terms.append(along[2])
            fresh["along"] = lax.ppermute(total_of(*terms).astype(bf16), every, turn_pairs(1 if turn == 2 else turn))
        if n == 1:
            fresh["input"] = input_grad
        loose = {key: fresh.pop(key) for key in ("two",) if key in fresh}
        fresh = dict(zip(fresh, lax.optimization_barrier(tuple(fresh.values())))) | loose
        input_grad = fresh.get("input", input_grad)
        if n < len(order):
            boths[order[n]] = fresh["both"]
        if n:
            ones[order[n - 1]], twos[order[n - 1]] = fresh["one"], fresh["two"]
        if n >= 2:
            along[order[n - 2]] = fresh["along"]
    terms = blocks[0][0], twos[0], ones[0], along[1], along[3]
    keep, give = halves(place, *terms)
    return *deliver(place, keep, lax.ppermute(give, every, core_pairs()), conv_rows, head_cols, gains), input_grad


def shards(
    features,
    conv_master,
    head_master,
    scale_master,
    join_master,
    affine_scale,
    affine_shift,
    head_cotangent,
    pool_cotangent,
    box_counts,
    proposals,
):
    images, rows, cols, depth = features.shape
    total = head_master.shape[1]
    strip = Strip(rows, cols)
    every = ("dp", "space")
    own_gain, own_join = scale_master.shape[0], join_master.shape[0]
    staged = lax.axis_size("dp") == 8 and lax.axis_size("space") == 4
    line, rank = lax.axis_index("dp"), lax.axis_index("space")
    place = jnp.stack([rank, jnp.int32(lax.axis_size("space")), box_counts[0], line // 2, line % 2]).astype(jnp.int32)
    spread = jnp.asarray(spread_matrix(strip), bf16)
    x = features.reshape(rows * cols, depth)
    if staged:
        packed = pack(strip, conv_master, head_master, scale_master, join_master, x, spread.T)
        conv_rows = conv_master.shape[0]

        def begin(edges, blocks):
            return prepare(strip, place, x, edges, blocks, LAYERS * 9 * depth // conv_rows)

        conv_full = conv_rows, *staged_gather(every, *packed, begin)
    else:
        conv_full = lax.all_gather(conv_master.astype(bf16), every, axis=0, tiled=True)
        head_full = lax.all_gather(head_master.astype(bf16), every, axis=0, tiled=True)
        small = jnp.concatenate([scale_master, join_master]).astype(bf16)
        small = lax.all_gather(small[None], every, axis=0, tiled=True).astype(f32)
        small = jnp.concatenate([small[:, :own_gain].reshape(1, total), small[:, own_gain:].reshape(SCALES, total)], axis=0)
        means = []
        for s in range(1, SCALES):
            at = strip.starts(0)[s] - strip.starts(0)[1]
            pick = spread[:, at : at + strip.sizes(0)[s]]
            means.append((mm(pick, x, TN) * (0.25**s)).astype(bf16))
        x = with_rows(strip, [x] + means, "space")
    results = forward(strip, place, x, conv_full, affine_scale, affine_shift, total)
    if staged:
        p0, p1, p2, a3, small, conv_full, head_full, acts = results
    else:
        p0, p1, p2, a3, acts = results
    pre = p0, p1, p2
    maps, pool, sums, dz, first, final, *halves = head(
        strip, place, a3, head_full, small, head_cotangent.reshape(rows * cols, total), pool_cotangent, proposals,
        spread, affine_scale, p2, staged,
    )
    block_rows = LAYERS * 9 * depth
    if staged:
        swap = functools.partial(lax.ppermute, axis_name=every, perm=core_pairs())
        *halves, dg_keep, dg_give = halves
        others = swap(acts)
        block_rows = packed[0].shape[0] * 2
    else:
        (head_grad,), halves = halves, []
        conv_rows = None
    grad = None
    for layer in (2, 1, 0):
        above, below = from_neighbour(final, 1, "space"), from_neighbour(first, -1, "space")
        if staged:
            keep, give = halves
            pair = [acts, others], [keep, swap(give)]
        else:
            pair = [acts], [dz]
        *grad, token = weight_grad(strip, layer, place, *pair, grad, block_rows, conv_rows)
        if layer == 2 and staged:
            grad = chip_head_grad(place, acts, others, dg_keep, swap(dg_give), sums, pool, grad, conv_rows)
        more = [affine_scale, pre[layer - 1]] if layer else [spread]
        dz, *edge = data_grad(strip, layer, place, dz, above, below, conv_full, token, more, staged)
        if layer:
            first, final, *halves = edge
    input_grad = dz
    me = line * lax.axis_size("space") + rank
    if staged:
        conv_grad, head_grad, gain_grad, join_grad, pooled, input_grad = staged_scatter(
            every, [grad[4 * n : 4 * n + 4] for n in range(4)], place, conv_rows, total, own_gain, input_grad, above, below
        )
    else:
        pooled = lax.psum(pool, "space") / box_counts.astype(f32)[:, None]
        sums = lax.psum(sums, every)
        gain_grad = lax.dynamic_slice_in_dim(sums[0], me * own_gain, own_gain)
        join_grad = lax.dynamic_slice_in_dim(sums[1:].reshape(-1), me * own_join, own_join)
        conv_grad = lax.psum_scatter(grad[0], every, scatter_dimension=0, tiled=True).astype(f32)
        head_grad = lax.psum_scatter(head_grad, every, scatter_dimension=0, tiled=True).astype(f32)
    return (
        maps.reshape(images, rows, cols, total),
        pooled,
        input_grad.reshape(images, rows, cols, depth),
        conv_grad,
        head_grad,
        gain_grad.reshape(-1),
        join_grad.reshape(-1),
    )


def solution(mesh):
    return jax.shard_map(
        shards,
        mesh=mesh,
        in_specs=(
            P("dp", "space", None, None),
            P(("dp", "space"), None),
            P(("dp", "space"), None),
            P(("dp", "space")),
            P(("dp", "space")),
            P(),
            P(),
            P("dp", "space", None, None),
            P("dp", None),
            P("dp"),
            P("dp", None),
        ),
        out_specs=(
            P("dp", "space", None, None),
            P("dp", None),
            P("dp", "space", None, None),
            P(("dp", "space"), None),
            P(("dp", "space"), None),
            P(("dp", "space")),
            P(("dp", "space")),
        ),
        check_vma=False,
    )
```

```python
import functools
import math

import jax
import jax.numpy as jnp
import numpy as np
from jax import lax
from jax.experimental import pallas as pl
from jax.experimental.pallas import tpu as pltpu
from jax.sharding import PartitionSpec as P

HEAD_CH = 256
TASK_HEADS = 7
SCALES = 3
LAYERS = 3
PAD = 8

epsilon = 1e-06
f32 = jnp.float32
bf16 = jnp.bfloat16
NN = (((1,), (0,)), ((), ()))
NT = (((1,), (1,)), ((), ()))
TN = (((0,), (0,)), ((), ()))


def mm(left, right, dims=NN):
    return lax.dot_general(left, right, dims, preferred_element_type=f32)


def split_mm(left, right):
    high = right.astype(bf16)
    low = (right - high.astype(f32)).astype(bf16)
    return mm(left, high) + mm(left, low)


class Strip:
    def __init__(self, rows, cols):
        self.rows = [rows >> s for s in range(SCALES)]
        self.cols = [cols >> s for s in range(SCALES)]

    def sizes(self, halo):
        return [(r + 2 * halo) * c for r, c in zip(self.rows, self.cols)]

    def starts(self, halo):
        sizes = self.sizes(halo)
        return [sum(sizes[:s]) for s in range(SCALES)]

    def total(self, halo):
        return sum(self.sizes(halo))

    def own(self, halo):
        return [st + halo * c for st, c in zip(self.starts(halo), self.cols)]


def spread_matrix(strip):
    rows, cols = strip.rows[0], strip.cols[0]
    parts = []
    for s in range(1, SCALES):
        mat = np.zeros((rows * cols, strip.rows[s] * strip.cols[s]), np.float32)
        for r in range(rows):
            for c in range(cols):
                mat[r * cols + c, (r >> s) * strip.cols[s] + (c >> s)] = 1.0
        parts.append(mat)
    return np.concatenate(parts, axis=1)


def column_of(strip, scale, count):
    return lax.broadcasted_iota(jnp.int32, (count, 1), 0) % strip.cols[scale]


def shifted_copies(strip, halo, act, wide, depth):
    for s in range(SCALES):
        start, count, cols = strip.starts(halo)[s], strip.sizes(halo)[s], strip.cols[s]
        column = column_of(strip, s, count)
        for k in range(3):
            rows = act[PAD + start + k - 1 : PAD + start + k - 1 + count, :]
            if k == 0:
                rows = jnp.where(column == 0, 0.0, rows)
            if k == 2:
                rows = jnp.where(column == cols - 1, 0.0, rows)
            wide[start : start + count, k * depth : (k + 1) * depth] = rows.astype(bf16)


def patches(strip, halo, wide, cells, depth, flip=False, base=0):
    for s in range(SCALES):
        cols = strip.cols[s]
        count = strip.sizes(halo)[s]
        source, target = strip.starts(halo + 1)[s], strip.starts(halo)[s]
        for ky in range(3):
            first = source + (2 - ky if flip else ky) * cols
            for kx in range(3):
                col = (2 - kx if flip else kx) * depth
                tap = 3 * ky + kx
                cells[base + target : base + target + count, tap * depth : (tap + 1) * depth] = wide[
                    first : first + count, col : col + depth
                ]


FLIPS = ((1, 2), (2, 1))
TURNS = (0, 1, 3, 2)
GROUPS = (((0, 1, 2, 3),),) * 2 + (((0, 1, 2), (3,)), ((0,), (1,), (2,), (3,)))
SWAPS = {2: ((0, GROUPS[0][0]),), 3: ((1, GROUPS[1][0]), (2, GROUPS[2][0]), (3, GROUPS[3][0])), 4: ((2, GROUPS[2][1]), (3, GROUPS[3][1]), (3, GROUPS[3][2]))}
ITEMS = tuple(
    item
    for n in range(4)
    for item in [(n, True, (part,)) for part in range(4)] + [(n, False, group) for group in GROUPS[n]]
)


def across(place, part, core):
    rank = place[0]
    for bit in range(2):
        if part >> bit & 1:
            rank = rank ^ jnp.where(core == 0, FLIPS[0][bit], FLIPS[1][bit])
    return rank


def load_blocks(conv_rows, place, refs, weights, head_w, sem):
    depth = weights.shape[1]
    pieces, rows = head_w.shape[:2]
    head_rows = rows * conv_rows // weights.shape[0]
    layer_rows = weights.shape[0] // LAYERS
    last = [-(-layer_rows * (n + 1) // conv_rows) for n in range(LAYERS)]
    blocks = []
    for (n, own, parts), ref in zip(ITEMS, refs):
        core = place[4] if own else 1 - place[4]
        z = (place[3] + 4 - TURNS[n]) % 4
        for at, part in enumerate(parts):
            block = ref if len(parts) == 1 else ref.at[at]
            blocks.append((block, (z * 2 + core) * 4 + across(place, part, core)))
    for layer in range(LAYERS):
        for block, k in blocks:
            copy = pltpu.make_async_copy(
                block.at[pl.ds(0, conv_rows), :],
                weights.at[pl.ds(pl.multiple_of(k * conv_rows, 16), conv_rows), :],
                sem.at[layer],
            )
            inside = k < last[layer]
            if layer:
                inside = inside & (k >= last[layer - 1])
            pl.when(inside)(copy.start)
    for block, k in blocks:
        pltpu.make_async_copy(
            block.at[pl.ds(conv_rows, pieces * head_rows), :].reshape(pieces, head_rows, depth),
            head_w.at[:, pl.ds(pl.multiple_of(k * head_rows, 16), head_rows), :],
            sem.at[LAYERS],
        ).start()
    waits = []
    for first, stop in zip([0] + last, last):
        rows = weights.at[pl.ds(first * conv_rows, (stop - first) * conv_rows), :]
        waits.append(pltpu.make_async_copy(rows, rows, sem.at[len(waits)]))
    return waits + [pltpu.make_async_copy(head_w, head_w, sem.at[LAYERS])]


def prepare_kernel(strip, depth, place, x_ref, above_ref, below_ref, *refs):
    blocks, (cells, acts_ref, token, strips, act, wide, x_sem) = refs[:4], refs[4:]
    strips[...] = jnp.zeros(strips.shape, bf16)
    coarse = strips.shape[1]
    fetches = []
    for part in range(4):
        copy = pltpu.make_async_copy(
            blocks[part].at[pl.ds(blocks[part].shape[0] - coarse, coarse), :],
            strips.at[3 + across(place, part, place[4])],
            x_sem.at[part],
        )
        copy.start()
        fetches.append(copy)
    token[...] = jnp.zeros(token.shape, f32)
    at = PAD
    for ref in (above_ref, x_ref, below_ref):
        act[at : at + ref.shape[0], :] = ref[...].astype(f32)
        at += ref.shape[0]
    for copy in fetches:
        copy.wait()
    for s in range(1, SCALES):
        rows, cols = strip.rows[s], strip.cols[s]
        first = strip.starts(0)[s] - strip.starts(0)[1]
        for row in range(-3, rows + 3):
            source = strips[place[0] + 3 + row // rows, first + row % rows * cols : first + (row % rows + 1) * cols, :]
            act[at : at + cols, :] = source.astype(f32)
            at += cols
    first_patches(strip, depth, act, wide, cells, acts_ref)


def first_patches(strip, depth, act, wide, cells, acts_ref):
    for s in range(SCALES):
        start, size = strip.starts(1)[s], strip.sizes(1)[s]
        first = PAD + strip.starts(3)[s] + 2 * strip.cols[s]
        acts_ref[start : start + size, :] = act[first : first + size, :].astype(bf16)
    shifted_copies(strip, LAYERS, act, wide, depth)
    patches(strip, LAYERS - 1, wide, cells, depth)


def pack_kernel(strip, conv_ref, head_ref, gain_ref, join_ref, x_ref, gather_ref, own_ref, wide_ref, top_ref, bottom_ref):
    depth = conv_ref.shape[1]
    at = conv_ref.shape[0]
    rows, head_cols = head_ref.shape
    for ref in (own_ref, wide_ref):
        ref[:at, :] = conv_ref[...].astype(bf16)
    for first in range(0, head_cols, depth):
        width = min(depth, head_cols - first)
        piece = head_ref[:, first : first + width]
        if width < depth:
            small = jnp.concatenate([gain_ref[...], join_ref[...]], axis=1)
            small = jnp.concatenate([small, jnp.zeros((1, depth - width - small.shape[1]), f32)], axis=1)
            row = lax.broadcasted_iota(jnp.int32, (rows, depth - width), 0)
            small = jnp.where(row == 0, jnp.broadcast_to(small, (rows, depth - width)), 0.0)
            piece = jnp.concatenate([piece, small], axis=1)
        for ref in (own_ref, wide_ref):
            ref[at : at + rows, :] = piece.astype(bf16)
        at += rows
    x = x_ref[...]
    sums = mm(gather_ref[...], x)
    for s in range(1, SCALES):
        first = strip.starts(0)[s] - strip.starts(0)[1]
        size = strip.sizes(0)[s]
        wide_ref[at : at + size, :] = (sums[first : first + size] * (0.25**s)).astype(bf16)
        at += size
    edge = 3 * strip.cols[0]
    top_ref[...] = x_ref[:edge, :]
    bottom_ref[...] = x_ref[x.shape[0] - edge :, :]


def forward_kernel(strip, depth, staged, place, scale_ref, shift_ref, *refs):
    taps = 9 * depth
    halos = [LAYERS - 1 - layer for layer in range(LAYERS)]
    if staged:
        conv_rows, head_cols = staged
        expand_hbm, owner_ref, first_cells, *refs = refs
        blocks, refs = refs[: len(ITEMS)], refs[len(ITEMS) :]
        first_acts, refs = refs[0], refs[1:]
        p_refs, refs = refs[:3], refs[3:]
        a3_ref, small_ref, weights, head_ref, acts_ref, act, wide, cells, expand, sem = refs
        loads = load_blocks(conv_rows, place, blocks, weights, head_ref, sem)
        expand_load = pltpu.make_async_copy(expand_hbm, expand, sem.at[LAYERS + 1])
        expand_load.start()
        acts_ref[: first_acts.shape[0], :] = first_acts[...]
    else:
        x_ref, w_hbm, *refs = refs
        p_refs, refs = refs[:3], refs[3:]
        a3_ref, acts_ref, weights, act, wide, cells, sem = refs
        load = pltpu.make_async_copy(w_hbm, weights, sem.at[0])
        load.start()
        act[PAD : PAD + strip.total(3), :] = x_ref[...].astype(f32)
        first_cells = cells
        first_patches(strip, depth, act, wide, cells, acts_ref)
        load.wait()
    here, ranks = place[0], place[1]
    flat = strip.starts(0)
    for layer, halo in enumerate(halos):
        count = strip.total(halo)
        if layer:
            shifted_copies(strip, halo + 1, act, wide, depth)
            patches(strip, halo, wide, cells, depth)
        used = cells if layer else first_cells
        own = strip.own(halo)
        if staged:
            loads[layer].wait()
        for half in range(depth // 256):
            lanes = slice(half * 256, (half + 1) * 256)
            z = mm(used[:count, :], weights[layer * taps : (layer + 1) * taps, lanes])
            p = z * scale_ref[layer : layer + 1, lanes] + shift_ref[layer : layer + 1, lanes]
            a = (p / (1.0 + jnp.exp(-p))).astype(bf16)
            for s in range(SCALES):
                size = strip.sizes(0)[s]
                p_refs[layer][flat[s] : flat[s] + size, lanes] = p[own[s] : own[s] + size]
            if layer == LAYERS - 1:
                a3_ref[:, lanes] = a
                acts_ref[LAYERS * strip.total(1) :, lanes] = a
            else:
                for s in range(SCALES):
                    start, size = strip.starts(halo)[s], strip.sizes(halo)[s]
                    row = lax.broadcasted_iota(jnp.int32, (size, 1), 0) // strip.cols[s]
                    row = row + here * strip.rows[s] - halo
                    inside = (row >= 0) & (row < ranks * strip.rows[s])
                    kept = jnp.where(inside, a[start : start + size].astype(f32), 0.0)
                    act[PAD + start : PAD + start + size, lanes] = kept
                    edge = (halo - 1) * strip.cols[s]
                    first, size = (layer + 1) * strip.total(1) + strip.starts(1)[s], strip.sizes(1)[s]
                    acts_ref[first : first + size, lanes] = kept[edge : edge + size].astype(bf16)
    if staged:
        loads[LAYERS].wait()
        expand_load.wait()
        owners, spare = owner_ref.shape[0], expand.shape[0]
        pieces, depth_rows = head_ref.shape[:2]
        row = lax.broadcasted_iota(jnp.int32, (owners, depth_rows), 0)
        col = lax.broadcasted_iota(jnp.int32, (owners, depth_rows), 1)
        pick = jnp.where(col == row * (depth_rows // owners), 1.0, 0.0).astype(bf16)
        picked = mm(pick, head_ref[pieces - 1, :, depth - spare :]).astype(bf16)
        for n in range(1 + SCALES):
            cols = slice(n * head_cols, (n + 1) * head_cols)
            spread = mm(picked, expand[:, cols]) * owner_ref[:, cols].astype(f32)
            small_ref[n : n + 1, :] = jnp.sum(spread, axis=0, keepdims=True)


def slope(p):
    sigma = 1.0 / (1.0 + jnp.exp(-p))
    return sigma * (1.0 + p * (1.0 - sigma))


def head_kernel(
    strip, split, place, a3_ref, w_ref, small_ref, cot_ref, pool_cot_ref, where_ref, spread_ref, gather_ref,
    scale_ref, p2_ref, maps_ref, pool_ref, sums_ref, *refs,
):
    if split:
        *grads, keep_ref, give_ref, dg_all = refs
    else:
        *grads, w_grad_ref, dg_all = refs
    fine = strip.sizes(0)[0]
    starts, sizes = strip.starts(0), strip.sizes(0)
    parts = [slice(starts[s], starts[s] + sizes[s]) for s in range(SCALES)]
    slots = where_ref.shape[1]
    pixel = lax.broadcasted_iota(jnp.int32, (fine, slots), 0) + place[0] * fine
    slot = lax.broadcasted_iota(jnp.int32, (fine, slots), 1)
    hits = jnp.where((where_ref[...] == pixel) & (slot < place[2]), 1.0, 0.0)
    hits = jnp.sum(hits, axis=-1, keepdims=True)
    share = pool_cot_ref[...] / place[2].astype(f32)
    heads = maps_ref.shape[1] // HEAD_CH
    depth = a3_ref.shape[1]
    per = depth // HEAD_CH
    da3 = None
    for head in range(heads):
        lanes = slice(head * HEAD_CH, (head + 1) * HEAD_CH)
        if split:
            weight = w_ref[head // per, :, head % per * HEAD_CH : (head % per + 1) * HEAD_CH]
        else:
            weight = w_ref[:, lanes]
        g = mm(a3_ref[...], weight)
        inverse = lax.rsqrt(jnp.sum(g * g, axis=-1, keepdims=True) + epsilon)
        unit = g * inverse
        gain = small_ref[0:1, lanes]
        join = [small_ref[1 + s : 2 + s, lanes] for s in range(SCALES)]
        normed = unit * gain
        coarse = jnp.concatenate([normed[parts[s]] * join[s] for s in range(1, SCALES)], axis=0)
        joined = normed[:fine] * join[0] + split_mm(spread_ref[...], coarse)
        maps_ref[:, lanes] = joined.astype(bf16)
        fused = cot_ref[:, lanes]
        if head == 0:
            pool_ref[...] = jnp.sum(joined * hits, axis=0, keepdims=True)
            fused = fused.astype(f32) + hits * share
            down_coarse = split_mm(gather_ref[...], fused)
        else:
            down_coarse = mm(gather_ref[...], fused)
        down = jnp.concatenate([fused.astype(f32), down_coarse], axis=0)
        product = down * normed
        scaled = []
        for s in range(SCALES):
            sums_ref[s + 1 : s + 2, lanes] = jnp.sum(product[parts[s]], axis=0, keepdims=True)
            scaled.append(down[parts[s]] * join[s])
        dn = jnp.concatenate(scaled, axis=0)
        sums_ref[0:1, lanes] = jnp.sum(dn * unit, axis=0, keepdims=True)
        du = dn * gain
        dg = (inverse * (du - unit * jnp.sum(du * unit, axis=-1, keepdims=True))).astype(bf16)
        dg_all[head] = dg
        if not split:
            w_grad_ref[:, lanes] = mm(a3_ref[...], dg, TN).astype(bf16)
        part = mm(dg, weight, NT)
        da3 = part if da3 is None else da3 + part
    layer = LAYERS - 1
    dz = da3 * scale_ref[layer : layer + 1, :] * slope(p2_ref[...])
    emit_grad(strip, place, dz.astype(bf16), *grads)
    if split:
        width = HEAD_CH
        first = place[4] == 0
        half = heads * width // 2
        for start in range(0, half, width // 2):
            left = dg_all[start // width, :, start % width : start % width + width // 2]
            at = half + start
            right = dg_all[at // width, :, at % width : at % width + width // 2]
            keep_ref[:, start : start + width // 2] = jnp.where(first, left, right)
            give_ref[:, start : start + width // 2] = jnp.where(first, right, left)


def emit_grad(strip, place, dz, dz_ref, first_ref, last_ref, keep_ref=None, give_ref=None):
    dz_ref[...] = dz
    edge = 0
    odd = place[0] % 2 == 1
    for start, size, cols in zip(strip.starts(0), strip.sizes(0), strip.cols):
        first, last = dz[start : start + cols], dz[start + size - cols : start + size]
        first_ref[edge : edge + cols, :] = jnp.where(odd, first, last)
        last_ref[edge : edge + cols, :] = jnp.where(odd, last, first)
        edge += cols
    if keep_ref is not None:
        middle = dz.shape[1] // 2
        left, right = dz[:, :middle], dz[:, middle:]
        first = place[4] == 0
        keep_ref[...] = jnp.where(first, left, right)
        give_ref[...] = jnp.where(first, right, left)


def store_blocks(place, pieces, block_refs, sem):
    for turn in range(4):
        for part in range(4):
            out = block_refs[4 * turn + part]
            z = (place[3] + turn) % 4
            rank = across(place, part, place[4])
            for core in range(2):
                k = (z * 2 + core) * 4 + rank
                base = core * (out.shape[0] // 2)
                for condition, source, row in pieces(k):
                    target = out.at[pl.ds(base + row, math.prod(source.shape[:-1])), :]
                    if len(source.shape) > 2:
                        target = target.reshape(source.shape)
                    copy = pltpu.make_async_copy(source, target, sem)
                    if condition is None:
                        copy.start()
                    else:
                        pl.when(condition)(copy.start)


def weight_grad_kernel(strip, depth, layer, images, conv_rows, place, *refs):
    acts, grads = refs[:images], refs[images : 2 * images]
    *outs, token, act, wide, cells, dz, result, sem = refs[2 * images :]
    own, count = strip.total(0), strip.total(1)
    for n in range(images):
        act[PAD : PAD + count, :] = acts[n][layer * count : (layer + 1) * count, :].astype(f32)
        shifted_copies(strip, 1, act, wide, depth)
        patches(strip, 0, wide, cells, depth, base=n * own)
        dz[n * own : (n + 1) * own, :] = grads[n][...]
    for tap in range(9):
        lanes = slice(tap * depth, (tap + 1) * depth)
        result[lanes, :] = mm(cells[:, lanes], dz[...], TN).astype(bf16)
    rows = 9 * depth
    first_row, stop_row = layer * rows, (layer + 1) * rows
    token[...] = jnp.zeros(token.shape, f32)
    if conv_rows is None:
        copy = pltpu.make_async_copy(result, outs[-1].at[pl.ds(first_row, rows), :], sem)
        copy.start()
        copy.wait()
        return

    def pieces(k):
        out = []
        inside = (k * conv_rows >= first_row) & ((k + 1) * conv_rows <= stop_row)
        start = jnp.where(inside, k * conv_rows - first_row, 0)
        out.append((inside, result.at[pl.ds(pl.multiple_of(start, 16), conv_rows), :], 0))
        if first_row % conv_rows:
            size = conv_rows - first_row % conv_rows
            out.append((k == first_row // conv_rows, result.at[pl.ds(0, size), :], conv_rows - size))
        if stop_row % conv_rows:
            size = stop_row % conv_rows
            out.append((k == stop_row // conv_rows, result.at[pl.ds(rows - size, size), :], 0))
        return out

    store_blocks(place, pieces, outs[-16:], sem)
    pltpu.make_async_copy(result, result, sem).wait()


def chip_head_grad_kernel(conv_rows, place, a3_ref, other_ref, keep_ref, got_ref, sums_ref, pool_ref, owner_ref, expand, *refs):
    refs = refs[-(16 + 4) :]
    outs, (a3, dg, result, out_sem) = refs[:16], refs[16:]
    own = keep_ref.shape[0]
    for n, ref in enumerate((a3_ref, other_ref)):
        pltpu.make_async_copy(ref.at[pl.ds(ref.shape[0] - own, own), :], a3.at[pl.ds(n * own, own), :], out_sem).start()
    pltpu.make_async_copy(a3, a3, out_sem).wait()
    dg[:own, :] = keep_ref[...]
    dg[own:, :] = got_ref[...]
    width = result.shape[2]
    cols = dg.shape[1]
    for piece in range(result.shape[0]):
        stop = min(cols, (piece + 1) * width)
        lanes = slice(piece * width, stop)
        result[piece, :, : stop - piece * width] = mm(a3[...], dg[:, lanes], TN).astype(bf16)
    owners, depth_rows, spare = owner_ref.shape[0], result.shape[1], width - cols % width
    small = None
    for n in range(sums_ref.shape[0]):
        lanes = slice(n * sums_ref.shape[1], (n + 1) * sums_ref.shape[1])
        each = (sums_ref[n : n + 1, :] * owner_ref[:, lanes].astype(f32)).astype(bf16)
        term = mm(each, expand[:, lanes], NT)
        small = term if small is None else small + term
    row = lax.broadcasted_iota(jnp.int32, (depth_rows, owners), 0)
    col = lax.broadcasted_iota(jnp.int32, (depth_rows, owners), 1)
    tail = None
    for n in range(small.shape[1] // spare):
        pick = jnp.where(row == col * (depth_rows // owners) + n, 1.0, 0.0).astype(bf16)
        term = mm(pick, small[:, n * spare : (n + 1) * spare].astype(bf16))
        tail = term if tail is None else tail + term
    row = lax.broadcasted_iota(jnp.int32, (depth_rows, spare), 0)
    each = depth_rows // owners
    mine = row // (each * 4) == place[3] * 2 + place[4]
    for n in range(2):
        here = mine & (row % each == 2 + 2 * place[0] + n)
        tail = jnp.where(here, pool_ref[:, n * spare : (n + 1) * spare], tail)
    result[result.shape[0] - 1, :, cols % width :] = tail.astype(bf16)
    rows = (outs[0].shape[0] // 2 - conv_rows) // result.shape[0]

    def pieces(k):
        return [(None, result.at[:, pl.ds(pl.multiple_of(k * rows, 16), rows), :], conv_rows)]

    store_blocks(place, pieces, outs, out_sem)
    pltpu.make_async_copy(result, result, out_sem).wait()


def halves_kernel(place, *refs):
    *terms, keep_ref, give_ref = refs
    whole = total_of(*[t[...] for t in terms])
    half = keep_ref.shape[0]
    first = place[4] == 0
    keep_ref[...] = jnp.where(first, whole[:half], whole[half:])
    give_ref[...] = jnp.where(first, whole[half:], whole[:half])


def deliver_kernel(place, keep_ref, got_ref, conv_ref, head_ref, gain_ref, join_ref, pool_ref):
    first = place[4] == 0
    keep, got = keep_ref[...], got_ref[...]
    width = keep.shape[1]
    rows = head_ref.shape[0]
    half = head_ref.shape[1] // 2
    for n, side in enumerate((jnp.where(first, keep, got), jnp.where(first, got, keep))):
        conv_ref[:, n * width : (n + 1) * width] = side[: conv_ref.shape[0]]
        at = conv_ref.shape[0]
        for col in range(0, half, width):
            size = min(width, half - col)
            head_ref[:, n * half + col : n * half + col + size] = side[at : at + rows, :size]
            at += rows
    lanes = half % width
    small = (keep + got)[at - rows : at, lanes:]
    pooled = None
    for s in range(4):
        term = jnp.concatenate([small[2 + 2 * s : 3 + 2 * s], small[3 + 2 * s : 4 + 2 * s]], axis=1)
        pooled = term if pooled is None else pooled + term
    pool_ref[...] = pooled / place[2].astype(f32)
    small = jnp.concatenate([small[n : n + 1] for n in range(2)], axis=1)
    gains = gain_ref.shape[1]
    gain_ref[...] = small[:, :gains]
    join_ref[...] = small[:, gains : gains + join_ref.shape[1]]


def data_grad_kernel(
    strip, depth, layer, place, dz_ref, above_ref, below_ref, w_ref, _, *refs
):
    refs, (act, wide, cells) = refs[:-3], refs[-3:]
    last = layer == 0
    if last:
        spread_ref, out_ref = refs
    else:
        scale_ref, p_ref, *outs = refs
    edge = 0
    odd = place[0] % 2 == 1
    for s in range(SCALES):
        start, size, cols = strip.starts(1)[s], strip.sizes(0)[s], strip.cols[s]
        flat = strip.starts(0)[s]
        near, far = above_ref[edge : edge + cols, :], below_ref[edge : edge + cols, :]
        act[PAD + start : PAD + start + cols, :] = jnp.where(odd, near, far).astype(f32)
        act[PAD + start + cols : PAD + start + cols + size, :] = dz_ref[flat : flat + size, :].astype(f32)
        act[PAD + start + cols + size : PAD + start + 2 * cols + size, :] = jnp.where(odd, far, near).astype(f32)
        edge += cols
    shifted_copies(strip, 1, act, wide, depth)
    patches(strip, 0, wide, cells, depth, flip=True)
    base = layer * 9 * depth
    value = None
    for tap in range(9):
        term = mm(
            cells[:, tap * depth : (tap + 1) * depth], w_ref[base + tap * depth : base + (tap + 1) * depth, :], NT
        )
        value = term if value is None else value + term
    if last:
        fine = strip.sizes(0)[0]
        coarse = jnp.concatenate(
            [
                value[st : st + size] * (0.25**s)
                for s, (st, size) in enumerate(zip(strip.starts(0), strip.sizes(0)))
                if s
            ],
            axis=0,
        )
        out_ref[...] = value[:fine] + split_mm(spread_ref[...], coarse)
    else:
        dz = value * scale_ref[layer - 1 : layer, :] * slope(p_ref[...])
        emit_grad(strip, place, dz.astype(bf16), *outs)


def vmem(shape=None, index=None):
    if shape is None:
        return pl.BlockSpec(memory_space=pltpu.VMEM)
    return pl.BlockSpec(shape, index)


SMEM = pl.BlockSpec(memory_space=pltpu.SMEM)
ANY = pl.BlockSpec(memory_space=pl.ANY)


def params(mebibytes):
    return pltpu.CompilerParams(vmem_limit_bytes=mebibytes << 20)


def small_layout(owners, cols, spare):
    gains = cols // owners
    expand = np.zeros((spare, (1 + SCALES) * cols), np.float32)
    owner = np.zeros((owners, (1 + SCALES) * cols), np.float32)
    for n in range((1 + SCALES) * cols):
        size = gains if n < cols else SCALES * gains
        at = n if n < cols else n - cols
        expand[at % size + (0 if n < cols else gains), n] = 1.0
        owner[at // size, n] = 1.0
    return jnp.asarray(expand, bf16), jnp.asarray(owner, bf16)


def pack(strip, conv, head_w, gain, join, x, gather):
    depth = conv.shape[1]
    rows = conv.shape[0] + head_w.shape[0] * -(-head_w.shape[1] // depth)
    edge = 3 * strip.cols[0]
    return pl.pallas_call(
        functools.partial(pack_kernel, strip),
        name="pack",
        out_shape=[jax.ShapeDtypeStruct((n, depth), bf16) for n in (rows, rows + gather.shape[0], edge, edge)],
        in_specs=[vmem()] * 6,
        out_specs=[vmem()] * 4,
        compiler_params=params(60),
    )(conv, head_w, gain[None], join[None], x, gather)


def on_chip(values):
    return [pltpu.with_memory_space_constraint(v, pltpu.MemorySpace.VMEM) for v in values]


def off_chip(values):
    return [pltpu.with_memory_space_constraint(v, pltpu.MemorySpace.HBM) for v in values]


def forward_scratch(strip, depth, halo):
    return [
        pltpu.VMEM((strip.total(halo) + 2 * PAD, depth), f32),
        pltpu.VMEM((strip.total(halo), 3 * depth), bf16),
    ]


def prepare(strip, place, x, edges, blocks, owners):
    depth = x.shape[1]
    coarse = strip.total(0) - strip.sizes(0)[0]
    return pl.pallas_call(
        functools.partial(prepare_kernel, strip, depth),
        name="prepare",
        out_shape=[
            pltpu.VMEM((strip.total(LAYERS - 1), 9 * depth), bf16),
            pltpu.VMEM((strip.total(1), depth), bf16),
            jax.ShapeDtypeStruct((8, 128), f32),
        ],
        in_specs=[SMEM] + [vmem()] * 3 + [ANY] * len(blocks),
        out_specs=[vmem()] * 3,
        scratch_shapes=[pltpu.VMEM((6 + owners // 8, coarse, depth), bf16)]
        + forward_scratch(strip, depth, LAYERS)
        + [pltpu.SemaphoreType.DMA((4,))],
        compiler_params=params(10),
    )(place, x, *edges, *off_chip(blocks))


def forward(strip, place, x, conv, scale, shift, head_cols):
    depth = scale.shape[1]
    own = strip.total(0)
    rows = LAYERS * 9 * depth
    acts = (LAYERS * strip.total(1) + own, depth)
    staged = isinstance(conv, tuple)
    cells = pltpu.VMEM((strip.total(1 if staged else LAYERS - 1), 9 * depth), bf16)
    if staged:
        conv_rows, prepared, blocks = conv
        expand, owner = small_layout(rows // conv_rows, head_cols, -head_cols % depth)
        first_cells, first_acts = on_chip(prepared)
        inputs = [expand, owner, first_cells, *off_chip(blocks), first_acts]
        in_specs = [ANY, vmem(), vmem()] + [ANY] * len(blocks) + [vmem()]
        outs = [pltpu.VMEM((own, depth), f32)] * 3 + [
            pltpu.VMEM((own, depth), bf16),
            pltpu.VMEM((1 + SCALES, head_cols), f32),
            pltpu.VMEM((rows, depth), bf16),
            pltpu.VMEM((-(-head_cols // depth), depth, depth), bf16),
            pltpu.VMEM(acts, bf16),
        ]
        scratch = forward_scratch(strip, depth, LAYERS - 1)
        scratch += [cells, pltpu.VMEM(expand.shape, bf16), pltpu.SemaphoreType.DMA((LAYERS + 2,))]
    else:
        inputs, in_specs = [x, conv], [vmem(), ANY]
        outs = [jax.ShapeDtypeStruct((own, depth), f32)] * 3
        outs += [jax.ShapeDtypeStruct(shape, bf16) for shape in ((own, depth), acts)]
        scratch = [pltpu.VMEM((rows, depth), bf16)] + forward_scratch(strip, depth, LAYERS)
        scratch += [cells, pltpu.SemaphoreType.DMA((1,))]
    return pl.pallas_call(
        functools.partial(forward_kernel, strip, depth, (conv_rows, head_cols) if staged else None),
        name="forward",
        out_shape=outs,
        in_specs=[SMEM, vmem(), vmem()] + in_specs,
        out_specs=[vmem()] * len(outs),
        scratch_shapes=scratch,
        compiler_params=params(28 if staged else 54),
    )(place, scale, shift, *inputs)


def head(strip, place, a3, weight, small, cot, pool_cot, where, spread, scale, p2, split):
    own, depth = a3.shape
    total = small.shape[1]
    fine = strip.sizes(0)[0]
    edge = sum(strip.cols)
    outs = [
        jax.ShapeDtypeStruct((fine, total), bf16),
        jax.ShapeDtypeStruct((1, HEAD_CH), f32),
        jax.ShapeDtypeStruct((1 + SCALES, total), f32),
    ]
    outs += [jax.ShapeDtypeStruct((n, depth), bf16) for n in (own, edge, edge)]
    if split:
        outs += [jax.ShapeDtypeStruct((own, n // 2), bf16) for n in (depth, depth, total, total)]
    else:
        outs += [jax.ShapeDtypeStruct((depth, total), bf16)]
    return pl.pallas_call(
        functools.partial(head_kernel, strip, split),
        name="heads",
        out_shape=outs,
        in_specs=[SMEM] + [vmem()] * 10,
        out_specs=[vmem()] * len(outs),
        scratch_shapes=[pltpu.VMEM((total // HEAD_CH, own, HEAD_CH), bf16)],
        compiler_params=params(24),
    )(place, a3, weight, small, cot, pool_cot, where, spread, spread.T, scale, p2)


def weight_grad(strip, layer, place, acts, grads, into, rows, conv_rows):
    own, half = grads[0].shape
    depth = acts[0].shape[1]
    images = len(acts)
    count_here = strip.total(1)
    into = into or []
    count = 1 if conv_rows is None else 16
    return pl.pallas_call(
        functools.partial(weight_grad_kernel, strip, depth, layer, images, conv_rows),
        name="weight_grad",
        out_shape=[pltpu.HBM((rows, half), bf16)] * count + [jax.ShapeDtypeStruct((8, 128), f32)],
        in_specs=[SMEM] + [vmem()] * (2 * images) + [ANY] * len(into),
        out_specs=[ANY] * count + [vmem()],
        scratch_shapes=[
            pltpu.VMEM((count_here + 2 * PAD, depth), f32),
            pltpu.VMEM((count_here, 3 * depth), bf16),
            pltpu.VMEM((images * own, 9 * depth), bf16),
            pltpu.VMEM((images * own, half), bf16),
            pltpu.VMEM((9 * depth, half), bf16),
            pltpu.SemaphoreType.DMA,
        ],
        input_output_aliases={1 + 2 * images + n: n for n in range(len(into))},
        compiler_params=params(22),
    )(place, *acts, *grads, *off_chip(into))


def chip_head_grad(place, a3, other, keep, got, sums, pool, blocks, conv_rows):
    own, depth = keep.shape[0], a3.shape[1]
    half = blocks[0].shape[1]
    expand, owner = small_layout(LAYERS * 9 * depth // conv_rows, sums.shape[1], -sums.shape[1] % depth)
    pieces = -(-keep.shape[1] // half)
    return pl.pallas_call(
        functools.partial(chip_head_grad_kernel, conv_rows),
        name="chip_head_grad",
        out_shape=[pltpu.HBM(b.shape, bf16) for b in blocks],
        in_specs=[SMEM, ANY, ANY] + [vmem()] * 6 + [ANY] * 16,
        out_specs=[ANY] * 16,
        scratch_shapes=[
            pltpu.VMEM((2 * own, depth), bf16),
            pltpu.VMEM((2 * own, keep.shape[1]), bf16),
            pltpu.VMEM((pieces, depth, half), bf16),
            pltpu.SemaphoreType.DMA,
        ],
        input_output_aliases={9 + n: n for n in range(16)},
        compiler_params=params(14),
    )(place, a3, other, keep, got, sums, pool, owner, expand, *off_chip(blocks))


def data_grad(strip, layer, place, dz, above, below, conv, token, others, split):
    if split:
        conv = pltpu.with_memory_space_constraint(conv, pltpu.MemorySpace.VMEM)
    own, depth = dz.shape
    last = layer == 0
    edge = sum(strip.cols)

    if last:
        outs = [jax.ShapeDtypeStruct((strip.sizes(0)[0], depth), f32)]
    else:
        outs = [jax.ShapeDtypeStruct((n, depth), bf16) for n in (own, edge, edge)]
        outs += [jax.ShapeDtypeStruct((own, depth // 2), bf16)] * (2 * split)
    return pl.pallas_call(
        functools.partial(data_grad_kernel, strip, depth, layer),
        name="data_grad",
        out_shape=outs,
        in_specs=[SMEM] + [vmem()] * 4 + [ANY] + [vmem()] * len(others),
        out_specs=[vmem()] * len(outs),
        scratch_shapes=[
            pltpu.VMEM((strip.total(1) + 2 * PAD, depth), f32),
            pltpu.VMEM((strip.total(1), 3 * depth), bf16),
            pltpu.VMEM((own, 9 * depth), bf16),
        ],
        compiler_params=params(14 if split else 32),
    )(place, dz, above, below, conv, token, *others)


def halves(place, *terms):
    rows, width = terms[0].shape
    return pl.pallas_call(
        halves_kernel,
        name="halves",
        out_shape=[jax.ShapeDtypeStruct((rows // 2, width), f32)] * 2,
        in_specs=[SMEM] + [vmem()] * len(terms),
        out_specs=[vmem()] * 2,
        compiler_params=params(16),
    )(place, *terms)


def deliver(place, keep, got, conv_rows, head_cols, gains):
    width = keep.shape[1]
    head_rows = (keep.shape[0] - conv_rows) // -(-(head_cols // 2) // width)
    return pl.pallas_call(
        deliver_kernel,
        name="deliver",
        out_shape=[
            jax.ShapeDtypeStruct((conv_rows, 2 * width), f32),
            jax.ShapeDtypeStruct((head_rows, head_cols), f32),
            jax.ShapeDtypeStruct((1, gains), f32),
            jax.ShapeDtypeStruct((1, SCALES * gains), f32),
            jax.ShapeDtypeStruct((1, HEAD_CH), f32),
        ],
        in_specs=[SMEM] + [vmem()] * 2,
        out_specs=[vmem()] * 5,
        compiler_params=params(8),
    )(place, keep, got)


def from_neighbour(cells, distance, axis):
    count = lax.axis_size(axis)
    pairs = [(i, i + distance) for i in range(count) if 0 <= i + distance < count]
    return lax.ppermute(cells, axis, pairs)


def with_partner(cells, first, axis):
    ranks = range(first, lax.axis_size(axis) - 1, 2)
    return lax.ppermute(cells, axis, [pair for i in ranks for pair in ((i, i + 1), (i + 1, i))])


def with_rows(strip, levels, axis):
    above = [[] for _ in levels]
    below = [[] for _ in levels]
    left = [3] * len(levels)
    distance = 1
    while max(left) > 0:
        take = [min(n, r) for n, r in zip(left, strip.rows)]
        tails = [v[v.shape[0] - t * c :] for v, t, c in zip(levels, take, strip.cols) if t]
        heads = [v[: t * c] for v, t, c in zip(levels, take, strip.cols) if t]
        got_tail = from_neighbour(jnp.concatenate(tails, axis=0), distance, axis)
        got_head = from_neighbour(jnp.concatenate(heads, axis=0), -distance, axis)
        at = 0
        for s, (t, c) in enumerate(zip(take, strip.cols)):
            if t:
                above[s].insert(0, got_tail[at : at + t * c])
                below[s].append(got_head[at : at + t * c])
                at += t * c
        left = [n - t for n, t in zip(left, take)]
        distance += 1
    return jnp.concatenate([v for s, own in enumerate(levels) for v in above[s] + [own] + below[s]], axis=0)


def after(value, *others):
    return lax.optimization_barrier((value,) + others)[0]


def turn_pairs(step):
    return [((z * 2 + c) * 4 + s, (((z + step) % 4) * 2 + c) * 4 + s) for z in range(4) for c in range(2) for s in range(4)]


def flip_pairs(which):
    return [((z * 2 + c) * 4 + s, (z * 2 + c) * 4 + (s ^ FLIPS[c][which])) for z in range(4) for c in range(2) for s in range(4)]


def core_pairs():
    return [((z * 2 + c) * 4 + s, (z * 2 + 1 - c) * 4 + s) for z in range(4) for c in range(2) for s in range(4)]


def staged_gather(every, own, wide, tops, bottoms, begin):
    def swap(n, parts):
        mine = lines, ones, twos, boths
        chosen = [mine[part][n] for part in parts]
        return lax.ppermute(jnp.stack(chosen) if len(parts) > 1 else chosen[0], every, core_pairs())

    lines, ones, twos, boths, swaps = [wide], [], [], [], [[] for _ in TURNS]
    ends = len(TURNS) - 1
    for turn in range(len(TURNS) + 1):
        fresh = {}
        if turn < len(TURNS):
            fresh["one"] = lax.ppermute(lines[turn], every, flip_pairs(0))
            fresh["two"] = lax.ppermute(lines[turn], every, flip_pairs(1))
        if turn < ends:
            step = TURNS[turn + 1]
            if step == 2:
                fresh["line"] = lax.ppermute(after(lines[1], *ones), every, turn_pairs(1))
            else:
                fresh["line"] = lax.ppermute(after(own, *ones) if ones else own, every, turn_pairs(step))
        if turn:
            fresh["both"] = lax.ppermute(ones[turn - 1], every, flip_pairs(1))
        for n, parts in SWAPS.get(turn, ()):
            swaps[n].append(swap(n, parts))
        if turn == ends:
            *prepared, fresh["token"] = begin(edges, [lines[0], ones[0], twos[0], boths[0]])
        if not turn:
            fresh["above"] = from_neighbour(bottoms, 1, "space")
            fresh["below"] = from_neighbour(tops, -1, "space")
        fresh = dict(zip(fresh, lax.optimization_barrier(tuple(fresh.values()))))
        if not turn:
            edges = [fresh["above"], fresh["below"]]
        if turn < len(TURNS):
            ones.append(fresh["one"])
            twos.append(fresh["two"])
        if turn < ends:
            lines.append(fresh["line"])
        if turn:
            boths.append(fresh["both"])
    swaps[ends].append(swap(ends, GROUPS[ends][-1]))
    mine = [lines, ones, twos, boths]
    groups = {(n, group): array for n in range(len(TURNS)) for group, array in zip(GROUPS[n], swaps[n])}
    return prepared, [mine[parts[0]][n] if own_side else groups[n, parts] for n, own_side, parts in ITEMS]


def total_of(*terms):
    return sum((t.astype(f32) for t in terms[1:]), terms[0].astype(f32))


def staged_scatter(every, blocks, place, conv_rows, head_cols, gains, input_grad, *hold):
    order = TURNS[::-1]
    boths, ones, twos, parts = {}, {}, {}, {}
    along = {}
    for n in range(len(order) + 1):
        fresh = {}
        if n < len(order):
            both = blocks[order[n]][3]
            fresh["both"] = lax.ppermute(both if n else after(both, *hold), every, flip_pairs(1))
        if n:
            turn = order[n - 1]
            fresh["two"] = lax.ppermute(blocks[turn][2], every, flip_pairs(1))
            fresh["one"] = lax.ppermute(total_of(blocks[turn][1], boths[turn]).astype(bf16), every, flip_pairs(0))
        if n >= 2:
            turn = order[n - 2]
            terms = [blocks[turn][0], twos[turn], ones[turn]]
            if turn == 1:
                terms.append(along[2])
            fresh["along"] = lax.ppermute(total_of(*terms).astype(bf16), every, turn_pairs(1 if turn == 2 else turn))
        if n == 1:
            fresh["input"] = input_grad
        loose = {key: fresh.pop(key) for key in ("two",) if key in fresh}
        fresh = dict(zip(fresh, lax.optimization_barrier(tuple(fresh.values())))) | loose
        input_grad = fresh.get("input", input_grad)
        if n < len(order):
            boths[order[n]] = fresh["both"]
        if n:
            ones[order[n - 1]], twos[order[n - 1]] = fresh["one"], fresh["two"]
        if n >= 2:
            along[order[n - 2]] = fresh["along"]
    terms = blocks[0][0], twos[0], ones[0], along[1], along[3]
    keep, give = halves(place, *terms)
    return *deliver(place, keep, lax.ppermute(give, every, core_pairs()), conv_rows, head_cols, gains), input_grad


def shards(
    features,
    conv_master,
    head_master,
    scale_master,
    join_master,
    affine_scale,
    affine_shift,
    head_cotangent,
    pool_cotangent,
    box_counts,
    proposals,
):
    images, rows, cols, depth = features.shape
    total = head_master.shape[1]
    strip = Strip(rows, cols)
    every = ("dp", "space")
    own_gain, own_join = scale_master.shape[0], join_master.shape[0]
    staged = lax.axis_size("dp") == 8 and lax.axis_size("space") == 4
    line, rank = lax.axis_index("dp"), lax.axis_index("space")
    place = jnp.stack([rank, jnp.int32(lax.axis_size("space")), box_counts[0], line // 2, line % 2]).astype(jnp.int32)
    spread = jnp.asarray(spread_matrix(strip), bf16)
    x = features.reshape(rows * cols, depth)
    if staged:
        packed = pack(strip, conv_master, head_master, scale_master, join_master, x, spread.T)
        conv_rows = conv_master.shape[0]

        def begin(edges, blocks):
            return prepare(strip, place, x, edges, blocks, LAYERS * 9 * depth // conv_rows)

        conv_full = conv_rows, *staged_gather(every, *packed, begin)
    else:
        conv_full = lax.all_gather(conv_master.astype(bf16), every, axis=0, tiled=True)
        head_full = lax.all_gather(head_master.astype(bf16), every, axis=0, tiled=True)
        small = jnp.concatenate([scale_master, join_master]).astype(bf16)
        small = lax.all_gather(small[None], every, axis=0, tiled=True).astype(f32)
        small = jnp.concatenate([small[:, :own_gain].reshape(1, total), small[:, own_gain:].reshape(SCALES, total)], axis=0)
        means = []
        for s in range(1, SCALES):
            at = strip.starts(0)[s] - strip.starts(0)[1]
            pick = spread[:, at : at + strip.sizes(0)[s]]
            means.append((mm(pick, x, TN) * (0.25**s)).astype(bf16))
        x = with_rows(strip, [x] + means, "space")
    results = forward(strip, place, x, conv_full, affine_scale, affine_shift, total)
    if staged:
        p0, p1, p2, a3, small, conv_full, head_full, acts = results
    else:
        p0, p1, p2, a3, acts = results
    pre = p0, p1, p2
    maps, pool, sums, dz, first, final, *halves = head(
        strip, place, a3, head_full, small, head_cotangent.reshape(rows * cols, total), pool_cotangent, proposals,
        spread, affine_scale, p2, staged,
    )
    block_rows = LAYERS * 9 * depth
    if staged:
        swap = functools.partial(lax.ppermute, axis_name=every, perm=core_pairs())
        *halves, dg_keep, dg_give = halves
        others = swap(acts)
        block_rows = packed[0].shape[0] * 2
    else:
        (head_grad,), halves = halves, []
        conv_rows = None
    grad = None
    for layer in (2, 1, 0):
        above, below = with_partner(first, 0, "space"), with_partner(final, 1, "space")
        if staged:
            keep, give = halves
            pair = [acts, others], [keep, swap(give)]
        else:
            pair = [acts], [dz]
        *grad, token = weight_grad(strip, layer, place, *pair, grad, block_rows, conv_rows)
        if layer == 2 and staged:
            grad = chip_head_grad(place, acts, others, dg_keep, swap(dg_give), sums, pool, grad, conv_rows)
        more = [affine_scale, pre[layer - 1]] if layer else [spread]
        dz, *edge = data_grad(strip, layer, place, dz, above, below, conv_full, token, more, staged)
        if layer:
            first, final, *halves = edge
    input_grad = dz
    me = line * lax.axis_size("space") + rank
    if staged:
        conv_grad, head_grad, gain_grad, join_grad, pooled, input_grad = staged_scatter(
            every, [grad[4 * n : 4 * n + 4] for n in range(4)], place, conv_rows, total, own_gain, input_grad, above, below
        )
    else:
        pooled = lax.psum(pool, "space") / box_counts.astype(f32)[:, None]
        sums = lax.psum(sums, every)
        gain_grad = lax.dynamic_slice_in_dim(sums[0], me * own_gain, own_gain)
        join_grad = lax.dynamic_slice_in_dim(sums[1:].reshape(-1), me * own_join, own_join)
        conv_grad = lax.psum_scatter(grad[0], every, scatter_dimension=0, tiled=True).astype(f32)
        head_grad = lax.psum_scatter(head_grad, every, scatter_dimension=0, tiled=True).astype(f32)
    return (
        maps.reshape(images, rows, cols, total),
        pooled,
        input_grad.reshape(images, rows, cols, depth),
        conv_grad,
        head_grad,
        gain_grad.reshape(-1),
        join_grad.reshape(-1),
    )


def solution(mesh):
    return jax.shard_map(
        shards,
        mesh=mesh,
        in_specs=(
            P("dp", "space", None, None),
            P(("dp", "space"), None),
            P(("dp", "space"), None),
            P(("dp", "space")),
            P(("dp", "space")),
            P(),
            P(),
            P("dp", "space", None, None),
            P("dp", None),
            P("dp"),
            P("dp", None),
        ),
        out_specs=(
            P("dp", "space", None, None),
            P("dp", None),
            P("dp", "space", None, None),
            P(("dp", "space"), None),
            P(("dp", "space"), None),
            P(("dp", "space")),
            P(("dp", "space")),
        ),
        check_vma=False,
    )
```
